32 devices in a mesh: rows: 2 (over x), cent: 16 (over z, y, core).
Axes of the slice: x: 2, y: 2, z: 4, core: 2. Of those that a mesh axis runs over, the one named last changes fastest.
Arguments:
- embeddings: bfloat16 [2048, 768], P(('rows', 'cent')), may hold values from -33 to 33
- centroids: bfloat16 [2048, 768], P('cent'), may hold values from -4 to 4
- group_length: int32 [2], P('rows'), may hold values from 256 to 1024, as said below
Outputs:
- new_centroids: bfloat16 [2048, 768], P('cent')
- new_moments: bfloat16 [2048, 768], P('cent')
- loglik: float32 [2048], P(('rows', 'cent'))
The draws below stay inside these ranges and needn't reach their ends.
Inputs may be any that keep to these rules, and one draw needn't show every extreme that they name: Row group g uses its first group_length[g] of its 1024 row slots; at least one group uses all of them.
All inputs are finite; a program needn't handle non-finite values.
Results may differ from the reference program's by a relative error of at most 0.0047.
Values may be sent and summed in bfloat16 or wider, within the bound.
A program may use at most 64 MiB of HBM per device.

```python
import math
import jax
import jax.numpy as jnp
from jax import lax

D = 768
K = 2048
ROWS_GROUP = 1024
GROUPS = 2
ROWS = 2048


def centroid_table(key):
    values_base = jax.random.normal(jax.random.fold_in(key, 71), (K, D), jnp.float32)
    values_base = jnp.clip(values_base, -4.0, 4.0)
    row_index = jnp.arange(K, dtype=jnp.int32)
    partner = row_index % 61 == 1
    shifted = jnp.roll(jnp.roll(values_base, 1, axis=1), 1, axis=0)
    return jnp.where(partner[:, None], shifted, values_base)


def draw_centroids(key, part):
    return centroid_table(key).astype(jnp.bfloat16)


def draw_embeddings(key, part):
    values_base = jnp.clip(jax.random.normal(jax.random.fold_in(key, 72), (ROWS, D), jnp.float32), -6.0, 6.0)
    return values_base.astype(jnp.bfloat16)


def draw_group_length(key, part):
    lengths = jax.random.randint(jax.random.fold_in(key, 81), (GROUPS,), ROWS_GROUP // 4, ROWS_GROUP + 1, dtype=jnp.int32)
    full_group = jax.random.randint(jax.random.fold_in(key, 82), (), 0, GROUPS, dtype=jnp.int32)
    return jnp.where(jnp.arange(GROUPS, dtype=jnp.int32) == full_group, ROWS_GROUP, lengths).astype(jnp.int32)


def setup_inputs(seed: int = 0) -> dict:
    splits = jax.random.split(jax.random.key(seed), 4)
    embeddings = draw_embeddings(jax.random.fold_in(splits[3], 71), 0)
    centroids = draw_centroids(jax.random.fold_in(splits[3], 71), 0)
    group_length = draw_group_length(jax.random.fold_in(splits[3], 71), 0)
    return dict(embeddings=embeddings, centroids=centroids, group_length=group_length)


def reference(embeddings, centroids, group_length):
    cent_wide = centroids.astype(jnp.float32)
    squared_norm = lax.optimization_barrier(jnp.sum(cent_wide * cent_wide, axis=1))
    factor = 3.0 / math.sqrt(D)
    row_blocks = embeddings.reshape(GROUPS, ROWS_GROUP, D)

    def group_step(state_in, group_item):
        weighted, moments, weight_mass = state_in
        block_rows, used_rows = group_item
        inner = jnp.dot(block_rows, centroids.T, preferred_element_type=jnp.float32)
        logits = factor * (inner - 0.5 * squared_norm[None, :])
        row_lse = jax.nn.logsumexp(logits, axis=1)
        valid_rows = jnp.arange(ROWS_GROUP, dtype=jnp.int32) < used_rows
        responsibility = jnp.where(valid_rows[:, None], jnp.exp(logits - row_lse[:, None]), 0.0).astype(jnp.bfloat16)
        rows_wide = block_rows.astype(jnp.float32)
        squares = (rows_wide * rows_wide).astype(jnp.bfloat16)
        weighted = weighted + jnp.dot(responsibility.T, block_rows, preferred_element_type=jnp.float32)
        moments = moments + jnp.dot(responsibility.T, squares, preferred_element_type=jnp.float32)
        weight_mass = weight_mass + lax.optimization_barrier(jnp.sum(responsibility.astype(jnp.float32), axis=0))
        loglik = jnp.where(valid_rows, row_lse, jnp.zeros_like(row_lse))
        return ((weighted, moments, weight_mass), loglik)
    zero_state = (jnp.zeros((K, D), jnp.float32), jnp.zeros((K, D), jnp.float32), jnp.zeros((K,), jnp.float32))
    totals, loglik = lax.scan(group_step, zero_state, (row_blocks, group_length))
    weighted, moments, weight_mass = totals
    denominator = weight_mass[:, None] + 1.0
    new_centroids = ((weighted + 1.0 * cent_wide) / denominator).astype(jnp.bfloat16)
    new_moments = ((moments + 1.0) / denominator).astype(jnp.bfloat16)
    return (new_centroids, new_moments, loglik.reshape(ROWS))
```

```python
import functools
import math

import jax
import jax.numpy as jnp
from jax import lax
from jax.experimental import pallas as pl
from jax.experimental.pallas import tpu as pltpu
from jax.sharding import PartitionSpec as P

score_factor = 3.0
prior_weight = 1.0
MESH = pl.DeviceIdType.MESH
contract_width = (((1,), (1,)), ((), ()))
contract_rows = (((1,), (0,)), ((), ()))


lanes = 128


def sums_kernel(
    groups, shards, column_step, split,
    length_ref, emb_hbm, cent_hbm,
    cent_out, mom_out, lik_out, inverse_out,
    cent_ref, rows_all, squares, weights, parts, stats, masses,
    own_sem, cent_sem, z_send, z_recv, y_send, y_recv, c_send, c_recv,
    p_send, p_recv, s_send, s_recv, m_send, m_recv,
):
    g = lax.axis_index("rows")
    i = lax.axis_index("cent")
    row_count, width = emb_hbm.shape
    cents = cent_ref.shape[0]
    total = shards * row_count
    piece_rows = row_count // split
    line = shards // 4
    spot = lax.rem(i, 4)
    place = i // 4
    core = lax.rem(i, 2)
    core_peer = i + 1 - 2 * core
    y_spot = lax.rem(spot + 2, 4)
    y_peer = place * 4 + y_spot
    factor = score_factor / math.sqrt(width)

    def across(step):
        return lax.rem(g + step, groups)

    def signal(peer):
        pl.semaphore_signal(barrier, inc=1, device_id=peer, device_id_type=MESH)

    barrier = pltpu.get_barrier_semaphore()
    for peer in [(g, y_peer), (g, core_peer)] + [(across(s), i) for s in range(1, groups)]:
        signal(peer)
    has_right = place < line - 1
    has_left = place > 0
    pl.when(has_right)(lambda: signal((g, i + 4)))
    pl.when(has_left)(lambda: signal((g, i - 4)))
    own = [
        pltpu.make_async_copy(
            emb_hbm.at[pl.ds(h * piece_rows, piece_rows)], rows_all.at[i * split + h], own_sem.at[h]
        )
        for h in range(split)
    ]
    for copy in own:
        copy.start()
    cent_copy = pltpu.make_async_copy(cent_hbm, cent_ref, cent_sem)
    cent_copy.start()
    for copy in own:
        copy.wait()
    sides = has_right.astype(jnp.int32) + has_left.astype(jnp.int32)
    pl.semaphore_wait(barrier, 1 + groups + sides)

    def describe(src, dst, send_sem, recv_sem, peer):
        return pltpu.make_async_remote_copy(
            src_ref=src, dst_ref=dst, send_sem=send_sem, recv_sem=recv_sem,
            device_id=peer, device_id_type=MESH,
        )

    def send(*spec):
        copy = describe(*spec)
        copy.start()
        return copy

    def z_copy(unit, way, s, h):
        slot = rows_all.at[unit]
        peer = (g, i + 4 if way == 0 else i - 4)
        return describe(slot, slot, z_send.at[way, s, h], z_recv.at[way, s, h], peer)

    def y_copy(unit, k, h):
        slot = rows_all.at[unit]
        return describe(slot, slot, y_send.at[k, h], y_recv.at[k, h], (g, y_peer))

    def c_copy(unit, k, h):
        slot = rows_all.at[unit]
        return describe(slot, slot, c_send.at[k, h], c_recv.at[k, h], (g, core_peer))

    def square(unit):
        wide = rows_all[unit].astype(jnp.float32)
        squares[unit] = (wide * wide).astype(jnp.bfloat16)

    steps = 2 * line - 1
    order = [(way, s) for s in range(1, line) for way in range(2)]

    def present(way, s):
        return place >= s if way == 0 else place + s < line

    def unit_of(way, s, where, h):
        source = place - s if way == 0 else place + s
        return (source * 4 + where) * split + h

    for h in range(split):
        unit = i * split + h
        pl.when(has_right)(lambda: z_copy(unit, 0, 1, h).start())
        pl.when(has_left)(lambda: z_copy(unit, 1, 1, h).start())
        y_copy(unit, 0, h).start()
        c_copy(unit, 0, h).start()
    for h in range(split):
        square(i * split + h)
    for k, (way, s) in enumerate(order, 1):
        for h in range(split):
            def relay():
                unit = unit_of(way, s, spot, h)
                z_copy(unit, way, s, h).wait_recv()
                onward = has_right if way == 0 else has_left
                if s + 1 < line:
                    pl.when(onward)(lambda: z_copy(unit, way, s + 1, h).start())
                y_copy(unit, k, h).start()
                c_copy(unit, k, h).start()
                square(unit)

            pl.when(present(way, s))(relay)
    for h in range(split):
        unit = unit_of(0, 0, y_spot, h)
        y_copy(unit, 0, h).wait_recv()
        c_copy(unit, steps, h).start()
        square(unit)
    for k, (way, s) in enumerate(order, 1):
        for h in range(split):
            def pass_on():
                unit = unit_of(way, s, y_spot, h)
                y_copy(unit, k, h).wait_recv()
                c_copy(unit, steps + k, h).start()
                square(unit)

            pl.when(present(way, s))(pass_on)
    other = spot + 1 - 2 * core
    for j, where in enumerate((other, lax.rem(other + 2, 4))):
        for h in range(split):
            unit = unit_of(0, 0, where, h)
            c_copy(unit, j * steps, h).wait_recv()
            square(unit)
        for k, (way, s) in enumerate(order, 1):
            for h in range(split):
                def take():
                    unit = unit_of(way, s, where, h)
                    c_copy(unit, j * steps + k, h).wait_recv()
                    square(unit)

                pl.when(present(way, s))(take)
    sent = []
    cent_copy.wait()
    cent_wide = cent_ref[...].astype(jnp.float32)
    half_norm = 0.5 * jnp.sum(cent_wide * cent_wide, axis=1, keepdims=True)

    slots = split * max(1, min(shards, 512 // row_count))
    chunk = slots * piece_rows
    chunks = shards * split // slots

    def score(k, carry):
        first = k * slots
        columns = k * chunk
        if not isinstance(k, int):
            columns = pl.multiple_of(columns, chunk)
        block = rows_all[pl.ds(first, slots)].reshape(chunk, width)
        inner = lax.dot_general(
            cent_ref[...], block, contract_width, preferred_element_type=jnp.float32
        )
        logits = factor * (inner - half_norm)
        peak = jnp.max(logits, axis=0, keepdims=True)
        weight = jnp.exp(logits - peak)
        weights[:, pl.ds(columns, chunk)] = weight
        parts[0, 0:1, pl.ds(columns, chunk)] = peak
        parts[0, 1:2, pl.ds(columns, chunk)] = jnp.sum(weight, axis=0, keepdims=True)
        return carry

    for k in range(chunks) if chunks <= 4 else ():
        score(k, 0)
    if chunks > 4:
        lax.fori_loop(0, chunks, score, 0)

    own_peak = parts[0, 0:1, :]

    def joined(part_list):
        highest = part_list[0][0]
        for peak, _ in part_list[1:]:
            highest = jnp.maximum(highest, peak)
        amount = None
        for peak, exp_sum in part_list:
            term = exp_sum * jnp.exp(peak - highest)
            amount = term if amount is None else amount + term
        return highest, amount

    def part(k):
        return parts[k, 0:1, :], parts[k, 1:2, :]

    hop = send(parts.at[0], parts.at[1], p_send.at[0], p_recv.at[0], (g, core_peer))

    hop.wait()
    peak, amount = joined([part(0), part(1)])
    parts[2, 0:1, :] = peak
    parts[2, 1:2, :] = amount
    hops = []
    for k in range(2 * line - 1, 0, -1):
        peer = lax.rem(place + k // 2, line) * 4 + lax.rem(spot + 2 * (k % 2), 4)
        hops.append(send(parts.at[2], parts.at[2 + k], p_send.at[k], p_recv.at[k], (g, peer)))
    for hop in hops:
        hop.wait_recv()
    sent += hops
    peak, amount = joined([part(2 + k) for k in range(2 * line)])
    lse = peak + jnp.log(amount)
    valid = lax.broadcasted_iota(jnp.int32, (1, total), 1) < length_ref[0]
    scale = jnp.where(valid, jnp.exp(own_peak - lse), 0.0)
    resp = (weights[...] * scale).astype(jnp.bfloat16)

    ones = jnp.ones((8, total), jnp.bfloat16)
    masses[g] = lax.dot_general(ones, resp, contract_width, preferred_element_type=jnp.float32)
    s_copies = {}
    for s in range(1, groups):
        sent.append(
            send(masses.at[g], masses.at[g], m_send.at[s], m_recv.at[s], (across(s), i))
        )
    m_copies = sent[len(sent) - (groups - 1):]
    pieces = 2 * (width // column_step)
    for k in range(pieces):
        left = (k // 2) * column_step
        source = rows_all if k % 2 == 0 else squares
        block = source[:, :, left:left + column_step].reshape(total, column_step)
        sums = lax.dot_general(resp, block, contract_rows, preferred_element_type=jnp.float32)
        stats[g, k] = sums.astype(jnp.bfloat16)
        for s in range(1, groups):
            s_copies[k, s] = send(
                stats.at[g, k], stats.at[g, k], s_send.at[k, s], s_recv.at[k, s], (across(s), i)
            )

    own_lik = jnp.where(valid, lse, 0.0)
    pick = own_lik[:, 0:row_count]
    for j in range(1, shards):
        pick = jnp.where(i == j, own_lik[:, j * row_count:(j + 1) * row_count], pick)
    lik_out[...] = pick

    for copy in m_copies:
        copy.wait_recv()
    mass = masses[0, 0:1, :]
    for r in range(1, groups):
        mass = mass + masses[r, 0:1, :]
    inverse = 1.0 / (mass + prior_weight)
    inverse_out[...] = jnp.transpose(jnp.broadcast_to(inverse, (cents, cents)))
    for k in range(pieces):
        for s in range(1, groups):
            s_copies[k, s].wait_recv()
        left = (k // 2) * column_step
        sums = stats[0, k].astype(jnp.float32)
        for r in range(1, groups):
            sums = sums + stats[r, k].astype(jnp.float32)
        if k % 2 == 0:
            sums = sums + prior_weight * cent_ref[:, left:left + column_step].astype(jnp.float32)
            cent_out[:, left:left + column_step] = sums
        else:
            mom_out[:, left:left + column_step] = sums + prior_weight
    for h in range(split):
        unit = i * split + h
        pl.when(has_right)(lambda: z_copy(unit, 0, 1, h).wait_send())
        pl.when(has_left)(lambda: z_copy(unit, 1, 1, h).wait_send())
        y_copy(unit, 0, h).wait_send()
        c_copy(unit, 0, h).wait_send()
        c_copy(unit_of(0, 0, y_spot, h), steps, h).wait_send()
    for k, (way, s) in enumerate(order, 1):
        for h in range(split):
            def finish():
                unit = unit_of(way, s, spot, h)
                onward = has_right if way == 0 else has_left
                if s + 1 < line:
                    pl.when(onward)(lambda: z_copy(unit, way, s + 1, h).wait_send())
                y_copy(unit, k, h).wait_send()
                c_copy(unit, k, h).wait_send()
                c_copy(unit_of(way, s, y_spot, h), steps + k, h).wait_send()

            pl.when(present(way, s))(finish)
    for copy in sent + list(s_copies.values()):
        copy.wait_send()


def gather_kernel(
    shards, split,
    length_ref, emb_hbm, cent_hbm,
    cent_out, mom_out, lik_out, inverse_out,
    cent_ref, rows_all, weights, resp, peaks, pair, parts, lses,
    own_sem, cent_sem, ready, o_send, z_send, z_recv, y_send, y_recv, x_send, x_recv,
    c_send, c_recv, q_send, q_recv, p_send, p_recv, l_send, l_recv,
):
    g = lax.axis_index("rows")
    i = lax.axis_index("cent")
    row_count, width = emb_hbm.shape
    cents = cent_ref.shape[0]
    total = shards * row_count
    piece = row_count // split
    line = shards // 4
    chunk = 4 * row_count
    spread = chunk // lanes
    spot = lax.rem(i, 4)
    place = i // 4
    core = lax.rem(i, 2)
    core_peer = i + 1 - 2 * core
    core_spot = spot + 1 - 2 * core
    y_spot = lax.rem(spot + 2, 4)
    core_y_spot = lax.rem(core_spot + 2, 4)
    y_peer = place * 4 + y_spot
    there = 1 - g
    factor = score_factor / math.sqrt(width)

    def signal(sem, peer):
        pl.semaphore_signal(sem, inc=1, device_id=peer, device_id_type=MESH)

    barrier = pltpu.get_barrier_semaphore()
    has_right = place < line - 1
    has_left = place > 0
    pl.when(has_right)(lambda: signal(barrier, (g, i + 4)))
    pl.when(has_left)(lambda: signal(barrier, (g, i - 4)))
    for peer in [(g, y_peer), (there, i), (g, core_peer)]:
        signal(barrier, peer)
    own = [
        pltpu.make_async_copy(
            emb_hbm.at[pl.ds(h * piece, piece)],
            rows_all.at[g, i, pl.ds(h * piece, piece)], own_sem.at[h],
        )
        for h in range(split)
    ]
    for copy in own:
        copy.start()
    cent_copy = pltpu.make_async_copy(cent_hbm, cent_ref, cent_sem)
    cent_copy.start()
    for copy in own:
        copy.wait()
    sides = has_right.astype(jnp.int32) + has_left.astype(jnp.int32)
    pl.semaphore_wait(barrier, 3 + sides)

    def slot(group, q, where, h):
        return rows_all.at[group, q * 4 + where, pl.ds(h * piece, piece)]

    def move(ref, send_sem, recv_sem, peer):
        return pltpu.make_async_remote_copy(
            src_ref=ref, dst_ref=ref, send_sem=send_sem, recv_sem=recv_sem,
            device_id=peer, device_id_type=MESH,
        )

    def z_own(way, s, h):
        peer = (g, i + 4 * s if way == 0 else i - 4 * s)
        return move(slot(g, place, spot, h), o_send.at[way, s, h], z_recv.at[place, h], peer)

    def z_move(way, q, h):
        peer = (g, i + 4 if way == 0 else i - 4)
        return move(slot(g, q, spot, h), z_send.at[q, h], z_recv.at[q, h], peer)

    def y_move(q, h):
        return move(slot(g, q, spot, h), y_send.at[q, h], y_recv.at[q, h], (g, y_peer))

    def y_come(q, h):
        return move(slot(g, q, y_spot, h), y_send.at[q, h], y_recv.at[q, h], (g, y_peer))

    def x_move(q, side, h):
        where = spot if side == 0 else y_spot
        return move(slot(g, q, where, h), x_send.at[q, side, h], x_recv.at[q, side, h], (there, i))

    def x_come(q, side, h):
        where = spot if side == 0 else y_spot
        return move(
            slot(there, q, where, h), x_send.at[q, side, h], x_recv.at[q, side, h], (there, i)
        )

    def c_move(mine, q, side, h):
        where = spot if side == 0 else y_spot
        t = 0 if mine else 1
        return move(
            slot(g if mine else there, q, where, h),
            c_send.at[t, q, side, h], c_recv.at[t, q, side, h], (g, core_peer),
        )

    def c_come(mine, q, side, h):
        where = core_spot if side == 0 else core_y_spot
        t = 0 if mine else 1
        return move(
            slot(g if mine else there, q, where, h),
            c_send.at[t, q, side, h], c_recv.at[t, q, side, h], (g, core_peer),
        )

    def source(way, s):
        return place - s if way == 0 else place + s

    def present(way, s):
        return place >= s if way == 0 else place + s < line

    def onward(way, s):
        if way == 0:
            return jnp.logical_and(place > s, has_right)
        return jnp.logical_and(place + s < line - 1, has_left)

    def starts(way):
        return has_right if way == 0 else has_left

    def ends(way):
        return place == 0 if way == 0 else place == line - 1

    def both(fn, cond):
        for way in range(2):
            pl.when(cond(way))(functools.partial(fn, way))

    def z_take(way, s, h):
        def take():
            q = source(way, s)
            z_move(way, q, h).wait_recv()
            if s + 1 < line:
                pl.when(onward(way, s))(lambda: z_move(way, q, h).start())
            y_move(q, h).start()
            x_move(q, 0, h).start()
            c_move(True, q, 0, h).start()

        pl.when(present(way, s))(take)

    def y_take(way, s, h):
        def take():
            q = source(way, s)
            y_come(q, h).wait_recv()
            x_move(q, 1, h).start()
            c_move(True, q, 1, h).start()

        pl.when(present(way, s))(take)

    for h in range(split):
        both(lambda way: z_own(way, 1, h).start(), starts)
        y_move(place, h).start()
        x_move(place, 0, h).start()
    for h in range(split):
        c_move(True, place, 0, h).start()
    if line > 2:
        pl.when(jnp.logical_and(place == 1, has_right))(lambda: signal(ready.at[0], (g, i + 4)))
        pl.when(jnp.logical_and(place == line - 2, has_left))(lambda: signal(ready.at[1], (g, i - 4)))

        def pass_up():
            pl.semaphore_wait(ready.at[0], 1)
            pl.when(has_right)(lambda: signal(ready.at[0], (g, i + 4)))

        def pass_down():
            pl.semaphore_wait(ready.at[1], 1)
            pl.when(has_left)(lambda: signal(ready.at[1], (g, i - 4)))

        pl.when(place >= 2)(pass_up)
        pl.when(place <= line - 3)(pass_down)

        def far(way):
            for h in range(split):
                for s in range(2, line):
                    z_own(way, s, h).start()

        both(far, ends)
    for h in range(split):
        for way in range(2):
            z_take(way, 1, h)
    for h in range(split):
        y_come(place, h).wait_recv()
        x_move(place, 1, h).start()
        c_move(True, place, 1, h).start()
    for h in range(split):
        for s in range(2, line):
            for way in range(2):
                z_take(way, s, h)
    for s in range(1, line):
        for h in range(split):
            for way in range(2):
                y_take(way, s, h)

    cent_copy.wait()
    cent_wide = cent_ref[...].astype(jnp.float32)
    half_norm = 0.5 * jnp.sum(cent_wide * cent_wide, axis=1, keepdims=True)

    def score(mine, q):
        t = 0 if mine else 1
        group = g if mine else there
        for side in range(2):
            for h in range(split):
                c_come(mine, q, side, h).wait_recv()
        block = rows_all[group, pl.ds(q * 4, 4)].reshape(chunk, width)
        inner = lax.dot_general(
            cent_ref[...], block, contract_width, preferred_element_type=jnp.float32
        )
        logits = factor * (inner - half_norm)
        peak = jnp.max(logits, axis=0, keepdims=True)
        weight = jnp.exp(logits - peak)
        weights[t, q] = weight
        amount = jnp.sum(weight, axis=0, keepdims=True)
        for r in range(spread):
            peaks[t, q, r:r + 1, :] = peak[:, r * lanes:(r + 1) * lanes]
            if mine:
                pair[0, q, r:r + 1, :] = (peak + jnp.log(amount))[:, r * lanes:(r + 1) * lanes]

    def joined(values):
        highest = values[0]
        for value in values[1:]:
            highest = jnp.maximum(highest, value)
        amount = jnp.exp(values[0] - highest)
        for value in values[1:]:
            amount = amount + jnp.exp(value - highest)
        return highest + jnp.log(amount)

    for j in range(line):
        score(True, lax.rem(place + j, line))

    def send(src, dst, send_sem, recv_sem, peer):
        copy = pltpu.make_async_remote_copy(
            src_ref=src, dst_ref=dst, send_sem=send_sem, recv_sem=recv_sem,
            device_id=peer, device_id_type=MESH,
        )
        copy.start()
        return copy

    hop = send(pair.at[0], pair.at[1], q_send, q_recv, (g, core_peer))
    hop.wait()
    parts[0] = joined([pair[0], pair[1]])
    hops = []
    for k in range(2 * line - 1, 0, -1):
        peer = lax.rem(place + k // 2, line) * 4 + lax.rem(spot + 2 * (k % 2), 4)
        hops.append(send(parts.at[0], parts.at[k], p_send.at[k], p_recv.at[k], (g, peer)))

    def x_take(q, side, h):
        x_come(q, side, h).wait_recv()
        c_move(False, q, side, h).start()

    def x_take_if(way, s, side, h):
        pl.when(present(way, s))(lambda: x_take(source(way, s), side, h))

    for h in range(split):
        x_take(place, 0, h)
    for h in range(split):
        for way in range(2):
            x_take_if(way, 1, 0, h)
    for h in range(split):
        x_take(place, 1, h)
    score(False, place)
    for hop in hops:
        hop.wait_recv()
    lse = joined([parts[k] for k in range(2 * line)])
    position = (
        lax.broadcasted_iota(jnp.int32, lse.shape, 0) * chunk
        + lax.broadcasted_iota(jnp.int32, lse.shape, 1) * lanes
        + lax.broadcasted_iota(jnp.int32, lse.shape, 2)
    )
    valid = position < length_ref[0]
    lses[0] = jnp.where(valid, lse, jnp.inf)
    cross = send(lses.at[0], lses.at[1], l_send, l_recv, (there, i))
    own_lik = jnp.where(valid, lse, 0.0)
    count = line
    pick = own_lik
    for j in range(1, line):
        pick = jnp.where(place == j, own_lik[j:j + 1], pick[0:1]) if j > 1 else jnp.where(
            place == 1, own_lik[1:2], own_lik[0:1]
        )
    pick = pick[0]
    pick = jnp.concatenate([pick[r:r + 1, :] for r in range(spread)], axis=1)
    pick = jnp.where(spot >= 2, pick[:, 2 * row_count:], pick[:, :2 * row_count])
    lik_out[...] = jnp.where(core == 1, pick[:, row_count:], pick[:, :row_count])

    ones = jnp.ones((8, total), jnp.bfloat16)

    def gather_stats(mine):
        t = 0 if mine else 1
        scale = jnp.exp(peaks[t] - lses[t])
        for q in range(line):
            for r in range(spread):
                left = r * lanes
                resp[:, q * chunk + left:q * chunk + left + lanes] = (
                    weights[t, q, :, left:left + lanes] * scale[q, r:r + 1, :]
                ).astype(jnp.bfloat16)
        mass = lax.dot_general(ones, resp[...], contract_width, preferred_element_type=jnp.float32)
        block = rows_all[g if mine else there].reshape(total, width)
        weighted = lax.dot_general(resp[...], block, contract_rows, preferred_element_type=jnp.float32)
        wide = block.astype(jnp.float32)
        square = (wide * wide).astype(jnp.bfloat16)
        moments = lax.dot_general(resp[...], square, contract_rows, preferred_element_type=jnp.float32)
        return mass, weighted, moments

    mass, weighted, moments = gather_stats(True)
    cent_out[...] = weighted + prior_weight * cent_wide
    mom_out[...] = moments + prior_weight
    for h in range(split):
        for s in range(2, line):
            for way in range(2):
                x_take_if(way, s, 0, h)
    for s in range(1, line):
        for h in range(split):
            for way in range(2):
                x_take_if(way, s, 1, h)
    for j in range(1, line):
        score(False, lax.rem(place + j, line))
    cross.wait_recv()
    mass_there, weighted, moments = gather_stats(False)
    cent_out[...] += weighted
    mom_out[...] += moments
    inverse = 1.0 / (mass[0:1, :] + mass_there[0:1, :] + prior_weight)
    inverse_out[...] = jnp.transpose(jnp.broadcast_to(inverse, (cents, cents)))

    for h in range(split):
        both(lambda way: z_own(way, 1, h).wait_send(), starts)

        def far_done(way):
            for s in range(2, line):
                z_own(way, s, h).wait_send()

        if line > 2:
            both(far_done, ends)
    for s in range(1, line):
        for way in range(2):
            if s + 1 < line:
                def relayed():
                    for h in range(split):
                        z_move(way, source(way, s), h).wait_send()

                pl.when(onward(way, s))(relayed)
    for q in range(line):
        for h in range(split):
            y_move(q, h).wait_send()
            for side in range(2):
                x_move(q, side, h).wait_send()
                c_move(True, q, side, h).wait_send()
                c_move(False, q, side, h).wait_send()
    for copy in hops + [cross]:
        copy.wait_send()


def gather_call(shards, row_count, width, cents, out_shape):
    line = shards // 4
    split = 4
    total = shards * row_count
    spread = 4 * row_count // lanes
    vmem = pl.BlockSpec(memory_space=pltpu.VMEM)
    hbm = pl.BlockSpec(memory_space=pltpu.HBM)
    dma = pltpu.SemaphoreType.DMA
    tile = (line, spread, lanes)
    return pl.pallas_call(
        functools.partial(gather_kernel, shards, split),
        out_shape=out_shape,
        in_specs=[pl.BlockSpec(memory_space=pltpu.SMEM), hbm, hbm],
        out_specs=(vmem, vmem, vmem, vmem),
        scratch_shapes=[
            pltpu.VMEM((cents, width), jnp.bfloat16),
            pltpu.VMEM((2, shards, row_count, width), jnp.bfloat16),
            pltpu.VMEM((2, line, cents, 4 * row_count), jnp.float32),
            pltpu.VMEM((cents, total), jnp.bfloat16),
            pltpu.VMEM((2, *tile), jnp.float32),
            pltpu.VMEM((2, *tile), jnp.float32),
            pltpu.VMEM((2 * line, *tile), jnp.float32),
            pltpu.VMEM((2, *tile), jnp.float32),
            dma((split,)), dma, pltpu.SemaphoreType.REGULAR((2,)),
            dma((2, line, split)), dma((line, split)), dma((line, split)),
            dma((line, split)), dma((line, split)),
            dma((line, 2, split)), dma((line, 2, split)),
            dma((2, line, 2, split)), dma((2, line, 2, split)),
            dma, dma, dma((2 * line,)), dma((2 * line,)), dma, dma,
        ],
        compiler_params=pltpu.CompilerParams(
            collective_id=0, has_side_effects=True, vmem_limit_bytes=32 * 1024 * 1024
        ),
        name="soft_em",
    )


def solution(mesh):
    groups = mesh.shape["rows"]
    shards = mesh.shape["cent"]
    line = shards // 4

    def step(embeddings, centroids, group_length):
        row_count, width = embeddings.shape
        cents = centroids.shape[0]
        total = row_count * shards
        column_step = 256 if width % 256 == 0 else width
        pieces = 2 * (width // column_step)
        split = 2 if row_count % 32 == 0 else 1
        vmem = pl.BlockSpec(memory_space=pltpu.VMEM)
        hbm = pl.BlockSpec(memory_space=pltpu.HBM)
        held = 4 * total * width + 4 * cents * total + 2 * (groups * 2 + 1) * cents * width
        steps = 2 * line - 1
        dma = pltpu.SemaphoreType.DMA
        out_shape = (
            jax.ShapeDtypeStruct((cents, width), jnp.float32),
            jax.ShapeDtypeStruct((cents, width), jnp.float32),
            jax.ShapeDtypeStruct((1, row_count), jnp.float32),
            jax.ShapeDtypeStruct((cents, cents), jnp.float32),
        )
        if groups == 2 and shards % 4 == 0 and row_count % 64 == 0 and total <= 2048:
            call = gather_call(shards, row_count, width, cents, out_shape)
        else:
            call = pl.pallas_call(
                functools.partial(sums_kernel, groups, shards, column_step, split),
                out_shape=out_shape,
                in_specs=[pl.BlockSpec(memory_space=pltpu.SMEM), hbm, hbm],
                out_specs=(vmem, vmem, vmem, vmem),
                scratch_shapes=[
                    pltpu.VMEM((cents, width), jnp.bfloat16),
                    pltpu.VMEM((shards * split, row_count // split, width), jnp.bfloat16),
                    pltpu.VMEM((shards * split, row_count // split, width), jnp.bfloat16),
                    pltpu.VMEM((cents, total), jnp.float32),
                    pltpu.VMEM((2 + 2 * line, 2, total), jnp.float32),
                    pltpu.VMEM((groups, pieces, cents, column_step), jnp.bfloat16),
                    pltpu.VMEM((groups, 8, cents), jnp.float32),
                    dma((split,)), dma, dma((2, line, split)), dma((2, line, split)),
                    dma((steps, split)), dma((steps, split)),
                    dma((2 * steps, split)), dma((2 * steps, split)),
                    dma((2 * line,)), dma((2 * line,)),
                    dma((pieces, groups)), dma((pieces, groups)),
                    dma((groups,)), dma((groups,)),
                ],
                compiler_params=pltpu.CompilerParams(
                    collective_id=0, has_side_effects=True, vmem_limit_bytes=2 * held + 4 * 1024 * 1024
                ),
                name="soft_em",
            )
        cent_sums, moment_sums, loglik, inverse = call(group_length, pltpu.with_memory_space_constraint(embeddings, pltpu.HBM), pltpu.with_memory_space_constraint(centroids, pltpu.HBM))
        new_centroids = (cent_sums * inverse[:, 0:1]).astype(jnp.bfloat16)
        new_moments = (moment_sums * inverse[:, 0:1]).astype(jnp.bfloat16)
        return new_centroids, new_moments, loglik.reshape(row_count)

    return jax.shard_map(
        step,
        mesh=mesh,
        in_specs=(P(("rows", "cent"), None), P("cent", None), P("rows")),
        out_specs=(P("cent", None), P("cent", None), P(("rows", "cent"))),
        check_vma=False,
    )
```

```python
import functools
import math

import jax
import jax.numpy as jnp
from jax import lax
from jax.experimental import pallas as pl
from jax.experimental.pallas import tpu as pltpu
from jax.sharding import PartitionSpec as P

score_factor = 3.0
prior_weight = 1.0
MESH = pl.DeviceIdType.MESH
contract_width = (((1,), (1,)), ((), ()))
contract_rows = (((1,), (0,)), ((), ()))


lanes = 128


def sums_kernel(
    groups, shards, column_step, split,
    length_ref, emb_hbm, cent_hbm,
    cent_out, mom_out, lik_out, inverse_out,
    cent_ref, rows_all, squares, weights, parts, stats, masses,
    own_sem, cent_sem, z_send, z_recv, y_send, y_recv, c_send, c_recv,
    p_send, p_recv, s_send, s_recv, m_send, m_recv,
):
    g = lax.axis_index("rows")
    i = lax.axis_index("cent")
    row_count, width = emb_hbm.shape
    cents = cent_ref.shape[0]
    total = shards * row_count
    piece_rows = row_count // split
    line = shards // 4
    spot = lax.rem(i, 4)
    place = i // 4
    core = lax.rem(i, 2)
    core_peer = i + 1 - 2 * core
    y_spot = lax.rem(spot + 2, 4)
    y_peer = place * 4 + y_spot
    factor = score_factor / math.sqrt(width)

    def across(step):
        return lax.rem(g + step, groups)

    def signal(peer):
        pl.semaphore_signal(barrier, inc=1, device_id=peer, device_id_type=MESH)

    barrier = pltpu.get_barrier_semaphore()
    for peer in [(g, y_peer), (g, core_peer)] + [(across(s), i) for s in range(1, groups)]:
        signal(peer)
    has_right = place < line - 1
    has_left = place > 0
    pl.when(has_right)(lambda: signal((g, i + 4)))
    pl.when(has_left)(lambda: signal((g, i - 4)))
    own = [
        pltpu.make_async_copy(
            emb_hbm.at[pl.ds(h * piece_rows, piece_rows)], rows_all.at[i * split + h], own_sem.at[h]
        )
        for h in range(split)
    ]
    for copy in own:
        copy.start()
    cent_copy = pltpu.make_async_copy(cent_hbm, cent_ref, cent_sem)
    cent_copy.start()
    for copy in own:
        copy.wait()
    sides = has_right.astype(jnp.int32) + has_left.astype(jnp.int32)
    pl.semaphore_wait(barrier, 1 + groups + sides)

    def describe(src, dst, send_sem, recv_sem, peer):
        return pltpu.make_async_remote_copy(
            src_ref=src, dst_ref=dst, send_sem=send_sem, recv_sem=recv_sem,
            device_id=peer, device_id_type=MESH,
        )

    def send(*spec):
        copy = describe(*spec)
        copy.start()
        return copy

    def z_copy(unit, way, s, h):
        slot = rows_all.at[unit]
        peer = (g, i + 4 if way == 0 else i - 4)
        return describe(slot, slot, z_send.at[way, s, h], z_recv.at[way, s, h], peer)

    def y_copy(unit, k, h):
        slot = rows_all.at[unit]
        return describe(slot, slot, y_send.at[k, h], y_recv.at[k, h], (g, y_peer))

    def c_copy(unit, k, h):
        slot = rows_all.at[unit]
        return describe(slot, slot, c_send.at[k, h], c_recv.at[k, h], (g, core_peer))

    def square(unit):
        wide = rows_all[unit].astype(jnp.float32)
        squares[unit] = (wide * wide).astype(jnp.bfloat16)

    steps = 2 * line - 1
    order = [(way, s) for s in range(1, line) for way in range(2)]

    def present(way, s):
        return place >= s if way == 0 else place + s < line

    def unit_of(way, s, where, h):
        source = place - s if way == 0 else place + s
        return (source * 4 + where) * split + h

    for h in range(split):
        unit = i * split + h
        pl.when(has_right)(lambda: z_copy(unit, 0, 1, h).start())
        pl.when(has_left)(lambda: z_copy(unit, 1, 1, h).start())
        y_copy(unit, 0, h).start()
        c_copy(unit, 0, h).start()
    for h in range(split):
        square(i * split + h)
    for k, (way, s) in enumerate(order, 1):
        for h in range(split):
            def relay():
                unit = unit_of(way, s, spot, h)
                z_copy(unit, way, s, h).wait_recv()
                onward = has_right if way == 0 else has_left
                if s + 1 < line:
                    pl.when(onward)(lambda: z_copy(unit, way, s + 1, h).start())
                y_copy(unit, k, h).start()
                c_copy(unit, k, h).start()
                square(unit)

            pl.when(present(way, s))(relay)
    for h in range(split):
        unit = unit_of(0, 0, y_spot, h)
        y_copy(unit, 0, h).wait_recv()
        c_copy(unit, steps, h).start()
        square(unit)
    for k, (way, s) in enumerate(order, 1):
        for h in range(split):
            def pass_on():
                unit = unit_of(way, s, y_spot, h)
                y_copy(unit, k, h).wait_recv()
                c_copy(unit, steps + k, h).start()
                square(unit)

            pl.when(present(way, s))(pass_on)
    other = spot + 1 - 2 * core
    for j, where in enumerate((other, lax.rem(other + 2, 4))):
        for h in range(split):
            unit = unit_of(0, 0, where, h)
            c_copy(unit, j * steps, h).wait_recv()
            square(unit)
        for k, (way, s) in enumerate(order, 1):
            for h in range(split):
                def take():
                    unit = unit_of(way, s, where, h)
                    c_copy(unit, j * steps + k, h).wait_recv()
                    square(unit)

                pl.when(present(way, s))(take)
    sent = []
    cent_copy.wait()
    cent_wide = cent_ref[...].astype(jnp.float32)
    half_norm = 0.5 * jnp.sum(cent_wide * cent_wide, axis=1, keepdims=True)

    slots = split * max(1, min(shards, 512 // row_count))
    chunk = slots * piece_rows
    chunks = shards * split // slots

    def score(k, carry):
        first = k * slots
        columns = k * chunk
        if not isinstance(k, int):
            columns = pl.multiple_of(columns, chunk)
        block = rows_all[pl.ds(first, slots)].reshape(chunk, width)
        inner = lax.dot_general(
            cent_ref[...], block, contract_width, preferred_element_type=jnp.float32
        )
        logits = factor * (inner - half_norm)
        peak = jnp.max(logits, axis=0, keepdims=True)
        weight = jnp.exp(logits - peak)
        weights[:, pl.ds(columns, chunk)] = weight
        parts[0, 0:1, pl.ds(columns, chunk)] = peak
        parts[0, 1:2, pl.ds(columns, chunk)] = jnp.sum(weight, axis=0, keepdims=True)
        return carry

    for k in range(chunks) if chunks <= 4 else ():
        score(k, 0)
    if chunks > 4:
        lax.fori_loop(0, chunks, score, 0)

    own_peak = parts[0, 0:1, :]

    def joined(part_list):
        highest = part_list[0][0]
        for peak, _ in part_list[1:]:
            highest = jnp.maximum(highest, peak)
        amount = None
        for peak, exp_sum in part_list:
            term = exp_sum * jnp.exp(peak - highest)
            amount = term if amount is None else amount + term
        return highest, amount

    def part(k):
        return parts[k, 0:1, :], parts[k, 1:2, :]

    hop = send(parts.at[0], parts.at[1], p_send.at[0], p_recv.at[0], (g, core_peer))

    hop.wait()
    peak, amount = joined([part(0), part(1)])
    parts[2, 0:1, :] = peak
    parts[2, 1:2, :] = amount
    hops = []
    for k in range(2 * line - 1, 0, -1):
        peer = lax.rem(place + k // 2, line) * 4 + lax.rem(spot + 2 * (k % 2), 4)
        hops.append(send(parts.at[2], parts.at[2 + k], p_send.at[k], p_recv.at[k], (g, peer)))
    for hop in hops:
        hop.wait_recv()
    sent += hops
    peak, amount = joined([part(2 + k) for k in range(2 * line)])
    lse = peak + jnp.log(amount)
    valid = lax.broadcasted_iota(jnp.int32, (1, total), 1) < length_ref[0]
    scale = jnp.where(valid, jnp.exp(own_peak - lse), 0.0)
    resp = (weights[...] * scale).astype(jnp.bfloat16)

    ones = jnp.ones((8, total), jnp.bfloat16)
    masses[g] = lax.dot_general(ones, resp, contract_width, preferred_element_type=jnp.float32)
    s_copies = {}
    for s in range(1, groups):
        sent.append(
            send(masses.at[g], masses.at[g], m_send.at[s], m_recv.at[s], (across(s), i))
        )
    m_copies = sent[len(sent) - (groups - 1):]
    pieces = 2 * (width // column_step)
    for k in range(pieces):
        left = (k // 2) * column_step
        source = rows_all if k % 2 == 0 else squares
        block = source[:, :, left:left + column_step].reshape(total, column_step)
        sums = lax.dot_general(resp, block, contract_rows, preferred_element_type=jnp.float32)
        stats[g, k] = sums.astype(jnp.bfloat16)
        for s in range(1, groups):
            s_copies[k, s] = send(
                stats.at[g, k], stats.at[g, k], s_send.at[k, s], s_recv.at[k, s], (across(s), i)
            )

    own_lik = jnp.where(valid, lse, 0.0)
    pick = own_lik[:, 0:row_count]
    for j in range(1, shards):
        pick = jnp.where(i == j, own_lik[:, j * row_count:(j + 1) * row_count], pick)
    lik_out[...] = pick

    for copy in m_copies:
        copy.wait_recv()
    mass = masses[0, 0:1, :]
    for r in range(1, groups):
        mass = mass + masses[r, 0:1, :]
    inverse = 1.0 / (mass + prior_weight)
    inverse_out[...] = jnp.transpose(jnp.broadcast_to(inverse, (cents, cents)))
    for k in range(pieces):
        for s in range(1, groups):
            s_copies[k, s].wait_recv()
        left = (k // 2) * column_step
        sums = stats[0, k].astype(jnp.float32)
        for r in range(1, groups):
            sums = sums + stats[r, k].astype(jnp.float32)
        if k % 2 == 0:
            sums = sums + prior_weight * cent_ref[:, left:left + column_step].astype(jnp.float32)
            cent_out[:, left:left + column_step] = sums
        else:
            mom_out[:, left:left + column_step] = sums + prior_weight
    for h in range(split):
        unit = i * split + h
        pl.when(has_right)(lambda: z_copy(unit, 0, 1, h).wait_send())
        pl.when(has_left)(lambda: z_copy(unit, 1, 1, h).wait_send())
        y_copy(unit, 0, h).wait_send()
        c_copy(unit, 0, h).wait_send()
        c_copy(unit_of(0, 0, y_spot, h), steps, h).wait_send()
    for k, (way, s) in enumerate(order, 1):
        for h in range(split):
            def finish():
                unit = unit_of(way, s, spot, h)
                onward = has_right if way == 0 else has_left
                if s + 1 < line:
                    pl.when(onward)(lambda: z_copy(unit, way, s + 1, h).wait_send())
                y_copy(unit, k, h).wait_send()
                c_copy(unit, k, h).wait_send()
                c_copy(unit_of(way, s, y_spot, h), steps + k, h).wait_send()

            pl.when(present(way, s))(finish)
    for copy in sent + list(s_copies.values()):
        copy.wait_send()


def gather_kernel(
    shards, split,
    length_ref, emb_hbm, cent_hbm,
    cent_out, mom_out, lik_out, inverse_out,
    cent_ref, rows_all, weights, resp, peaks, pair, parts, lses,
    own_sem, cent_sem, ready, z_send, z_recv, y_send, y_recv, x_send, x_recv,
    c_send, c_recv, q_send, q_recv, p_send, p_recv, l_send, l_recv,
):
    g = lax.axis_index("rows")
    i = lax.axis_index("cent")
    row_count, width = emb_hbm.shape
    cents = cent_ref.shape[0]
    total = shards * row_count
    piece = row_count // split
    line = shards // 4
    chunk = 4 * row_count
    spread = chunk // lanes
    spot = lax.rem(i, 4)
    place = i // 4
    core = lax.rem(i, 2)
    core_peer = i + 1 - 2 * core
    core_spot = spot + 1 - 2 * core
    y_spot = lax.rem(spot + 2, 4)
    core_y_spot = lax.rem(core_spot + 2, 4)
    y_peer = place * 4 + y_spot
    there = 1 - g
    factor = score_factor / math.sqrt(width)

    def signal(sem, peer):
        pl.semaphore_signal(sem, inc=1, device_id=peer, device_id_type=MESH)

    barrier = pltpu.get_barrier_semaphore()
    has_right = place < line - 1
    has_left = place > 0
    pl.when(has_right)(lambda: signal(barrier, (g, i + 4)))
    pl.when(has_left)(lambda: signal(barrier, (g, i - 4)))
    for peer in [(g, y_peer), (there, i), (g, core_peer)]:
        signal(barrier, peer)
    own = pltpu.make_async_copy(emb_hbm, rows_all.at[g, i], own_sem)
    own.start()
    cent_copy = pltpu.make_async_copy(cent_hbm, cent_ref, cent_sem)
    cent_copy.start()
    own.wait()
    sides = has_right.astype(jnp.int32) + has_left.astype(jnp.int32)
    pl.semaphore_wait(barrier, 3 + sides)

    def move(ref, send_sem, recv_sem, peer):
        return pltpu.make_async_remote_copy(
            src_ref=ref, dst_ref=ref, send_sem=send_sem, recv_sem=recv_sem,
            device_id=peer, device_id_type=MESH,
        )

    def slot(group, q, where, h):
        if h is None:
            return rows_all.at[group, q * 4 + where]
        return rows_all.at[group, q * 4 + where, pl.ds(h * piece, piece)]

    def column(side):
        return spot if side == 0 else y_spot

    def z_own(way, s, h):
        peer = (g, i + 4 * s if way == 0 else i - 4 * s)
        return move(slot(g, place, spot, h), z_send, z_recv.at[place, h], peer)

    def z_move(way, q, h):
        peer = (g, i + 4 if way == 0 else i - 4)
        return move(slot(g, q, spot, h), z_send, z_recv.at[q, h], peer)

    def y_move(q, h):
        return move(slot(g, q, spot, h), y_send, y_recv.at[q], (g, y_peer))

    def y_come(q):
        return move(slot(g, q, y_spot, None), y_send, y_recv.at[q], (g, y_peer))

    def x_move(q, side, h):
        return move(slot(g, q, column(side), h), x_send, x_recv.at[q, side], (there, i))

    def x_come(q, side):
        return move(slot(there, q, column(side), None), x_send, x_recv.at[q, side], (there, i))

    def c_move(mine, q, side, h):
        ref = slot(g if mine else there, q, column(side), h)
        return move(ref, c_send, c_recv.at[0 if mine else 1, q], (g, core_peer))

    def c_come(mine, q):
        ref = rows_all.at[g if mine else there, pl.ds(q * 4, 2)]
        return move(ref, c_send, c_recv.at[0 if mine else 1, q], (g, core_peer))

    def source(way, s):
        return place - s if way == 0 else place + s

    def present(way, s):
        return place >= s if way == 0 else place + s < line

    def onward(way, s):
        if way == 0:
            return jnp.logical_and(place > s, has_right)
        return jnp.logical_and(place + s < line - 1, has_left)

    def starts(way):
        return has_right if way == 0 else has_left

    def ends(way):
        return place == 0 if way == 0 else place == line - 1

    def both(fn, cond):
        for way in range(2):
            pl.when(cond(way))(functools.partial(fn, way))

    def z_take(way, s, h):
        def take():
            q = source(way, s)
            z_move(way, q, h).wait_recv()
            if s + 1 < line:
                pl.when(onward(way, s))(lambda: z_move(way, q, h).start())
            y_move(q, h).start()
            x_move(q, 0, h).start()
            c_move(True, q, 0, h).start()

        pl.when(present(way, s))(take)

    def y_take(way, s):
        def take():
            q = source(way, s)
            y_come(q).wait_recv()
            c_move(True, q, 1, None).start()
            x_move(q, 1, None).start()

        pl.when(present(way, s))(take)

    for h in range(split):
        both(lambda way: z_own(way, 1, h).start(), starts)
        y_move(place, h).start()
        x_move(place, 0, h).start()
    c_move(True, place, 0, None).start()
    if line > 2:
        pl.when(jnp.logical_and(place == 1, has_right))(lambda: signal(ready.at[0], (g, i + 4)))
        pl.when(jnp.logical_and(place == line - 2, has_left))(lambda: signal(ready.at[1], (g, i - 4)))

        def pass_up():
            pl.semaphore_wait(ready.at[0], 1)
            pl.when(has_right)(lambda: signal(ready.at[0], (g, i + 4)))

        def pass_down():
            pl.semaphore_wait(ready.at[1], 1)
            pl.when(has_left)(lambda: signal(ready.at[1], (g, i - 4)))

        pl.when(place >= 2)(pass_up)
        pl.when(place <= line - 3)(pass_down)

        def far(way):
            for h in range(split):
                for s in range(2, line):
                    z_own(way, s, h).start()

        both(far, ends)
    for h in range(split):
        for way in range(2):
            z_take(way, 1, h)
    y_come(place).wait_recv()
    x_move(place, 1, None).start()
    c_move(True, place, 1, None).start()
    for h in range(split):
        for s in range(2, line):
            for way in range(2):
                z_take(way, s, h)
    for s in range(1, line):
        for way in range(2):
            y_take(way, s)

    cent_copy.wait()
    cent_wide = cent_ref[...].astype(jnp.float32)
    half_norm = 0.5 * jnp.sum(cent_wide * cent_wide, axis=1, keepdims=True)

    def score(mine, q):
        t = 0 if mine else 1
        group = g if mine else there
        c_come(mine, q).wait_recv()
        block = rows_all[group, pl.ds(q * 4, 4)].reshape(chunk, width)
        inner = lax.dot_general(
            cent_ref[...], block, contract_width, preferred_element_type=jnp.float32
        )
        logits = factor * (inner - half_norm)
        peak = jnp.max(logits, axis=0, keepdims=True)
        weight = jnp.exp(logits - peak)
        weights[t, q] = weight
        amount = jnp.sum(weight, axis=0, keepdims=True)
        for r in range(spread):
            peaks[t, q, r:r + 1, :] = peak[:, r * lanes:(r + 1) * lanes]
            if mine:
                pair[0, q, r:r + 1, :] = (peak + jnp.log(amount))[:, r * lanes:(r + 1) * lanes]

    def joined(values):
        highest = values[0]
        for value in values[1:]:
            highest = jnp.maximum(highest, value)
        amount = jnp.exp(values[0] - highest)
        for value in values[1:]:
            amount = amount + jnp.exp(value - highest)
        return highest + jnp.log(amount)

    for j in range(line):
        score(True, lax.rem(place + j, line))

    def send(src, dst, send_sem, recv_sem, peer):
        copy = pltpu.make_async_remote_copy(
            src_ref=src, dst_ref=dst, send_sem=send_sem, recv_sem=recv_sem,
            device_id=peer, device_id_type=MESH,
        )
        copy.start()
        return copy

    hop = send(pair.at[0], pair.at[1], q_send, q_recv, (g, core_peer))
    hop.wait_recv()
    parts[0] = joined([pair[0], pair[1]])
    hops = []
    for k in range(2 * line - 1, 0, -1):
        peer = lax.rem(place + k // 2, line) * 4 + lax.rem(spot + 2 * (k % 2), 4)
        hops.append(send(parts.at[0], parts.at[k], p_send, p_recv, (g, peer)))

    def x_take(q, side):
        x_come(q, side).wait_recv()
        c_move(False, q, side, None).start()

    def x_take_if(way, s, side):
        pl.when(present(way, s))(lambda: x_take(source(way, s), side))

    x_take(place, 0)
    for way in range(2):
        x_take_if(way, 1, 0)
    x_take(place, 1)
    score(False, place)
    others = parts.at[pl.ds(1, 2 * line - 1)]
    arrived = move(others, p_send, p_recv, (g, y_peer))
    arrived.wait_recv()
    lse = joined([parts[k] for k in range(2 * line)])
    position = (
        lax.broadcasted_iota(jnp.int32, lse.shape, 0) * chunk
        + lax.broadcasted_iota(jnp.int32, lse.shape, 1) * lanes
        + lax.broadcasted_iota(jnp.int32, lse.shape, 2)
    )
    valid = position < length_ref[0]
    lses[0] = jnp.where(valid, lse, jnp.inf)
    cross = send(lses.at[0], lses.at[1], l_send, l_recv, (there, i))
    own_lik = jnp.where(valid, lse, 0.0)
    count = line
    pick = own_lik
    for j in range(1, line):
        pick = jnp.where(place == j, own_lik[j:j + 1], pick[0:1]) if j > 1 else jnp.where(
            place == 1, own_lik[1:2], own_lik[0:1]
        )
    pick = pick[0]
    pick = jnp.concatenate([pick[r:r + 1, :] for r in range(spread)], axis=1)
    pick = jnp.where(spot >= 2, pick[:, 2 * row_count:], pick[:, :2 * row_count])
    lik_out[...] = jnp.where(core == 1, pick[:, row_count:], pick[:, :row_count])

    ones = jnp.ones((8, total), jnp.bfloat16)

    def gather_stats(mine):
        t = 0 if mine else 1
        scale = jnp.exp(peaks[t] - lses[t])
        for q in range(line):
            for r in range(spread):
                left = r * lanes
                resp[:, q * chunk + left:q * chunk + left + lanes] = (
                    weights[t, q, :, left:left + lanes] * scale[q, r:r + 1, :]
                ).astype(jnp.bfloat16)
        mass = lax.dot_general(ones, resp[...], contract_width, preferred_element_type=jnp.float32)
        block = rows_all[g if mine else there].reshape(total, width)
        weighted = lax.dot_general(resp[...], block, contract_rows, preferred_element_type=jnp.float32)
        wide = block.astype(jnp.float32)
        square = (wide * wide).astype(jnp.bfloat16)
        moments = lax.dot_general(resp[...], square, contract_rows, preferred_element_type=jnp.float32)
        return mass, weighted, moments

    mass, weighted, moments = gather_stats(True)
    cent_out[...] = weighted + prior_weight * cent_wide
    mom_out[...] = moments + prior_weight
    for s in range(2, line):
        for way in range(2):
            x_take_if(way, s, 0)
    for s in range(1, line):
        for way in range(2):
            x_take_if(way, s, 1)
    for j in range(1, line):
        score(False, lax.rem(place + j, line))
    cross.wait_recv()
    mass_there, weighted, moments = gather_stats(False)
    cent_out[...] += weighted
    mom_out[...] += moments
    inverse = 1.0 / (mass[0:1, :] + mass_there[0:1, :] + prior_weight)
    inverse_out[...] = jnp.transpose(jnp.broadcast_to(inverse, (cents, cents)))

    for sem, count in ((z_send, line - 1), (y_send, line), (x_send, 2 * line), (c_send, 4 * line)):
        move(rows_all.at[g, pl.ds(0, count)], sem, own_sem, (g, y_peer)).wait_send()
    arrived.wait_send()
    hop.wait_send()
    cross.wait_send()


def gather_call(shards, row_count, width, cents, out_shape):
    line = shards // 4
    split = 4
    total = shards * row_count
    spread = 4 * row_count // lanes
    vmem = pl.BlockSpec(memory_space=pltpu.VMEM)
    hbm = pl.BlockSpec(memory_space=pltpu.HBM)
    dma = pltpu.SemaphoreType.DMA
    tile = (line, spread, lanes)
    return pl.pallas_call(
        functools.partial(gather_kernel, shards, split),
        out_shape=out_shape,
        in_specs=[pl.BlockSpec(memory_space=pltpu.SMEM), hbm, hbm],
        out_specs=(vmem, vmem, vmem, vmem),
        scratch_shapes=[
            pltpu.VMEM((cents, width), jnp.bfloat16),
            pltpu.VMEM((2, shards, row_count, width), jnp.bfloat16),
            pltpu.VMEM((2, line, cents, 4 * row_count), jnp.float32),
            pltpu.VMEM((cents, total), jnp.bfloat16),
            pltpu.VMEM((2, *tile), jnp.float32),
            pltpu.VMEM((2, *tile), jnp.float32),
            pltpu.VMEM((2 * line, *tile), jnp.float32),
            pltpu.VMEM((2, *tile), jnp.float32),
            dma, dma, pltpu.SemaphoreType.REGULAR((2,)),
            dma, dma((line, split)), dma, dma((line,)), dma, dma((line, 2)),
            dma, dma((2, line)), dma, dma, dma, dma, dma, dma,
        ],
        compiler_params=pltpu.CompilerParams(
            collective_id=0, has_side_effects=True, vmem_limit_bytes=32 * 1024 * 1024
        ),
        name="soft_em",
    )


def solution(mesh):
    groups = mesh.shape["rows"]
    shards = mesh.shape["cent"]
    line = shards // 4

    def step(embeddings, centroids, group_length):
        row_count, width = embeddings.shape
        cents = centroids.shape[0]
        total = row_count * shards
        column_step = 256 if width % 256 == 0 else width
        pieces = 2 * (width // column_step)
        split = 2 if row_count % 32 == 0 else 1
        vmem = pl.BlockSpec(memory_space=pltpu.VMEM)
        hbm = pl.BlockSpec(memory_space=pltpu.HBM)
        held = 4 * total * width + 4 * cents * total + 2 * (groups * 2 + 1) * cents * width
        steps = 2 * line - 1
        dma = pltpu.SemaphoreType.DMA
        out_shape = (
            jax.ShapeDtypeStruct((cents, width), jnp.float32),
            jax.ShapeDtypeStruct((cents, width), jnp.float32),
            jax.ShapeDtypeStruct((1, row_count), jnp.float32),
            jax.ShapeDtypeStruct((cents, cents), jnp.float32),
        )
        if groups == 2 and shards % 4 == 0 and row_count % 64 == 0 and total <= 2048:
            call = gather_call(shards, row_count, width, cents, out_shape)
        else:
            call = pl.pallas_call(
                functools.partial(sums_kernel, groups, shards, column_step, split),
                out_shape=out_shape,
                in_specs=[pl.BlockSpec(memory_space=pltpu.SMEM), hbm, hbm],
                out_specs=(vmem, vmem, vmem, vmem),
                scratch_shapes=[
                    pltpu.VMEM((cents, width), jnp.bfloat16),
                    pltpu.VMEM((shards * split, row_count // split, width), jnp.bfloat16),
                    pltpu.VMEM((shards * split, row_count // split, width), jnp.bfloat16),
                    pltpu.VMEM((cents, total), jnp.float32),
                    pltpu.VMEM((2 + 2 * line, 2, total), jnp.float32),
                    pltpu.VMEM((groups, pieces, cents, column_step), jnp.bfloat16),
                    pltpu.VMEM((groups, 8, cents), jnp.float32),
                    dma((split,)), dma, dma((2, line, split)), dma((2, line, split)),
                    dma((steps, split)), dma((steps, split)),
                    dma((2 * steps, split)), dma((2 * steps, split)),
                    dma((2 * line,)), dma((2 * line,)),
                    dma((pieces, groups)), dma((pieces, groups)),
                    dma((groups,)), dma((groups,)),
                ],
                compiler_params=pltpu.CompilerParams(
                    collective_id=0, has_side_effects=True, vmem_limit_bytes=2 * held + 4 * 1024 * 1024
                ),
                name="soft_em",
            )
        cent_sums, moment_sums, loglik, inverse = call(group_length, pltpu.with_memory_space_constraint(embeddings, pltpu.HBM), pltpu.with_memory_space_constraint(centroids, pltpu.HBM))
        new_centroids = (cent_sums * inverse[:, 0:1]).astype(jnp.bfloat16)
        new_moments = (moment_sums * inverse[:, 0:1]).astype(jnp.bfloat16)
        return new_centroids, new_moments, loglik.reshape(row_count)

    return jax.shard_map(
        step,
        mesh=mesh,
        in_specs=(P(("rows", "cent"), None), P("cent", None), P("rows")),
        out_specs=(P("cent", None), P("cent", None), P(("rows", "cent"))),
        check_vma=False,
    )
```

```python
import functools
import math

import jax
import jax.numpy as jnp
from jax import lax
from jax.experimental import pallas as pl
from jax.experimental.pallas import tpu as pltpu
from jax.sharding import PartitionSpec as P

score_factor = 3.0
prior_weight = 1.0
MESH = pl.DeviceIdType.MESH
contract_width = (((1,), (1,)), ((), ()))
contract_rows = (((1,), (0,)), ((), ()))


lanes = 128
masked = 1e30


def sums_kernel(
    groups, shards, column_step, split,
    length_ref, emb_hbm, cent_hbm,
    cent_out, mom_out, lik_out, inverse_out,
    cent_ref, rows_all, squares, weights, parts, stats, masses,
    own_sem, cent_sem, z_send, z_recv, y_send, y_recv, c_send, c_recv,
    p_send, p_recv, s_send, s_recv, m_send, m_recv,
):
    g = lax.axis_index("rows")
    i = lax.axis_index("cent")
    row_count, width = emb_hbm.shape
    cents = cent_ref.shape[0]
    total = shards * row_count
    piece_rows = row_count // split
    line = shards // 4
    spot = lax.rem(i, 4)
    place = i // 4
    core = lax.rem(i, 2)
    core_peer = i + 1 - 2 * core
    y_spot = lax.rem(spot + 2, 4)
    y_peer = place * 4 + y_spot
    factor = score_factor / math.sqrt(width)

    def across(step):
        return lax.rem(g + step, groups)

    def signal(peer):
        pl.semaphore_signal(barrier, inc=1, device_id=peer, device_id_type=MESH)

    barrier = pltpu.get_barrier_semaphore()
    for peer in [(g, y_peer), (g, core_peer)] + [(across(s), i) for s in range(1, groups)]:
        signal(peer)
    has_right = place < line - 1
    has_left = place > 0
    pl.when(has_right)(lambda: signal((g, i + 4)))
    pl.when(has_left)(lambda: signal((g, i - 4)))
    own = [
        pltpu.make_async_copy(
            emb_hbm.at[pl.ds(h * piece_rows, piece_rows)], rows_all.at[i * split + h], own_sem.at[h]
        )
        for h in range(split)
    ]
    for copy in own:
        copy.start()
    cent_copy = pltpu.make_async_copy(cent_hbm, cent_ref, cent_sem)
    cent_copy.start()
    for copy in own:
        copy.wait()
    sides = has_right.astype(jnp.int32) + has_left.astype(jnp.int32)
    pl.semaphore_wait(barrier, 1 + groups + sides)

    def describe(src, dst, send_sem, recv_sem, peer):
        return pltpu.make_async_remote_copy(
            src_ref=src, dst_ref=dst, send_sem=send_sem, recv_sem=recv_sem,
            device_id=peer, device_id_type=MESH,
        )

    def send(*spec):
        copy = describe(*spec)
        copy.start()
        return copy

    def z_copy(unit, way, s, h):
        slot = rows_all.at[unit]
        peer = (g, i + 4 if way == 0 else i - 4)
        return describe(slot, slot, z_send.at[way, s, h], z_recv.at[way, s, h], peer)

    def y_copy(unit, k, h):
        slot = rows_all.at[unit]
        return describe(slot, slot, y_send.at[k, h], y_recv.at[k, h], (g, y_peer))

    def c_copy(unit, k, h):
        slot = rows_all.at[unit]
        return describe(slot, slot, c_send.at[k, h], c_recv.at[k, h], (g, core_peer))

    def square(unit):
        wide = rows_all[unit].astype(jnp.float32)
        squares[unit] = (wide * wide).astype(jnp.bfloat16)

    steps = 2 * line - 1
    order = [(way, s) for s in range(1, line) for way in range(2)]

    def present(way, s):
        return place >= s if way == 0 else place + s < line

    def unit_of(way, s, where, h):
        source = place - s if way == 0 else place + s
        return (source * 4 + where) * split + h

    for h in range(split):
        unit = i * split + h
        pl.when(has_right)(lambda: z_copy(unit, 0, 1, h).start())
        pl.when(has_left)(lambda: z_copy(unit, 1, 1, h).start())
        y_copy(unit, 0, h).start()
        c_copy(unit, 0, h).start()
    for h in range(split):
        square(i * split + h)
    for k, (way, s) in enumerate(order, 1):
        for h in range(split):
            def relay():
                unit = unit_of(way, s, spot, h)
                z_copy(unit, way, s, h).wait_recv()
                onward = has_right if way == 0 else has_left
                if s + 1 < line:
                    pl.when(onward)(lambda: z_copy(unit, way, s + 1, h).start())
                y_copy(unit, k, h).start()
                c_copy(unit, k, h).start()
                square(unit)

            pl.when(present(way, s))(relay)
    for h in range(split):
        unit = unit_of(0, 0, y_spot, h)
        y_copy(unit, 0, h).wait_recv()
        c_copy(unit, steps, h).start()
        square(unit)
    for k, (way, s) in enumerate(order, 1):
        for h in range(split):
            def pass_on():
                unit = unit_of(way, s, y_spot, h)
                y_copy(unit, k, h).wait_recv()
                c_copy(unit, steps + k, h).start()
                square(unit)

            pl.when(present(way, s))(pass_on)
    other = spot + 1 - 2 * core
    for j, where in enumerate((other, lax.rem(other + 2, 4))):
        for h in range(split):
            unit = unit_of(0, 0, where, h)
            c_copy(unit, j * steps, h).wait_recv()
            square(unit)
        for k, (way, s) in enumerate(order, 1):
            for h in range(split):
                def take():
                    unit = unit_of(way, s, where, h)
                    c_copy(unit, j * steps + k, h).wait_recv()
                    square(unit)

                pl.when(present(way, s))(take)
    sent = []
    cent_copy.wait()
    cent_wide = cent_ref[...].astype(jnp.float32)
    half_norm = 0.5 * jnp.sum(cent_wide * cent_wide, axis=1, keepdims=True)

    slots = split * max(1, min(shards, 512 // row_count))
    chunk = slots * piece_rows
    chunks = shards * split // slots

    def score(k, carry):
        first = k * slots
        columns = k * chunk
        if not isinstance(k, int):
            columns = pl.multiple_of(columns, chunk)
        block = rows_all[pl.ds(first, slots)].reshape(chunk, width)
        inner = lax.dot_general(
            cent_ref[...], block, contract_width, preferred_element_type=jnp.float32
        )
        logits = factor * (inner - half_norm)
        peak = jnp.max(logits, axis=0, keepdims=True)
        weight = jnp.exp(logits - peak)
        weights[:, pl.ds(columns, chunk)] = weight
        parts[0, 0:1, pl.ds(columns, chunk)] = peak
        parts[0, 1:2, pl.ds(columns, chunk)] = jnp.sum(weight, axis=0, keepdims=True)
        return carry

    for k in range(chunks) if chunks <= 4 else ():
        score(k, 0)
    if chunks > 4:
        lax.fori_loop(0, chunks, score, 0)

    own_peak = parts[0, 0:1, :]

    def joined(part_list):
        highest = part_list[0][0]
        for peak, _ in part_list[1:]:
            highest = jnp.maximum(highest, peak)
        amount = None
        for peak, exp_sum in part_list:
            term = exp_sum * jnp.exp(peak - highest)
            amount = term if amount is None else amount + term
        return highest, amount

    def part(k):
        return parts[k, 0:1, :], parts[k, 1:2, :]

    hop = send(parts.at[0], parts.at[1], p_send.at[0], p_recv.at[0], (g, core_peer))

    hop.wait()
    peak, amount = joined([part(0), part(1)])
    parts[2, 0:1, :] = peak
    parts[2, 1:2, :] = amount
    hops = []
    for k in range(2 * line - 1, 0, -1):
        peer = lax.rem(place + k // 2, line) * 4 + lax.rem(spot + 2 * (k % 2), 4)
        hops.append(send(parts.at[2], parts.at[2 + k], p_send.at[k], p_recv.at[k], (g, peer)))
    for hop in hops:
        hop.wait_recv()
    sent += hops
    peak, amount = joined([part(2 + k) for k in range(2 * line)])
    lse = peak + jnp.log(amount)
    valid = lax.broadcasted_iota(jnp.int32, (1, total), 1) < length_ref[0]
    scale = jnp.where(valid, jnp.exp(own_peak - lse), 0.0)
    resp = (weights[...] * scale).astype(jnp.bfloat16)

    ones = jnp.ones((8, total), jnp.bfloat16)
    masses[g] = lax.dot_general(ones, resp, contract_width, preferred_element_type=jnp.float32)
    s_copies = {}
    for s in range(1, groups):
        sent.append(
            send(masses.at[g], masses.at[g], m_send.at[s], m_recv.at[s], (across(s), i))
        )
    m_copies = sent[len(sent) - (groups - 1):]
    pieces = 2 * (width // column_step)
    for k in range(pieces):
        left = (k // 2) * column_step
        source = rows_all if k % 2 == 0 else squares
        block = source[:, :, left:left + column_step].reshape(total, column_step)
        sums = lax.dot_general(resp, block, contract_rows, preferred_element_type=jnp.float32)
        stats[g, k] = sums.astype(jnp.bfloat16)
        for s in range(1, groups):
            s_copies[k, s] = send(
                stats.at[g, k], stats.at[g, k], s_send.at[k, s], s_recv.at[k, s], (across(s), i)
            )

    own_lik = jnp.where(valid, lse, 0.0)
    pick = own_lik[:, 0:row_count]
    for j in range(1, shards):
        pick = jnp.where(i == j, own_lik[:, j * row_count:(j + 1) * row_count], pick)
    lik_out[...] = pick

    for copy in m_copies:
        copy.wait_recv()
    mass = masses[0, 0:1, :]
    for r in range(1, groups):
        mass = mass + masses[r, 0:1, :]
    inverse = 1.0 / (mass + prior_weight)
    inverse_out[...] = jnp.transpose(jnp.broadcast_to(inverse, (cents, cents)))
    for k in range(pieces):
        for s in range(1, groups):
            s_copies[k, s].wait_recv()
        left = (k // 2) * column_step
        sums = stats[0, k].astype(jnp.float32)
        for r in range(1, groups):
            sums = sums + stats[r, k].astype(jnp.float32)
        if k % 2 == 0:
            sums = sums + prior_weight * cent_ref[:, left:left + column_step].astype(jnp.float32)
            cent_out[:, left:left + column_step] = sums
        else:
            mom_out[:, left:left + column_step] = sums + prior_weight
    for h in range(split):
        unit = i * split + h
        pl.when(has_right)(lambda: z_copy(unit, 0, 1, h).wait_send())
        pl.when(has_left)(lambda: z_copy(unit, 1, 1, h).wait_send())
        y_copy(unit, 0, h).wait_send()
        c_copy(unit, 0, h).wait_send()
        c_copy(unit_of(0, 0, y_spot, h), steps, h).wait_send()
    for k, (way, s) in enumerate(order, 1):
        for h in range(split):
            def finish():
                unit = unit_of(way, s, spot, h)
                onward = has_right if way == 0 else has_left
                if s + 1 < line:
                    pl.when(onward)(lambda: z_copy(unit, way, s + 1, h).wait_send())
                y_copy(unit, k, h).wait_send()
                c_copy(unit, k, h).wait_send()
                c_copy(unit_of(way, s, y_spot, h), steps + k, h).wait_send()

            pl.when(present(way, s))(finish)
    for copy in sent + list(s_copies.values()):
        copy.wait_send()


def gather_kernel(
    shards, split, turn, cross,
    length_ref, emb_hbm, cent_hbm,
    cent_out, mom_out, lik_out, inverse_out,
    cents_all, rows_all, squares, weights, resp, peaks, parts, lse_ref,
    own_sem, cent_sem, ready, know, z_send, z_recv, w_send, w_recv, y_send, y_recv, o_recv,
    x_send, x_recv, d_recv, c_send, c_recv, k_send, k_recv, p_send, p_recv,
):
    g = lax.axis_index("rows")
    i = lax.axis_index("cent")
    row_count, width = emb_hbm.shape
    cents = cents_all.shape[1]
    total = shards * row_count
    piece = row_count // split
    line = shards // 4
    chunk = 4 * row_count
    spread = chunk // lanes
    spot = lax.rem(i, 4)
    place = i // 4
    core = lax.rem(i, 2)
    core_peer = i + 1 - 2 * core
    core_spot = spot + 1 - 2 * core
    y_spot = lax.rem(spot + 2, 4)
    core_y_spot = lax.rem(core_spot + 2, 4)
    y_peer = place * 4 + y_spot
    there = 1 - g
    factor = score_factor / math.sqrt(width)

    def signal(sem, peer):
        pl.semaphore_signal(sem, inc=1, device_id=peer, device_id_type=MESH)

    barrier = pltpu.get_barrier_semaphore()
    has_right = place < line - 1
    has_left = place > 0
    pl.when(has_right)(lambda: signal(barrier, (g, i + 4)))
    pl.when(has_left)(lambda: signal(barrier, (g, i - 4)))
    for peer in [(g, y_peer), (there, i), (g, core_peer)]:
        signal(barrier, peer)
    own = pltpu.make_async_copy(emb_hbm, rows_all.at[g, i], own_sem)
    own.start()
    cent_copy = pltpu.make_async_copy(cent_hbm, cents_all.at[0], cent_sem)
    cent_copy.start()
    own.wait()
    sides = has_right.astype(jnp.int32) + has_left.astype(jnp.int32)
    pl.semaphore_wait(barrier, 3 + sides)

    def move(ref, send_sem, recv_sem, peer):
        return pltpu.make_async_remote_copy(
            src_ref=ref, dst_ref=ref, send_sem=send_sem, recv_sem=recv_sem,
            device_id=peer, device_id_type=MESH,
        )

    def slot(group, q, where, h):
        if h is None:
            return rows_all.at[group, q * 4 + where]
        return rows_all.at[group, q * 4 + where, pl.ds(h * piece, piece)]

    def column(side):
        return spot if side == 0 else y_spot

    def z_own(way, s, h):
        peer = (g, i + 4 * s if way == 0 else i - 4 * s)
        return move(slot(g, place, spot, h), z_send, z_recv.at[place, h], peer)

    def z_move(way, q, h):
        peer = (g, i + 4 if way == 0 else i - 4)
        return move(slot(g, q, spot, h), z_send, z_recv.at[q, h], peer)

    def low(ref, q, where):
        return ref.at[g, q * 4 + where, pl.ds(0, cross)]

    def high(ref, q, where):
        return ref.at[g, q * 4 + where, pl.ds(cross, row_count - cross)]

    def y_move(q, h):
        return move(slot(g, q, spot, h), y_send, y_recv.at[q], (g, y_peer))

    def y_own():
        return move(low(rows_all, place, spot), y_send, y_recv.at[place], (g, y_peer))

    def y_come(q):
        return move(low(rows_all, q, y_spot), y_send, y_recv.at[q], (g, y_peer))

    def o_own():
        return move(high(rows_all, place, spot), w_send, o_recv, (g, y_peer))

    def o_come():
        return move(high(rows_all, place, y_spot), w_send, o_recv, (g, y_peer))

    def w_move(way, q, s):
        peer = (g, i + 4 * s if way == 0 else i - 4 * s)
        return move(high(rows_all, q, y_spot), w_send, w_recv.at[q], peer)

    def cent_move(src, k, sem, peer):
        return pltpu.make_async_remote_copy(
            src_ref=cent_hbm if src is None else cents_all.at[src], dst_ref=cents_all.at[k],
            send_sem=k_send.at[sem], recv_sem=k_recv.at[k - 1], device_id=(g, peer), device_id_type=MESH,
        )

    def cent_come(k):
        return move(cents_all.at[k], k_send.at[0], k_recv.at[k - 1], (g, y_peer))

    def part(group, q, where, side):
        rows = pl.ds(0, turn) if side == 0 else pl.ds(turn, row_count - turn)
        return rows_all.at[group, q * 4 + where, rows]

    def x_move(q, h):
        return move(slot(g, q, spot, h), x_send, x_recv.at[q, 0], (there, i))

    def x_come(q):
        return move(slot(there, q, spot, None), x_send, x_recv.at[q, 0], (there, i))

    def x_turn(q):
        return move(part(g, q, y_spot, 0), x_send, x_recv.at[q, 1], (there, i))

    def x_turned(q):
        return move(part(there, q, y_spot, 0), x_send, x_recv.at[q, 1], (there, i))

    def y_turn(q):
        return move(part(there, q, spot, 1), y_send, d_recv.at[q], (g, y_peer))

    def y_turned(q):
        return move(part(there, q, y_spot, 1), y_send, d_recv.at[q], (g, y_peer))

    def c_low(q):
        return move(low(rows_all, q, y_spot), c_send, c_recv.at[0, q], (g, core_peer))

    def c_high(q):
        return move(high(rows_all, q, y_spot), c_send, c_recv.at[0, q], (g, core_peer))

    def c_turn(q, side):
        return move(part(there, q, y_spot, side), c_send, c_recv.at[1, q], (g, core_peer))

    def c_move(mine, q, side, h):
        ref = slot(g if mine else there, q, column(side), h)
        return move(ref, c_send, c_recv.at[0 if mine else 1, q], (g, core_peer))

    def c_come(mine, q):
        ref = rows_all.at[g if mine else there, pl.ds(q * 4, 2)]
        return move(ref, c_send, c_recv.at[0 if mine else 1, q], (g, core_peer))

    def source(way, s):
        return place - s if way == 0 else place + s

    def present(way, s):
        return place >= s if way == 0 else place + s < line

    def starts(way):
        return has_right if way == 0 else has_left

    def onward(way, s):
        if way == 0:
            return jnp.logical_and(place > s, has_right)
        return jnp.logical_and(place + s < line - 1, has_left)

    def ends(way):
        return place == 0 if way == 0 else place == line - 1

    def both(fn, cond):
        for way in range(2):
            pl.when(cond(way))(functools.partial(fn, way))

    def z_take(way, s, h):
        def take():
            q = source(way, s)
            z_move(way, q, h).wait_recv()
            if s + 1 < line:
                pl.when(onward(way, s))(lambda: z_move(way, q, h).start())
            if h * piece < cross:
                y_move(q, h).start()
            x_move(q, h).start()
            c_move(True, q, 0, h).start()

        pl.when(present(way, s))(take)

    def at(way, s, fn):
        if s == 0:
            fn(place)
        else:
            pl.when(present(way, s))(lambda: fn(source(way, s)))

    def y_take(q):
        y_come(q).wait_recv()
        x_turn(q).start()
        c_low(q).start()

    def x_take(q):
        x_come(q).wait_recv()
        y_turn(q).start()
        c_move(False, q, 0, None).start()

    def turn_take(q):
        x_turned(q).wait_recv()
        c_turn(q, 0).start()
        y_turned(q).wait_recv()
        c_turn(q, 1).start()

    def w_take(way, s):
        def take():
            q = source(way, s)
            w_move(way, q, 1).wait_recv()
            if s + 1 < line:
                pl.when(onward(way, s))(lambda: w_move(way, q, 1).start())
            c_high(q).start()

        if cross < row_count:
            pl.when(present(way, s))(take)

    def nth(j):
        orders = [sorted(range(line), key=lambda q: abs(q - p)) for p in range(line)]
        q = orders[0][j]
        for p in range(1, line):
            q = jnp.where(place == p, orders[p][j], q)
        return q

    near = [(way, 1) for way in range(2)]
    far = [(way, s) for s in range(2, line) for way in range(2)]
    for h in range(split):
        both(lambda way: z_own(way, 1, h).start(), starts)
    if cross < row_count:
        o_own().start()
    cent_move(None, 2, 0, y_peer).start()
    y_own().start()
    x_move(place, None).start()
    cent_move(None, 1, 1, core_peer).start()
    c_move(True, place, 0, None).start()

    cube = [(g, y_peer), (there, i), (g, core_peer)]
    for peer in cube:
        signal(know.at[0], peer)
    if line > 2:
        pl.when(jnp.logical_and(place == 1, has_right))(lambda: signal(ready.at[0], (g, i + 4)))
        pl.when(jnp.logical_and(place == line - 2, has_left))(lambda: signal(ready.at[1], (g, i - 4)))

        def pass_up():
            pl.semaphore_wait(ready.at[0], 1)
            pl.when(has_right)(lambda: signal(ready.at[0], (g, i + 4)))

        def pass_down():
            pl.semaphore_wait(ready.at[1], 1)
            pl.when(has_left)(lambda: signal(ready.at[1], (g, i - 4)))

        pl.when(place >= 2)(pass_up)
        pl.when(place <= line - 3)(pass_down)

        def far_go(way):
            for h in range(split):
                for s in range(2, line):
                    z_own(way, s, h).start()

        both(far_go, ends)

    cent_copy.wait()
    cent_wide = cents_all[0].astype(jnp.float32)
    half_norm = 0.5 * jnp.sum(cent_wide * cent_wide, axis=1, keepdims=True)

    def score(mine, q):
        t = 0 if mine else 1
        c_come(mine, q).wait_recv()
        group = g if mine else there
        block = rows_all[group, pl.ds(q * 4, 4)].reshape(chunk, width)
        inner = lax.dot_general(
            cents_all[0], block, contract_width, preferred_element_type=jnp.float32
        )
        logits = factor * (inner - half_norm)
        peak = jnp.max(logits, axis=0, keepdims=True)
        weights[t, q] = jnp.exp(logits - peak)
        for r in range(spread):
            peaks[t, q, r:r + 1, :] = peak[:, r * lanes:(r + 1) * lanes]
        wide = block.astype(jnp.float32)
        squares[group, pl.ds(q * 4, 4)] = (wide * wide).astype(jnp.bfloat16).reshape(
            4, row_count, width
        )

    def partial_lse(all_half, q):
        block = rows_all[g, q * 4 + spot]
        inner = lax.dot_general(
            cents_all[...].reshape(4 * cents, width), block, contract_width,
            preferred_element_type=jnp.float32,
        )
        logits = factor * (inner - all_half)
        peak = jnp.max(logits, axis=0, keepdims=True)
        value = peak + jnp.log(jnp.sum(jnp.exp(logits - peak), axis=0, keepdims=True))
        row = (q * 4 + spot) * row_count + lax.broadcasted_iota(jnp.int32, value.shape, 1)
        parts[g, i, pl.ds(q, 1), :] = jnp.where(row < length_ref[0], value, masked)

    for h in range(split):
        for way in range(2):
            z_take(way, 1, h)
    pl.semaphore_wait(know.at[0], 3)
    for peer in cube:
        signal(know.at[1], peer)
    if cross < row_count:
        o_come().wait_recv()
        both(lambda way: w_move(way, place, 1).start(), starts)

        def w_far(way):
            for s in range(2, line):
                w_move(way, place, s).start()

        if line > 2:
            both(w_far, ends)
        c_high(place).start()
    for h in range(split // 2):
        for way, s in far:
            z_take(way, s, h)
    pl.semaphore_wait(know.at[1], 3)
    for q in range(1, line):
        signal(know.at[2], (g, lax.rem(place + q, line) * 4 + spot))
    cent_come(2).wait_recv()
    cent_move(2, 3, 2, core_peer).start()
    y_take(place)
    x_take(place)
    for k in (1, 3):
        cent_come(k).wait_recv()
    wide = cents_all[...].reshape(4 * cents, width).astype(jnp.float32)
    all_half = 0.5 * jnp.sum(wide * wide, axis=1, keepdims=True)
    partial_lse(all_half, place)
    for way, s in near:
        at(way, s, functools.partial(partial_lse, all_half))
    for h in range(split // 2, split):
        for way, s in far:
            z_take(way, s, h)
    for way, s in far:
        at(way, s, functools.partial(partial_lse, all_half))

    pl.semaphore_wait(know.at[2], line - 1)
    mine_part = parts.at[g, i]
    for k in range(shards - 1, -1, -1):
        peer = lax.rem(i + k, shards)
        for group, t in ((there, 1), (g, 0)):
            if k > 0 or t:
                move_to = pltpu.make_async_remote_copy(
                    src_ref=mine_part, dst_ref=mine_part, send_sem=p_send.at[t],
                    recv_sem=p_recv.at[t], device_id=(group, peer), device_id_type=MESH,
                )
                move_to.start()

    def joined(values):
        highest = values[0]
        for value in values[1:]:
            highest = jnp.maximum(highest, value)
        amount = jnp.exp(values[0] - highest)
        for value in values[1:]:
            amount = amount + jnp.exp(value - highest)
        return highest + jnp.log(amount)

    def move_parts(group, count, k):
        return move(parts.at[group, pl.ds(0, count)], p_send.at[k], p_recv.at[k], (g, y_peer))

    def whole_lse(group):
        return [joined([parts[group, p * 4 + w] for p in range(line)]) for w in range(4)]

    ones = jnp.ones((8, total), jnp.bfloat16)

    def weigh(t, q, place_in_resp):
        for r in range(spread):
            left = r * lanes
            scale = jnp.exp(peaks[t, q, r:r + 1, :] - lse_ref[t, r, pl.ds(q, 1), :])
            resp[:, place_in_resp * chunk + left:place_in_resp * chunk + left + lanes] = (
                weights[t, q, :, left:left + lanes] * scale
            ).astype(jnp.bfloat16)

    def times(left, right):
        return lax.dot_general(left, right, contract_rows, preferred_element_type=jnp.float32)

    def mass_of(block):
        return lax.dot_general(
            ones[:, :block.shape[1]], block, contract_width, preferred_element_type=jnp.float32
        )

    def keep_lse(t, lse):
        for r in range(spread):
            lse_ref[t, r] = jnp.concatenate([lse[2 * r], lse[2 * r + 1]], axis=1)

    def add_there(orders):
        mass = 0.0
        weighted = cent_out[...]
        moments = mom_out[...]
        for n, q in enumerate(orders):
            weigh(1, q, n)
            block = resp[:, n * chunk:(n + 1) * chunk]
            mass = mass + mass_of(block)
            weighted = weighted + times(block, rows_all[there, pl.ds(q * 4, 4)].reshape(chunk, width))
            moments = moments + times(block, squares[there, pl.ds(q * 4, 4)].reshape(chunk, width))
        cent_out[...] = weighted
        mom_out[...] = moments
        return mass

    places = [place] + [nth(j) for j in range(1, line)]
    half = line // 2
    for way, s in near:
        w_take(way, s)
    for j in range(1, half):
        y_take(places[j])
        x_take(places[j])
    score(True, place)
    for way, s in far:
        w_take(way, s)
    for j in range(half, line):
        y_take(places[j])
        x_take(places[j])
    for j in range(1, half):
        score(True, places[j])
    for j in range(half):
        turn_take(places[j])
    for j in range(half, line):
        score(True, places[j])

    move_parts(g, shards - 1, 0).wait_recv()
    lse = whole_lse(g)
    keep_lse(0, lse)
    for q in range(line):
        weigh(0, q, q)
    mass = mass_of(resp[...])
    cent_out[...] = prior_weight * cent_wide + times(
        resp[...], rows_all[g].reshape(total, width)
    )
    mom_out[...] = prior_weight + times(resp[...], squares[g].reshape(total, width))
    for j in range(half):
        score(False, places[j])
    move_parts(there, shards, 1).wait_recv()
    keep_lse(1, whole_lse(there))
    mass = mass + add_there(places[:half])
    for j in range(half, line):
        turn_take(places[j])
    pick = lse[0]
    for w in range(1, 4):
        pick = jnp.where(spot == w, lse[w], pick)
    own_lik = pick[0:1]
    for q in range(1, line):
        own_lik = jnp.where(place == q, pick[q:q + 1], own_lik)
    row = i * row_count + lax.broadcasted_iota(jnp.int32, own_lik.shape, 1)
    lik_out[...] = jnp.where(row < length_ref[0], own_lik, 0.0)
    for j in range(half, line):
        score(False, places[j])
    mass = mass + add_there(places[half:])
    inverse = 1.0 / (mass[0:1, :] + prior_weight)
    inverse_out[...] = jnp.transpose(jnp.broadcast_to(inverse, (cents, cents)))

    def drain(sem, count):
        step = max(b for b in range(piece, row_count + 1, piece) if count % b == 0)
        rows = rows_all.at[g, pl.ds(0, count // step), pl.ds(0, step)]
        move(rows, sem, own_sem, (g, y_peer)).wait_send()

    drain(z_send, (line - 1) * row_count)
    drain(y_send, line * (cross + row_count - turn))
    drain(x_send, line * (row_count + turn))
    drain(c_send, 4 * line * row_count)
    if cross < row_count:
        drain(w_send, line * (row_count - cross))
    for k in range(3):
        move(cents_all.at[1], k_send.at[k], own_sem, (g, y_peer)).wait_send()
    move_parts(g, shards - 1, 0).wait_send()
    move_parts(there, shards, 1).wait_send()


def gather_call(shards, row_count, width, cents, out_shape):
    line = shards // 4
    split = 4
    cross = row_count // 2
    turn = row_count // 2
    total = shards * row_count
    spread = 4 * row_count // lanes
    vmem = pl.BlockSpec(memory_space=pltpu.VMEM)
    hbm = pl.BlockSpec(memory_space=pltpu.HBM)
    dma = pltpu.SemaphoreType.DMA
    regular = pltpu.SemaphoreType.REGULAR
    return pl.pallas_call(
        functools.partial(gather_kernel, shards, split, turn, cross),
        out_shape=out_shape,
        in_specs=[pl.BlockSpec(memory_space=pltpu.SMEM), hbm, hbm],
        out_specs=(vmem, vmem, vmem, vmem),
        scratch_shapes=[
            pltpu.VMEM((4, cents, width), jnp.bfloat16),
            pltpu.VMEM((2, shards, row_count, width), jnp.bfloat16),
            pltpu.VMEM((2, shards, row_count, width), jnp.bfloat16),
            pltpu.VMEM((2, line, cents, 4 * row_count), jnp.float32),
            pltpu.VMEM((cents, total), jnp.bfloat16),
            pltpu.VMEM((2, line, spread, lanes), jnp.float32),
            pltpu.VMEM((2, shards, line, row_count), jnp.float32),
            pltpu.VMEM((2, spread, line, lanes), jnp.float32),
            dma, dma, regular((2,)), regular((3,)),
            dma, dma((line, split)), dma, dma((line,)), dma, dma((line,)), dma,
            dma, dma((line, 2)), dma((line,)), dma, dma((2, line)), dma((3,)), dma((3,)),
            dma((2,)), dma((2,)),
        ],
        compiler_params=pltpu.CompilerParams(
            collective_id=0, has_side_effects=True, vmem_limit_bytes=32 * 1024 * 1024
        ),
        name="soft_em",
    )


def solution(mesh):
    groups = mesh.shape["rows"]
    shards = mesh.shape["cent"]
    line = shards // 4

    def step(embeddings, centroids, group_length):
        row_count, width = embeddings.shape
        cents = centroids.shape[0]
        total = row_count * shards
        column_step = 256 if width % 256 == 0 else width
        pieces = 2 * (width // column_step)
        split = 2 if row_count % 32 == 0 else 1
        vmem = pl.BlockSpec(memory_space=pltpu.VMEM)
        hbm = pl.BlockSpec(memory_space=pltpu.HBM)
        held = 4 * total * width + 4 * cents * total + 2 * (groups * 2 + 1) * cents * width
        steps = 2 * line - 1
        dma = pltpu.SemaphoreType.DMA
        out_shape = (
            jax.ShapeDtypeStruct((cents, width), jnp.float32),
            jax.ShapeDtypeStruct((cents, width), jnp.float32),
            jax.ShapeDtypeStruct((1, row_count), jnp.float32),
            jax.ShapeDtypeStruct((cents, cents), jnp.float32),
        )
        if groups == 2 and shards % 4 == 0 and shards > 4 and row_count % 64 == 0 and total <= 2048:
            call = gather_call(shards, row_count, width, cents, out_shape)
        else:
            call = pl.pallas_call(
                functools.partial(sums_kernel, groups, shards, column_step, split),
                out_shape=out_shape,
                in_specs=[pl.BlockSpec(memory_space=pltpu.SMEM), hbm, hbm],
                out_specs=(vmem, vmem, vmem, vmem),
                scratch_shapes=[
                    pltpu.VMEM((cents, width), jnp.bfloat16),
                    pltpu.VMEM((shards * split, row_count // split, width), jnp.bfloat16),
                    pltpu.VMEM((shards * split, row_count // split, width), jnp.bfloat16),
                    pltpu.VMEM((cents, total), jnp.float32),
                    pltpu.VMEM((2 + 2 * line, 2, total), jnp.float32),
                    pltpu.VMEM((groups, pieces, cents, column_step), jnp.bfloat16),
                    pltpu.VMEM((groups, 8, cents), jnp.float32),
                    dma((split,)), dma, dma((2, line, split)), dma((2, line, split)),
                    dma((steps, split)), dma((steps, split)),
                    dma((2 * steps, split)), dma((2 * steps, split)),
                    dma((2 * line,)), dma((2 * line,)),
                    dma((pieces, groups)), dma((pieces, groups)),
                    dma((groups,)), dma((groups,)),
                ],
                compiler_params=pltpu.CompilerParams(
                    collective_id=0, has_side_effects=True, vmem_limit_bytes=2 * held + 4 * 1024 * 1024
                ),
                name="soft_em",
            )
        cent_sums, moment_sums, loglik, inverse = call(group_length, pltpu.with_memory_space_constraint(embeddings, pltpu.HBM), pltpu.with_memory_space_constraint(centroids, pltpu.HBM))
        new_centroids = (cent_sums * inverse[:, 0:1]).astype(jnp.bfloat16)
        new_moments = (moment_sums * inverse[:, 0:1]).astype(jnp.bfloat16)
        return new_centroids, new_moments, loglik.reshape(row_count)

    return jax.shard_map(
        step,
        mesh=mesh,
        in_specs=(P(("rows", "cent"), None), P("cent", None), P("rows")),
        out_specs=(P("cent", None), P("cent", None), P(("rows", "cent"))),
        check_vma=False,
    )
```

```python
import functools
import math

import jax
import jax.numpy as jnp
from jax import lax
from jax.experimental import pallas as pl
from jax.experimental.pallas import tpu as pltpu
from jax.sharding import PartitionSpec as P

score_factor = 3.0
prior_weight = 1.0
MESH = pl.DeviceIdType.MESH
contract_width = (((1,), (1,)), ((), ()))
contract_rows = (((1,), (0,)), ((), ()))


lanes = 128
masked = 1e30


def sums_kernel(
    groups, shards, column_step, split,
    length_ref, emb_hbm, cent_hbm,
    cent_out, mom_out, lik_out, inverse_out,
    cent_ref, rows_all, squares, weights, parts, stats, masses,
    own_sem, cent_sem, z_send, z_recv, y_send, y_recv, c_send, c_recv,
    p_send, p_recv, s_send, s_recv, m_send, m_recv,
):
    g = lax.axis_index("rows")
    i = lax.axis_index("cent")
    row_count, width = emb_hbm.shape
    cents = cent_ref.shape[0]
    total = shards * row_count
    piece_rows = row_count // split
    line = shards // 4
    spot = lax.rem(i, 4)
    place = i // 4
    core = lax.rem(i, 2)
    core_peer = i + 1 - 2 * core
    y_spot = lax.rem(spot + 2, 4)
    y_peer = place * 4 + y_spot
    factor = score_factor / math.sqrt(width)

    def across(step):
        return lax.rem(g + step, groups)

    def signal(peer):
        pl.semaphore_signal(barrier, inc=1, device_id=peer, device_id_type=MESH)

    barrier = pltpu.get_barrier_semaphore()
    for peer in [(g, y_peer), (g, core_peer)] + [(across(s), i) for s in range(1, groups)]:
        signal(peer)
    has_right = place < line - 1
    has_left = place > 0
    pl.when(has_right)(lambda: signal((g, i + 4)))
    pl.when(has_left)(lambda: signal((g, i - 4)))
    own = [
        pltpu.make_async_copy(
            emb_hbm.at[pl.ds(h * piece_rows, piece_rows)], rows_all.at[i * split + h], own_sem.at[h]
        )
        for h in range(split)
    ]
    for copy in own:
        copy.start()
    cent_copy = pltpu.make_async_copy(cent_hbm, cent_ref, cent_sem)
    cent_copy.start()
    for copy in own:
        copy.wait()
    sides = has_right.astype(jnp.int32) + has_left.astype(jnp.int32)
    pl.semaphore_wait(barrier, 1 + groups + sides)

    def describe(src, dst, send_sem, recv_sem, peer):
        return pltpu.make_async_remote_copy(
            src_ref=src, dst_ref=dst, send_sem=send_sem, recv_sem=recv_sem,
            device_id=peer, device_id_type=MESH,
        )

    def send(*spec):
        copy = describe(*spec)
        copy.start()
        return copy

    def z_copy(unit, way, s, h):
        slot = rows_all.at[unit]
        peer = (g, i + 4 if way == 0 else i - 4)
        return describe(slot, slot, z_send.at[way, s, h], z_recv.at[way, s, h], peer)

    def y_copy(unit, k, h):
        slot = rows_all.at[unit]
        return describe(slot, slot, y_send.at[k, h], y_recv.at[k, h], (g, y_peer))

    def c_copy(unit, k, h):
        slot = rows_all.at[unit]
        return describe(slot, slot, c_send.at[k, h], c_recv.at[k, h], (g, core_peer))

    def square(unit):
        wide = rows_all[unit].astype(jnp.float32)
        squares[unit] = (wide * wide).astype(jnp.bfloat16)

    steps = 2 * line - 1
    order = [(way, s) for s in range(1, line) for way in range(2)]

    def present(way, s):
        return place >= s if way == 0 else place + s < line

    def unit_of(way, s, where, h):
        source = place - s if way == 0 else place + s
        return (source * 4 + where) * split + h

    for h in range(split):
        unit = i * split + h
        pl.when(has_right)(lambda: z_copy(unit, 0, 1, h).start())
        pl.when(has_left)(lambda: z_copy(unit, 1, 1, h).start())
        y_copy(unit, 0, h).start()
        c_copy(unit, 0, h).start()
    for h in range(split):
        square(i * split + h)
    for k, (way, s) in enumerate(order, 1):
        for h in range(split):
            def relay():
                unit = unit_of(way, s, spot, h)
                z_copy(unit, way, s, h).wait_recv()
                onward = has_right if way == 0 else has_left
                if s + 1 < line:
                    pl.when(onward)(lambda: z_copy(unit, way, s + 1, h).start())
                y_copy(unit, k, h).start()
                c_copy(unit, k, h).start()
                square(unit)

            pl.when(present(way, s))(relay)
    for h in range(split):
        unit = unit_of(0, 0, y_spot, h)
        y_copy(unit, 0, h).wait_recv()
        c_copy(unit, steps, h).start()
        square(unit)
    for k, (way, s) in enumerate(order, 1):
        for h in range(split):
            def pass_on():
                unit = unit_of(way, s, y_spot, h)
                y_copy(unit, k, h).wait_recv()
                c_copy(unit, steps + k, h).start()
                square(unit)

            pl.when(present(way, s))(pass_on)
    other = spot + 1 - 2 * core
    for j, where in enumerate((other, lax.rem(other + 2, 4))):
        for h in range(split):
            unit = unit_of(0, 0, where, h)
            c_copy(unit, j * steps, h).wait_recv()
            square(unit)
        for k, (way, s) in enumerate(order, 1):
            for h in range(split):
                def take():
                    unit = unit_of(way, s, where, h)
                    c_copy(unit, j * steps + k, h).wait_recv()
                    square(unit)

                pl.when(present(way, s))(take)
    sent = []
    cent_copy.wait()
    cent_wide = cent_ref[...].astype(jnp.float32)
    half_norm = 0.5 * jnp.sum(cent_wide * cent_wide, axis=1, keepdims=True)

    slots = split * max(1, min(shards, 512 // row_count))
    chunk = slots * piece_rows
    chunks = shards * split // slots

    def score(k, carry):
        first = k * slots
        columns = k * chunk
        if not isinstance(k, int):
            columns = pl.multiple_of(columns, chunk)
        block = rows_all[pl.ds(first, slots)].reshape(chunk, width)
        inner = lax.dot_general(
            cent_ref[...], block, contract_width, preferred_element_type=jnp.float32
        )
        logits = factor * (inner - half_norm)
        peak = jnp.max(logits, axis=0, keepdims=True)
        weight = jnp.exp(logits - peak)
        weights[:, pl.ds(columns, chunk)] = weight
        parts[0, 0:1, pl.ds(columns, chunk)] = peak
        parts[0, 1:2, pl.ds(columns, chunk)] = jnp.sum(weight, axis=0, keepdims=True)
        return carry

    for k in range(chunks) if chunks <= 4 else ():
        score(k, 0)
    if chunks > 4:
        lax.fori_loop(0, chunks, score, 0)

    own_peak = parts[0, 0:1, :]

    def joined(part_list):
        highest = part_list[0][0]
        for peak, _ in part_list[1:]:
            highest = jnp.maximum(highest, peak)
        amount = None
        for peak, exp_sum in part_list:
            term = exp_sum * jnp.exp(peak - highest)
            amount = term if amount is None else amount + term
        return highest, amount

    def part(k):
        return parts[k, 0:1, :], parts[k, 1:2, :]

    hop = send(parts.at[0], parts.at[1], p_send.at[0], p_recv.at[0], (g, core_peer))

    hop.wait()
    peak, amount = joined([part(0), part(1)])
    parts[2, 0:1, :] = peak
    parts[2, 1:2, :] = amount
    hops = []
    for k in range(2 * line - 1, 0, -1):
        peer = lax.rem(place + k // 2, line) * 4 + lax.rem(spot + 2 * (k % 2), 4)
        hops.append(send(parts.at[2], parts.at[2 + k], p_send.at[k], p_recv.at[k], (g, peer)))
    for hop in hops:
        hop.wait_recv()
    sent += hops
    peak, amount = joined([part(2 + k) for k in range(2 * line)])
    lse = peak + jnp.log(amount)
    valid = lax.broadcasted_iota(jnp.int32, (1, total), 1) < length_ref[0]
    scale = jnp.where(valid, jnp.exp(own_peak - lse), 0.0)
    resp = (weights[...] * scale).astype(jnp.bfloat16)

    ones = jnp.ones((8, total), jnp.bfloat16)
    masses[g] = lax.dot_general(ones, resp, contract_width, preferred_element_type=jnp.float32)
    s_copies = {}
    for s in range(1, groups):
        sent.append(
            send(masses.at[g], masses.at[g], m_send.at[s], m_recv.at[s], (across(s), i))
        )
    m_copies = sent[len(sent) - (groups - 1):]
    pieces = 2 * (width // column_step)
    for k in range(pieces):
        left = (k // 2) * column_step
        source = rows_all if k % 2 == 0 else squares
        block = source[:, :, left:left + column_step].reshape(total, column_step)
        sums = lax.dot_general(resp, block, contract_rows, preferred_element_type=jnp.float32)
        stats[g, k] = sums.astype(jnp.bfloat16)
        for s in range(1, groups):
            s_copies[k, s] = send(
                stats.at[g, k], stats.at[g, k], s_send.at[k, s], s_recv.at[k, s], (across(s), i)
            )

    own_lik = jnp.where(valid, lse, 0.0)
    pick = own_lik[:, 0:row_count]
    for j in range(1, shards):
        pick = jnp.where(i == j, own_lik[:, j * row_count:(j + 1) * row_count], pick)
    lik_out[...] = pick

    for copy in m_copies:
        copy.wait_recv()
    mass = masses[0, 0:1, :]
    for r in range(1, groups):
        mass = mass + masses[r, 0:1, :]
    inverse = 1.0 / (mass + prior_weight)
    inverse_out[...] = jnp.transpose(jnp.broadcast_to(inverse, (cents, cents)))
    for k in range(pieces):
        for s in range(1, groups):
            s_copies[k, s].wait_recv()
        left = (k // 2) * column_step
        sums = stats[0, k].astype(jnp.float32)
        for r in range(1, groups):
            sums = sums + stats[r, k].astype(jnp.float32)
        if k % 2 == 0:
            sums = sums + prior_weight * cent_ref[:, left:left + column_step].astype(jnp.float32)
            cent_out[:, left:left + column_step] = sums
        else:
            mom_out[:, left:left + column_step] = sums + prior_weight
    for h in range(split):
        unit = i * split + h
        pl.when(has_right)(lambda: z_copy(unit, 0, 1, h).wait_send())
        pl.when(has_left)(lambda: z_copy(unit, 1, 1, h).wait_send())
        y_copy(unit, 0, h).wait_send()
        c_copy(unit, 0, h).wait_send()
        c_copy(unit_of(0, 0, y_spot, h), steps, h).wait_send()
    for k, (way, s) in enumerate(order, 1):
        for h in range(split):
            def finish():
                unit = unit_of(way, s, spot, h)
                onward = has_right if way == 0 else has_left
                if s + 1 < line:
                    pl.when(onward)(lambda: z_copy(unit, way, s + 1, h).wait_send())
                y_copy(unit, k, h).wait_send()
                c_copy(unit, k, h).wait_send()
                c_copy(unit_of(way, s, y_spot, h), steps + k, h).wait_send()

            pl.when(present(way, s))(finish)
    for copy in sent + list(s_copies.values()):
        copy.wait_send()


def gather_kernel(
    shards, split, turn, cross, steps,
    length_ref, emb_hbm, cent_hbm,
    cent_out, mom_out, lik_out, inverse_out,
    cents_all, rows_all, squares, weights, resp, peaks, parts, lse_ref,
    own_sem, cent_sem, ready, know, z_send, z_recv, w_send, w_recv, y_send, y_recv, o_recv,
    x_send, x_recv, d_recv, c_send, c_recv, k_send, k_recv, p_send, p_recv,
):
    g = lax.axis_index("rows")
    i = lax.axis_index("cent")
    row_count, width = emb_hbm.shape
    cents = cents_all.shape[1]
    total = shards * row_count
    piece = row_count // split
    line = shards // 4
    chunk = 4 * row_count
    spread = chunk // lanes
    spot = lax.rem(i, 4)
    place = i // 4
    core = lax.rem(i, 2)
    core_peer = i + 1 - 2 * core
    core_spot = spot + 1 - 2 * core
    y_spot = lax.rem(spot + 2, 4)
    core_y_spot = lax.rem(core_spot + 2, 4)
    y_peer = place * 4 + y_spot
    there = 1 - g
    factor = score_factor / math.sqrt(width)

    def signal(sem, peer):
        pl.semaphore_signal(sem, inc=1, device_id=peer, device_id_type=MESH)

    barrier = pltpu.get_barrier_semaphore()
    has_right = place < line - 1
    has_left = place > 0
    pl.when(has_right)(lambda: signal(barrier, (g, i + 4)))
    pl.when(has_left)(lambda: signal(barrier, (g, i - 4)))
    for peer in [(g, y_peer), (there, i), (g, core_peer)]:
        signal(barrier, peer)
    own = pltpu.make_async_copy(emb_hbm, rows_all.at[g, i], own_sem)
    own.start()
    cent_copy = pltpu.make_async_copy(cent_hbm, cents_all.at[0], cent_sem)
    cent_copy.start()
    own.wait()
    sides = has_right.astype(jnp.int32) + has_left.astype(jnp.int32)
    pl.semaphore_wait(barrier, 3 + sides)

    def move(ref, send_sem, recv_sem, peer):
        return pltpu.make_async_remote_copy(
            src_ref=ref, dst_ref=ref, send_sem=send_sem, recv_sem=recv_sem,
            device_id=peer, device_id_type=MESH,
        )

    def slot(group, q, where, h):
        if h is None:
            return rows_all.at[group, q * 4 + where]
        return rows_all.at[group, q * 4 + where, pl.ds(h * piece, piece)]

    def column(side):
        return spot if side == 0 else y_spot

    def z_own(way, s, h):
        peer = (g, i + 4 * s if way == 0 else i - 4 * s)
        return move(slot(g, place, spot, h), z_send, z_recv.at[place, h], peer)

    def z_move(way, q, h):
        peer = (g, i + 4 if way == 0 else i - 4)
        return move(slot(g, q, spot, h), z_send, z_recv.at[q, h], peer)

    def low(ref, q, where):
        return ref.at[g, q * 4 + where, pl.ds(0, cross)]

    def high(ref, q, where):
        return ref.at[g, q * 4 + where, pl.ds(cross, row_count - cross)]

    def y_move(q, h):
        return move(slot(g, q, spot, h), y_send, y_recv.at[q], (g, y_peer))

    def y_own():
        return move(low(rows_all, place, spot), y_send, y_recv.at[place], (g, y_peer))

    def y_come(q):
        return move(low(rows_all, q, y_spot), y_send, y_recv.at[q], (g, y_peer))

    def o_own():
        return move(high(rows_all, place, spot), w_send, o_recv, (g, y_peer))

    def o_come():
        return move(high(rows_all, place, y_spot), w_send, o_recv, (g, y_peer))

    def w_move(way, q, s):
        peer = (g, i + 4 * s if way == 0 else i - 4 * s)
        return move(high(rows_all, q, y_spot), w_send, w_recv.at[q], peer)

    def cent_move(src, k, sem, peer):
        return pltpu.make_async_remote_copy(
            src_ref=cent_hbm if src is None else cents_all.at[src], dst_ref=cents_all.at[k],
            send_sem=k_send.at[sem], recv_sem=k_recv.at[k - 1], device_id=(g, peer), device_id_type=MESH,
        )

    def cent_come(k):
        return move(cents_all.at[k], k_send.at[0], k_recv.at[k - 1], (g, y_peer))

    def part(group, q, where, side):
        rows = pl.ds(0, turn) if side == 0 else pl.ds(turn, row_count - turn)
        return rows_all.at[group, q * 4 + where, rows]

    def x_move(q, h):
        side = 0 if h * piece < turn else 1
        return move(slot(g, q, spot, h), x_send, x_recv.at[q, side], (there, i))

    def x_own(side):
        return move(part(g, place, spot, side), x_send, x_recv.at[place, side], (there, i))

    def x_come(q, side):
        return move(part(there, q, spot, side), x_send, x_recv.at[q, side], (there, i))

    def c_part(q, side):
        return move(part(there, q, spot, side), c_send, c_recv.at[1, q], (g, core_peer))

    def x_turn(q):
        return move(part(g, q, y_spot, 0), x_send, x_recv.at[q, 2], (there, i))

    def x_turned(q):
        return move(part(there, q, y_spot, 0), x_send, x_recv.at[q, 2], (there, i))

    def y_turn(q):
        return move(part(there, q, spot, 1), y_send, d_recv.at[q], (g, y_peer))

    def y_turned(q):
        return move(part(there, q, y_spot, 1), y_send, d_recv.at[q], (g, y_peer))

    def c_low(q):
        return move(low(rows_all, q, y_spot), c_send, c_recv.at[0, q], (g, core_peer))

    def c_high(q):
        return move(high(rows_all, q, y_spot), c_send, c_recv.at[0, q], (g, core_peer))

    def c_turn(q, side):
        return move(part(there, q, y_spot, side), c_send, c_recv.at[1, q], (g, core_peer))

    def c_move(mine, q, side, h):
        ref = slot(g if mine else there, q, column(side), h)
        return move(ref, c_send, c_recv.at[0 if mine else 1, q], (g, core_peer))

    def c_come(mine, q):
        ref = rows_all.at[g if mine else there, pl.ds(q * 4, 2)]
        return move(ref, c_send, c_recv.at[0 if mine else 1, q], (g, core_peer))

    def source(way, s):
        return place - s if way == 0 else place + s

    def present(way, s):
        return place >= s if way == 0 else place + s < line

    def starts(way):
        return has_right if way == 0 else has_left

    def onward(way, s):
        if way == 0:
            return jnp.logical_and(place > s, has_right)
        return jnp.logical_and(place + s < line - 1, has_left)

    def ends(way):
        return place == 0 if way == 0 else place == line - 1

    def both(fn, cond):
        for way in range(2):
            pl.when(cond(way))(functools.partial(fn, way))

    def z_take(way, s, h):
        def take():
            q = source(way, s)
            z_move(way, q, h).wait_recv()
            if s + 1 < line:
                pl.when(onward(way, s))(lambda: z_move(way, q, h).start())
            if h * piece < cross:
                y_move(q, h).start()
            x_move(q, h).start()
            c_move(True, q, 0, h).start()

        pl.when(present(way, s))(take)

    def at(way, s, fn):
        if s == 0:
            fn(place)
        else:
            pl.when(present(way, s))(lambda: fn(source(way, s)))

    def y_take(q):
        y_come(q).wait_recv()
        x_turn(q).start()
        c_low(q).start()

    def x_take(q, side):
        x_come(q, side).wait_recv()
        if side == 1:
            y_turn(q).start()
        c_part(q, side).start()

    def turn_take(q, side):
        (y_turned if side else x_turned)(q).wait_recv()
        c_turn(q, side).start()

    def w_take(way, s):
        def take():
            q = source(way, s)
            w_move(way, q, 1).wait_recv()
            if s + 1 < line:
                pl.when(onward(way, s))(lambda: w_move(way, q, 1).start())
            c_high(q).start()

        if cross < row_count:
            pl.when(present(way, s))(take)

    def nth(j):
        orders = [sorted(range(line), key=lambda q: abs(q - p)) for p in range(line)]
        q = orders[0][j]
        for p in range(1, line):
            q = jnp.where(place == p, orders[p][j], q)
        return q

    near = [(way, 1) for way in range(2)]
    far = [(way, s) for s in range(2, line) for way in range(2)]
    for h in range(split):
        both(lambda way: z_own(way, 1, h).start(), starts)
    if cross < row_count:
        o_own().start()
    y_own().start()
    cent_move(None, 2, 0, y_peer).start()
    x_own(0).start()
    x_own(1).start()
    cent_move(None, 1, 1, core_peer).start()
    c_move(True, place, 0, None).start()

    cube = [(g, y_peer), (there, i), (g, core_peer)]
    for peer in cube:
        signal(know.at[0], peer)
    if line > 2:
        pl.when(jnp.logical_and(place == 1, has_right))(lambda: signal(ready.at[0], (g, i + 4)))
        pl.when(jnp.logical_and(place == line - 2, has_left))(lambda: signal(ready.at[1], (g, i - 4)))

        def pass_up():
            pl.semaphore_wait(ready.at[0], 1)
            pl.when(has_right)(lambda: signal(ready.at[0], (g, i + 4)))

        def pass_down():
            pl.semaphore_wait(ready.at[1], 1)
            pl.when(has_left)(lambda: signal(ready.at[1], (g, i - 4)))

        pl.when(place >= 2)(pass_up)
        pl.when(place <= line - 3)(pass_down)

        def far_go(way):
            for h in range(split):
                for s in range(2, line):
                    z_own(way, s, h).start()

        both(far_go, ends)

    cent_copy.wait()
    cent_wide = cents_all[0].astype(jnp.float32)
    half_norm = 0.5 * jnp.sum(cent_wide * cent_wide, axis=1, keepdims=True)

    def score(mine, q):
        t = 0 if mine else 1
        c_come(mine, q).wait_recv()
        group = g if mine else there
        block = rows_all[group, pl.ds(q * 4, 4)].reshape(chunk, width)
        inner = lax.dot_general(
            cents_all[0], block, contract_width, preferred_element_type=jnp.float32
        )
        logits = factor * (inner - half_norm)
        peak = jnp.max(logits, axis=0, keepdims=True)
        weights[t, q] = jnp.exp(logits - peak)
        for r in range(spread):
            peaks[t, q, r:r + 1, :] = peak[:, r * lanes:(r + 1) * lanes]
        wide = block.astype(jnp.float32)
        squares[group, pl.ds(q * 4, 4)] = (wide * wide).astype(jnp.bfloat16).reshape(
            4, row_count, width
        )

    def partial_lse(all_half, q):
        block = rows_all[g, q * 4 + spot]
        inner = lax.dot_general(
            cents_all[...].reshape(4 * cents, width), block, contract_width,
            preferred_element_type=jnp.float32,
        )
        logits = factor * (inner - all_half)
        peak = jnp.max(logits, axis=0, keepdims=True)
        value = peak + jnp.log(jnp.sum(jnp.exp(logits - peak), axis=0, keepdims=True))
        row = (q * 4 + spot) * row_count + lax.broadcasted_iota(jnp.int32, value.shape, 1)
        parts[g, i, pl.ds(q, 1), :] = jnp.where(row < length_ref[0], value, masked)

    def joined(values):
        highest = values[0]
        for value in values[1:]:
            highest = jnp.maximum(highest, value)
        amount = jnp.exp(values[0] - highest)
        for value in values[1:]:
            amount = amount + jnp.exp(value - highest)
        return highest + jnp.log(amount)

    def move_parts(group, count, k):
        return move(parts.at[group, pl.ds(0, count)], p_send.at[k], p_recv.at[k], (g, y_peer))

    def whole_lse(group):
        return [joined([parts[group, p * 4 + w] for p in range(line)]) for w in range(4)]

    ones = jnp.ones((8, total), jnp.bfloat16)

    def weigh(t, q, place_in_resp):
        for r in range(spread):
            left = r * lanes
            scale = jnp.exp(peaks[t, q, r:r + 1, :] - lse_ref[t, r, pl.ds(q, 1), :])
            resp[:, place_in_resp * chunk + left:place_in_resp * chunk + left + lanes] = (
                weights[t, q, :, left:left + lanes] * scale
            ).astype(jnp.bfloat16)

    def times(left, right):
        return lax.dot_general(left, right, contract_rows, preferred_element_type=jnp.float32)

    def mass_of(block):
        return lax.dot_general(
            ones[:, :block.shape[1]], block, contract_width, preferred_element_type=jnp.float32
        )

    def keep_lse(t, lse):
        for r in range(spread):
            lse_ref[t, r] = jnp.concatenate([lse[2 * r], lse[2 * r + 1]], axis=1)

    def add_there(orders):
        mass = 0.0
        weighted = cent_out[...]
        moments = mom_out[...]
        for n, q in enumerate(orders):
            weigh(1, q, line + n)
            block = resp[:, total + n * chunk:total + (n + 1) * chunk]
            mass = mass + mass_of(block)
            weighted = weighted + times(block, rows_all[there, pl.ds(q * 4, 4)].reshape(chunk, width))
            moments = moments + times(block, squares[there, pl.ds(q * 4, 4)].reshape(chunk, width))
        cent_out[...] = weighted
        mom_out[...] = moments
        return mass

    places = [place] + [nth(j) for j in range(1, line)]
    state = {"half": None, "mass": None, "lse": None, "told": False, "ready": [], "there": False, "moments": False}

    def near_rows(h):
        for way, s in near:
            z_take(way, s, h)

    def far_rows(h):
        for way, s in far:
            z_take(way, s, h)

    def other_column(_):
        if cross == row_count:
            return
        o_come().wait_recv()
        both(lambda way: w_move(way, place, 1).start(), starts)

        def w_far(way):
            for s in range(2, line):
                w_move(way, place, s).start()

        if line > 2:
            both(w_far, ends)
        c_high(place).start()

    def tell(_):
        pl.semaphore_wait(know.at[0], 3)
        for peer in cube:
            signal(know.at[1], peer)

    def tell_line(_):
        pl.semaphore_wait(know.at[1], 3)
        for q in range(1, line):
            signal(know.at[2], (g, lax.rem(place + q, line) * 4 + spot))

    def cents_out(_):
        cent_move(None, 2, 0, y_peer).start()

    def half_of(k):
        wide = cents_all[k].astype(jnp.float32)
        return 0.5 * jnp.sum(wide * wide, axis=1, keepdims=True)

    def cents_in(_):
        cent_come(2).wait_recv()
        cent_move(2, 3, 2, core_peer).start()
        cent_come(1).wait_recv()
        state["halves"] = [half_norm, half_of(1), half_of(2)]

    def cents_ready(_):
        cent_come(3).wait_recv()
        state["half"] = jnp.concatenate([*state["halves"], half_of(3)], axis=0)

    def normaliser(k):
        if k == 0:
            partial_lse(state["half"], place)
        for way, s in (near, far)[k - 1] if k else ():
            at(way, s, functools.partial(partial_lse, state["half"]))

    def send_parts(_):
        pl.semaphore_wait(know.at[2], line - 1)
        mine_part = parts.at[g, i]
        for k in range(shards - 1, -1, -1):
            peer = lax.rem(i + k, shards)
            for group, t in ((there, 1), (g, 0)):
                if k > 0 or t:
                    pltpu.make_async_remote_copy(
                        src_ref=mine_part, dst_ref=mine_part, send_sem=p_send.at[t],
                        recv_sem=p_recv.at[t], device_id=(group, peer), device_id_type=MESH,
                    ).start()

    def crossed(k):
        for way, s in (near, far)[k]:
            w_take(way, s)

    def own_sums(_):
        move_parts(g, shards - 1, 0).wait_recv()
        lse = whole_lse(g)
        keep_lse(0, lse)
        for q in range(line):
            weigh(0, q, q)
        state["mass"] = mass_of(resp[:, :total])
        cent_out[...] = prior_weight * cent_wide + times(
            resp[:, :total], rows_all[g].reshape(total, width)
        )
        state["lse"] = lse

    def own_moments(_):
        mom_out[...] = prior_weight + times(resp[:, :total], squares[g].reshape(total, width))
        state["moments"] = True

    def score_there(j):
        score(False, places[j])
        state["ready"].append(places[j])

    def sums_there(_):
        if not state["moments"] or not state["ready"]:
            return
        if not state["there"]:
            move_parts(there, shards, 1).wait_recv()
            keep_lse(1, whole_lse(there))
            state["there"] = True
        state["mass"] = state["mass"] + add_there(state["ready"])
        state["ready"] = []

    def write_lik(_):
        lse = state["lse"]
        pick = lse[0]
        for w in range(1, 4):
            pick = jnp.where(spot == w, lse[w], pick)
        own_lik = pick[0:1]
        for q in range(1, line):
            own_lik = jnp.where(place == q, pick[q:q + 1], own_lik)
        row = i * row_count + lax.broadcasted_iota(jnp.int32, own_lik.shape, 1)
        lik_out[...] = jnp.where(row < length_ref[0], own_lik, 0.0)

    acts = {
        "N": near_rows, "Z": far_rows, "O": other_column, "E": tell, "F": tell_line,
        "K": cents_out, "I": cents_in, "C": cents_ready, "A": normaliser, "L": send_parts,
        "W": crossed, "Y": lambda j: y_take(places[j]), "H": lambda j: x_take(places[j], 1),
        "G": lambda j: x_take(places[j], 0), "T": lambda j: turn_take(places[j], 0),
        "D": lambda j: turn_take(places[j], 1), "S": lambda j: score(True, places[j]),
        "s": score_there, "R": own_sums, "M": own_moments, "r": sums_there, "l": write_lik,
    }
    for step in steps:
        acts[step[0]](int(step[1:] or 0))
    mass = state["mass"]
    inverse = 1.0 / (mass[0:1, :] + prior_weight)
    inverse_out[...] = jnp.transpose(jnp.broadcast_to(inverse, (cents, cents)))

    def drain(sem, count):
        step = max(b for b in range(piece, row_count + 1, piece) if count % b == 0)
        rows = rows_all.at[g, pl.ds(0, count // step), pl.ds(0, step)]
        move(rows, sem, own_sem, (g, y_peer)).wait_send()

    drain(z_send, (line - 1) * row_count)
    drain(y_send, line * (cross + row_count - turn))
    drain(x_send, line * (row_count + turn))
    drain(c_send, 4 * line * row_count)
    if cross < row_count:
        drain(w_send, line * (row_count - cross))
    for k in range(3):
        move(cents_all.at[1], k_send.at[k], own_sem, (g, y_peer)).wait_send()
    move_parts(g, shards - 1, 0).wait_send()
    move_parts(there, shards, 1).wait_send()


schedule = (
    "N0", "N1", "Y0", "E", "O", "N2", "S0", "G1", "H0", "N3", "G0", "Z1",
    "Z0", "F", "I", "T0", "Z2", "W0", "H1", "Z3", "Y1", "C", "A0", "A1",
    "A2", "Y2", "L", "H2", "Y3", "G2", "D0", "H3", "W1", "S1", "D1", "s0",
    "T1", "S3", "G3", "S2", "s1", "R", "T2", "D2", "M", "T3", "D3", "r",
    "s2", "l", "s3", "r",
)


def gather_steps(line, split):
    assert line == 4 and split == 4
    return schedule


def gather_call(shards, row_count, width, cents, out_shape):
    line = shards // 4
    split = 4
    cross = row_count * 2 // 4
    turn = row_count * 2 // 4
    total = shards * row_count
    spread = 4 * row_count // lanes
    vmem = pl.BlockSpec(memory_space=pltpu.VMEM)
    hbm = pl.BlockSpec(memory_space=pltpu.HBM)
    dma = pltpu.SemaphoreType.DMA
    regular = pltpu.SemaphoreType.REGULAR
    return pl.pallas_call(
        functools.partial(gather_kernel, shards, split, turn, cross, gather_steps(line, split)),
        out_shape=out_shape,
        in_specs=[pl.BlockSpec(memory_space=pltpu.SMEM), hbm, hbm],
        out_specs=(vmem, vmem, vmem, vmem),
        scratch_shapes=[
            pltpu.VMEM((4, cents, width), jnp.bfloat16),
            pltpu.VMEM((2, shards, row_count, width), jnp.bfloat16),
            pltpu.VMEM((2, shards, row_count, width), jnp.bfloat16),
            pltpu.VMEM((2, line, cents, 4 * row_count), jnp.float32),
            pltpu.VMEM((cents, 2 * total), jnp.bfloat16),
            pltpu.VMEM((2, line, spread, lanes), jnp.float32),
            pltpu.VMEM((2, shards, line, row_count), jnp.float32),
            pltpu.VMEM((2, spread, line, lanes), jnp.float32),
            dma, dma, regular((2,)), regular((3,)),
            dma, dma((line, split)), dma, dma((line,)), dma, dma((line,)), dma,
            dma, dma((line, 3)), dma((line,)), dma, dma((2, line)), dma((3,)), dma((3,)),
            dma((2,)), dma((2,)),
        ],
        compiler_params=pltpu.CompilerParams(
            collective_id=0, has_side_effects=True, vmem_limit_bytes=32 * 1024 * 1024
        ),
        name="soft_em",
    )


def solution(mesh):
    groups = mesh.shape["rows"]
    shards = mesh.shape["cent"]
    line = shards // 4

    def step(embeddings, centroids, group_length):
        row_count, width = embeddings.shape
        cents = centroids.shape[0]
        total = row_count * shards
        column_step = 256 if width % 256 == 0 else width
        pieces = 2 * (width // column_step)
        split = 2 if row_count % 32 == 0 else 1
        vmem = pl.BlockSpec(memory_space=pltpu.VMEM)
        hbm = pl.BlockSpec(memory_space=pltpu.HBM)
        held = 4 * total * width + 4 * cents * total + 2 * (groups * 2 + 1) * cents * width
        steps = 2 * line - 1
        dma = pltpu.SemaphoreType.DMA
        out_shape = (
            jax.ShapeDtypeStruct((cents, width), jnp.float32),
            jax.ShapeDtypeStruct((cents, width), jnp.float32),
            jax.ShapeDtypeStruct((1, row_count), jnp.float32),
            jax.ShapeDtypeStruct((cents, cents), jnp.float32),
        )
        if groups == 2 and shards == 16 and row_count % 64 == 0 and total <= 2048:
            call = gather_call(shards, row_count, width, cents, out_shape)
        else:
            call = pl.pallas_call(
                functools.partial(sums_kernel, groups, shards, column_step, split),
                out_shape=out_shape,
                in_specs=[pl.BlockSpec(memory_space=pltpu.SMEM), hbm, hbm],
                out_specs=(vmem, vmem, vmem, vmem),
                scratch_shapes=[
                    pltpu.VMEM((cents, width), jnp.bfloat16),
                    pltpu.VMEM((shards * split, row_count // split, width), jnp.bfloat16),
                    pltpu.VMEM((shards * split, row_count // split, width), jnp.bfloat16),
                    pltpu.VMEM((cents, total), jnp.float32),
                    pltpu.VMEM((2 + 2 * line, 2, total), jnp.float32),
                    pltpu.VMEM((groups, pieces, cents, column_step), jnp.bfloat16),
                    pltpu.VMEM((groups, 8, cents), jnp.float32),
                    dma((split,)), dma, dma((2, line, split)), dma((2, line, split)),
                    dma((steps, split)), dma((steps, split)),
                    dma((2 * steps, split)), dma((2 * steps, split)),
                    dma((2 * line,)), dma((2 * line,)),
                    dma((pieces, groups)), dma((pieces, groups)),
                    dma((groups,)), dma((groups,)),
                ],
                compiler_params=pltpu.CompilerParams(
                    collective_id=0, has_side_effects=True, vmem_limit_bytes=2 * held + 4 * 1024 * 1024
                ),
                name="soft_em",
            )
        cent_sums, moment_sums, loglik, inverse = call(group_length, pltpu.with_memory_space_constraint(embeddings, pltpu.HBM), pltpu.with_memory_space_constraint(centroids, pltpu.HBM))
        new_centroids = (cent_sums * inverse[:, 0:1]).astype(jnp.bfloat16)
        new_moments = (moment_sums * inverse[:, 0:1]).astype(jnp.bfloat16)
        return new_centroids, new_moments, loglik.reshape(row_count)

    return jax.shard_map(
        step,
        mesh=mesh,
        in_specs=(P(("rows", "cent"), None), P("cent", None), P("rows")),
        out_specs=(P("cent", None), P("cent", None), P(("rows", "cent"))),
        check_vma=False,
    )
```

```python
import functools
import math

import jax
import jax.numpy as jnp
from jax import lax
from jax.experimental import pallas as pl
from jax.experimental.pallas import tpu as pltpu
from jax.sharding import PartitionSpec as P

score_factor = 3.0
prior_weight = 1.0
MESH = pl.DeviceIdType.MESH
contract_width = (((1,), (1,)), ((), ()))
contract_rows = (((1,), (0,)), ((), ()))


lanes = 128
masked = 1e30


def sums_kernel(
    groups, shards, column_step, split,
    length_ref, emb_hbm, cent_hbm,
    cent_out, mom_out, lik_out, inverse_out,
    cent_ref, rows_all, squares, weights, parts, stats, masses,
    own_sem, cent_sem, z_send, z_recv, y_send, y_recv, c_send, c_recv,
    p_send, p_recv, s_send, s_recv, m_send, m_recv,
):
    g = lax.axis_index("rows")
    i = lax.axis_index("cent")
    row_count, width = emb_hbm.shape
    cents = cent_ref.shape[0]
    total = shards * row_count
    piece_rows = row_count // split
    line = shards // 4
    spot = lax.rem(i, 4)
    place = i // 4
    core = lax.rem(i, 2)
    core_peer = i + 1 - 2 * core
    y_spot = lax.rem(spot + 2, 4)
    y_peer = place * 4 + y_spot
    factor = score_factor / math.sqrt(width)

    def across(step):
        return lax.rem(g + step, groups)

    def signal(peer):
        pl.semaphore_signal(barrier, inc=1, device_id=peer, device_id_type=MESH)

    barrier = pltpu.get_barrier_semaphore()
    for peer in [(g, y_peer), (g, core_peer)] + [(across(s), i) for s in range(1, groups)]:
        signal(peer)
    has_right = place < line - 1
    has_left = place > 0
    pl.when(has_right)(lambda: signal((g, i + 4)))
    pl.when(has_left)(lambda: signal((g, i - 4)))
    own = [
        pltpu.make_async_copy(
            emb_hbm.at[pl.ds(h * piece_rows, piece_rows)], rows_all.at[i * split + h], own_sem.at[h]
        )
        for h in range(split)
    ]
    for copy in own:
        copy.start()
    cent_copy = pltpu.make_async_copy(cent_hbm, cent_ref, cent_sem)
    cent_copy.start()
    for copy in own:
        copy.wait()
    sides = has_right.astype(jnp.int32) + has_left.astype(jnp.int32)
    pl.semaphore_wait(barrier, 1 + groups + sides)

    def describe(src, dst, send_sem, recv_sem, peer):
        return pltpu.make_async_remote_copy(
            src_ref=src, dst_ref=dst, send_sem=send_sem, recv_sem=recv_sem,
            device_id=peer, device_id_type=MESH,
        )

    def send(*spec):
        copy = describe(*spec)
        copy.start()
        return copy

    def z_copy(unit, way, s, h):
        slot = rows_all.at[unit]
        peer = (g, i + 4 if way == 0 else i - 4)
        return describe(slot, slot, z_send.at[way, s, h], z_recv.at[way, s, h], peer)

    def y_copy(unit, k, h):
        slot = rows_all.at[unit]
        return describe(slot, slot, y_send.at[k, h], y_recv.at[k, h], (g, y_peer))

    def c_copy(unit, k, h):
        slot = rows_all.at[unit]
        return describe(slot, slot, c_send.at[k, h], c_recv.at[k, h], (g, core_peer))

    def square(unit):
        wide = rows_all[unit].astype(jnp.float32)
        squares[unit] = (wide * wide).astype(jnp.bfloat16)

    steps = 2 * line - 1
    order = [(way, s) for s in range(1, line) for way in range(2)]

    def present(way, s):
        return place >= s if way == 0 else place + s < line

    def unit_of(way, s, where, h):
        source = place - s if way == 0 else place + s
        return (source * 4 + where) * split + h

    for h in range(split):
        unit = i * split + h
        pl.when(has_right)(lambda: z_copy(unit, 0, 1, h).start())
        pl.when(has_left)(lambda: z_copy(unit, 1, 1, h).start())
        y_copy(unit, 0, h).start()
        c_copy(unit, 0, h).start()
    for h in range(split):
        square(i * split + h)
    for k, (way, s) in enumerate(order, 1):
        for h in range(split):
            def relay():
                unit = unit_of(way, s, spot, h)
                z_copy(unit, way, s, h).wait_recv()
                onward = has_right if way == 0 else has_left
                if s + 1 < line:
                    pl.when(onward)(lambda: z_copy(unit, way, s + 1, h).start())
                y_copy(unit, k, h).start()
                c_copy(unit, k, h).start()
                square(unit)

            pl.when(present(way, s))(relay)
    for h in range(split):
        unit = unit_of(0, 0, y_spot, h)
        y_copy(unit, 0, h).wait_recv()
        c_copy(unit, steps, h).start()
        square(unit)
    for k, (way, s) in enumerate(order, 1):
        for h in range(split):
            def pass_on():
                unit = unit_of(way, s, y_spot, h)
                y_copy(unit, k, h).wait_recv()
                c_copy(unit, steps + k, h).start()
                square(unit)

            pl.when(present(way, s))(pass_on)
    other = spot + 1 - 2 * core
    for j, where in enumerate((other, lax.rem(other + 2, 4))):
        for h in range(split):
            unit = unit_of(0, 0, where, h)
            c_copy(unit, j * steps, h).wait_recv()
            square(unit)
        for k, (way, s) in enumerate(order, 1):
            for h in range(split):
                def take():
                    unit = unit_of(way, s, where, h)
                    c_copy(unit, j * steps + k, h).wait_recv()
                    square(unit)

                pl.when(present(way, s))(take)
    sent = []
    cent_copy.wait()
    cent_wide = cent_ref[...].astype(jnp.float32)
    half_norm = 0.5 * jnp.sum(cent_wide * cent_wide, axis=1, keepdims=True)

    slots = split * max(1, min(shards, 512 // row_count))
    chunk = slots * piece_rows
    chunks = shards * split // slots

    def score(k, carry):
        first = k * slots
        columns = k * chunk
        if not isinstance(k, int):
            columns = pl.multiple_of(columns, chunk)
        block = rows_all[pl.ds(first, slots)].reshape(chunk, width)
        inner = lax.dot_general(
            cent_ref[...], block, contract_width, preferred_element_type=jnp.float32
        )
        logits = factor * (inner - half_norm)
        peak = jnp.max(logits, axis=0, keepdims=True)
        weight = jnp.exp(logits - peak)
        weights[:, pl.ds(columns, chunk)] = weight
        parts[0, 0:1, pl.ds(columns, chunk)] = peak
        parts[0, 1:2, pl.ds(columns, chunk)] = jnp.sum(weight, axis=0, keepdims=True)
        return carry

    for k in range(chunks) if chunks <= 4 else ():
        score(k, 0)
    if chunks > 4:
        lax.fori_loop(0, chunks, score, 0)

    own_peak = parts[0, 0:1, :]

    def joined(part_list):
        highest = part_list[0][0]
        for peak, _ in part_list[1:]:
            highest = jnp.maximum(highest, peak)
        amount = None
        for peak, exp_sum in part_list:
            term = exp_sum * jnp.exp(peak - highest)
            amount = term if amount is None else amount + term
        return highest, amount

    def part(k):
        return parts[k, 0:1, :], parts[k, 1:2, :]

    hop = send(parts.at[0], parts.at[1], p_send.at[0], p_recv.at[0], (g, core_peer))

    hop.wait()
    peak, amount = joined([part(0), part(1)])
    parts[2, 0:1, :] = peak
    parts[2, 1:2, :] = amount
    hops = []
    for k in range(2 * line - 1, 0, -1):
        peer = lax.rem(place + k // 2, line) * 4 + lax.rem(spot + 2 * (k % 2), 4)
        hops.append(send(parts.at[2], parts.at[2 + k], p_send.at[k], p_recv.at[k], (g, peer)))
    for hop in hops:
        hop.wait_recv()
    sent += hops
    peak, amount = joined([part(2 + k) for k in range(2 * line)])
    lse = peak + jnp.log(amount)
    valid = lax.broadcasted_iota(jnp.int32, (1, total), 1) < length_ref[0]
    scale = jnp.where(valid, jnp.exp(own_peak - lse), 0.0)
    resp = (weights[...] * scale).astype(jnp.bfloat16)

    ones = jnp.ones((8, total), jnp.bfloat16)
    masses[g] = lax.dot_general(ones, resp, contract_width, preferred_element_type=jnp.float32)
    s_copies = {}
    for s in range(1, groups):
        sent.append(
            send(masses.at[g], masses.at[g], m_send.at[s], m_recv.at[s], (across(s), i))
        )
    m_copies = sent[len(sent) - (groups - 1):]
    pieces = 2 * (width // column_step)
    for k in range(pieces):
        left = (k // 2) * column_step
        source = rows_all if k % 2 == 0 else squares
        block = source[:, :, left:left + column_step].reshape(total, column_step)
        sums = lax.dot_general(resp, block, contract_rows, preferred_element_type=jnp.float32)
        stats[g, k] = sums.astype(jnp.bfloat16)
        for s in range(1, groups):
            s_copies[k, s] = send(
                stats.at[g, k], stats.at[g, k], s_send.at[k, s], s_recv.at[k, s], (across(s), i)
            )

    own_lik = jnp.where(valid, lse, 0.0)
    pick = own_lik[:, 0:row_count]
    for j in range(1, shards):
        pick = jnp.where(i == j, own_lik[:, j * row_count:(j + 1) * row_count], pick)
    lik_out[...] = pick

    for copy in m_copies:
        copy.wait_recv()
    mass = masses[0, 0:1, :]
    for r in range(1, groups):
        mass = mass + masses[r, 0:1, :]
    inverse = 1.0 / (mass + prior_weight)
    inverse_out[...] = jnp.transpose(jnp.broadcast_to(inverse, (cents, cents)))
    for k in range(pieces):
        for s in range(1, groups):
            s_copies[k, s].wait_recv()
        left = (k // 2) * column_step
        sums = stats[0, k].astype(jnp.float32)
        for r in range(1, groups):
            sums = sums + stats[r, k].astype(jnp.float32)
        if k % 2 == 0:
            sums = sums + prior_weight * cent_ref[:, left:left + column_step].astype(jnp.float32)
            cent_out[:, left:left + column_step] = sums
        else:
            mom_out[:, left:left + column_step] = sums + prior_weight
    for h in range(split):
        unit = i * split + h
        pl.when(has_right)(lambda: z_copy(unit, 0, 1, h).wait_send())
        pl.when(has_left)(lambda: z_copy(unit, 1, 1, h).wait_send())
        y_copy(unit, 0, h).wait_send()
        c_copy(unit, 0, h).wait_send()
        c_copy(unit_of(0, 0, y_spot, h), steps, h).wait_send()
    for k, (way, s) in enumerate(order, 1):
        for h in range(split):
            def finish():
                unit = unit_of(way, s, spot, h)
                onward = has_right if way == 0 else has_left
                if s + 1 < line:
                    pl.when(onward)(lambda: z_copy(unit, way, s + 1, h).wait_send())
                y_copy(unit, k, h).wait_send()
                c_copy(unit, k, h).wait_send()
                c_copy(unit_of(way, s, y_spot, h), steps + k, h).wait_send()

            pl.when(present(way, s))(finish)
    for copy in sent + list(s_copies.values()):
        copy.wait_send()


def gather_kernel(
    shards, split, turn, cross, steps,
    length_ref, emb_hbm, cent_hbm,
    cent_out, mom_out, lik_out, inverse_out,
    cents_all, rows_all, squares, weights, resp, peaks, parts, lse_ref,
    own_sem, cent_sem, ready, know, z_send, z_recv, w_send, w_recv, y_send, y_recv, o_recv,
    x_send, x_recv, d_recv, c_send, c_recv, k_send, k_recv, p_send, p_recv,
):
    g = lax.axis_index("rows")
    i = lax.axis_index("cent")
    row_count, width = emb_hbm.shape
    cents = cents_all.shape[1]
    total = shards * row_count
    piece = row_count // split
    line = shards // 4
    chunk = 4 * row_count
    spread = chunk // lanes
    spot = lax.rem(i, 4)
    place = i // 4
    core = lax.rem(i, 2)
    core_peer = i + 1 - 2 * core
    core_spot = spot + 1 - 2 * core
    y_spot = lax.rem(spot + 2, 4)
    core_y_spot = lax.rem(core_spot + 2, 4)
    y_peer = place * 4 + y_spot
    there = 1 - g
    factor = score_factor / math.sqrt(width)

    def signal(sem, peer):
        pl.semaphore_signal(sem, inc=1, device_id=peer, device_id_type=MESH)

    barrier = pltpu.get_barrier_semaphore()
    has_right = place < line - 1
    has_left = place > 0
    pl.when(has_right)(lambda: signal(barrier, (g, i + 4)))
    pl.when(has_left)(lambda: signal(barrier, (g, i - 4)))
    for peer in [(g, y_peer), (there, i), (g, core_peer)]:
        signal(barrier, peer)
    own = pltpu.make_async_copy(emb_hbm, rows_all.at[g, i], own_sem)
    own.start()
    cent_copy = pltpu.make_async_copy(cent_hbm, cents_all.at[0], cent_sem)
    cent_copy.start()
    own.wait()
    sides = has_right.astype(jnp.int32) + has_left.astype(jnp.int32)
    pl.semaphore_wait(barrier, 3 + sides)

    def move(ref, send_sem, recv_sem, peer):
        return pltpu.make_async_remote_copy(
            src_ref=ref, dst_ref=ref, send_sem=send_sem, recv_sem=recv_sem,
            device_id=peer, device_id_type=MESH,
        )

    def slot(group, q, where, h):
        if h is None:
            return rows_all.at[group, q * 4 + where]
        return rows_all.at[group, q * 4 + where, pl.ds(h * piece, piece)]

    def column(side):
        return spot if side == 0 else y_spot

    def z_own(way, s, h):
        peer = (g, i + 4 * s if way == 0 else i - 4 * s)
        return move(slot(g, place, spot, h), z_send, z_recv.at[place, h], peer)

    def z_move(way, q, h):
        peer = (g, i + 4 if way == 0 else i - 4)
        return move(slot(g, q, spot, h), z_send, z_recv.at[q, h], peer)

    def low(ref, q, where):
        return ref.at[g, q * 4 + where, pl.ds(0, cross)]

    def high(ref, q, where):
        return ref.at[g, q * 4 + where, pl.ds(cross, row_count - cross)]

    def y_move(q, h):
        return move(slot(g, q, spot, h), y_send, y_recv.at[q], (g, y_peer))

    def y_own():
        return move(low(rows_all, place, spot), y_send, y_recv.at[place], (g, y_peer))

    def y_come(q):
        return move(low(rows_all, q, y_spot), y_send, y_recv.at[q], (g, y_peer))

    def o_own():
        return move(high(rows_all, place, spot), w_send, o_recv, (g, y_peer))

    def o_come():
        return move(high(rows_all, place, y_spot), w_send, o_recv, (g, y_peer))

    def w_move(way, q, s):
        peer = (g, i + 4 * s if way == 0 else i - 4 * s)
        return move(high(rows_all, q, y_spot), w_send, w_recv.at[q], peer)

    def cent_move(src, k, sem, peer):
        return pltpu.make_async_remote_copy(
            src_ref=cent_hbm if src is None else cents_all.at[src], dst_ref=cents_all.at[k],
            send_sem=k_send.at[sem], recv_sem=k_recv.at[k - 1], device_id=(g, peer), device_id_type=MESH,
        )

    def cent_come(k):
        return move(cents_all.at[k], k_send.at[0], k_recv.at[k - 1], (g, y_peer))

    def part(group, q, where, side):
        rows = pl.ds(0, turn) if side == 0 else pl.ds(turn, row_count - turn)
        return rows_all.at[group, q * 4 + where, rows]

    def x_move(q, h):
        side = 0 if h * piece < turn else 1
        return move(slot(g, q, spot, h), x_send, x_recv.at[q, side], (there, i))

    def x_own(side):
        return move(part(g, place, spot, side), x_send, x_recv.at[place, side], (there, i))

    def x_come(q, side):
        return move(part(there, q, spot, side), x_send, x_recv.at[q, side], (there, i))

    def c_part(q, side):
        return move(part(there, q, spot, side), c_send, c_recv.at[1, q], (g, core_peer))

    def x_turn(q):
        return move(part(g, q, y_spot, 0), x_send, x_recv.at[q, 2], (there, i))

    def x_turned(q):
        return move(part(there, q, y_spot, 0), x_send, x_recv.at[q, 2], (there, i))

    def y_turn(q):
        return move(part(there, q, spot, 1), y_send, d_recv.at[q], (g, y_peer))

    def y_turned(q):
        return move(part(there, q, y_spot, 1), y_send, d_recv.at[q], (g, y_peer))

    def c_low(q):
        return move(low(rows_all, q, y_spot), c_send, c_recv.at[0, q], (g, core_peer))

    def c_high(q):
        return move(high(rows_all, q, y_spot), c_send, c_recv.at[0, q], (g, core_peer))

    def c_turn(q, side):
        return move(part(there, q, y_spot, side), c_send, c_recv.at[1, q], (g, core_peer))

    def c_move(mine, q, side, h):
        ref = slot(g if mine else there, q, column(side), h)
        return move(ref, c_send, c_recv.at[0 if mine else 1, q], (g, core_peer))

    def c_come(mine, q):
        ref = rows_all.at[g if mine else there, pl.ds(q * 4, 2)]
        return move(ref, c_send, c_recv.at[0 if mine else 1, q], (g, core_peer))

    def source(way, s):
        return place - s if way == 0 else place + s

    def present(way, s):
        return place >= s if way == 0 else place + s < line

    def starts(way):
        return has_right if way == 0 else has_left

    def onward(way, s):
        if way == 0:
            return jnp.logical_and(place > s, has_right)
        return jnp.logical_and(place + s < line - 1, has_left)

    def ends(way):
        return place == 0 if way == 0 else place == line - 1

    def both(fn, cond):
        for way in range(2):
            pl.when(cond(way))(functools.partial(fn, way))

    def z_take(way, s, h):
        def take():
            q = source(way, s)
            z_move(way, q, h).wait_recv()
            if s + 1 < line:
                pl.when(onward(way, s))(lambda: z_move(way, q, h).start())
            if h * piece < cross:
                y_move(q, h).start()
            x_move(q, h).start()
            c_move(True, q, 0, h).start()

        pl.when(present(way, s))(take)

    def at(way, s, fn):
        if s == 0:
            fn(place)
        else:
            pl.when(present(way, s))(lambda: fn(source(way, s)))

    def y_take(q):
        y_come(q).wait_recv()
        x_turn(q).start()
        c_low(q).start()

    def x_take(q, side):
        x_come(q, side).wait_recv()
        if side == 1:
            y_turn(q).start()
        c_part(q, side).start()

    def turn_take(q, side):
        (y_turned if side else x_turned)(q).wait_recv()
        c_turn(q, side).start()

    def w_take(way, s):
        def take():
            q = source(way, s)
            w_move(way, q, 1).wait_recv()
            if s + 1 < line:
                pl.when(onward(way, s))(lambda: w_move(way, q, 1).start())
            c_high(q).start()

        if cross < row_count:
            pl.when(present(way, s))(take)

    def nth(j):
        orders = [sorted(range(line), key=lambda q: abs(q - p)) for p in range(line)]
        q = orders[0][j]
        for p in range(1, line):
            q = jnp.where(place == p, orders[p][j], q)
        return q

    near = [(way, 1) for way in range(2)]
    far = [(way, s) for s in range(2, line) for way in range(2)]
    for h in range(split):
        both(lambda way: z_own(way, 1, h).start(), starts)
    if cross < row_count:
        o_own().start()
    y_own().start()
    cent_move(None, 2, 0, y_peer).start()
    x_own(0).start()
    x_own(1).start()
    cent_move(None, 1, 1, core_peer).start()
    c_move(True, place, 0, None).start()

    cube = [(g, y_peer), (there, i), (g, core_peer)]
    for peer in cube:
        signal(know.at[0], peer)
    if line > 2:
        pl.when(jnp.logical_and(place == 1, has_right))(lambda: signal(ready.at[0], (g, i + 4)))
        pl.when(jnp.logical_and(place == line - 2, has_left))(lambda: signal(ready.at[1], (g, i - 4)))

        def pass_up():
            pl.semaphore_wait(ready.at[0], 1)
            pl.when(has_right)(lambda: signal(ready.at[0], (g, i + 4)))

        def pass_down():
            pl.semaphore_wait(ready.at[1], 1)
            pl.when(has_left)(lambda: signal(ready.at[1], (g, i - 4)))

        pl.when(place >= 2)(pass_up)
        pl.when(place <= line - 3)(pass_down)

        def far_go(way):
            for h in range(split):
                for s in range(2, line):
                    z_own(way, s, h).start()

        both(far_go, ends)

    cent_copy.wait()
    cent_wide = cents_all[0].astype(jnp.float32)
    half_norm = 0.5 * jnp.sum(cent_wide * cent_wide, axis=1, keepdims=True)

    def score(mine, q):
        t = 0 if mine else 1
        c_come(mine, q).wait_recv()
        group = g if mine else there
        block = rows_all[group, pl.ds(q * 4, 4)].reshape(chunk, width)
        inner = lax.dot_general(
            cents_all[0], block, contract_width, preferred_element_type=jnp.float32
        )
        logits = factor * (inner - half_norm)
        peak = jnp.max(logits, axis=0, keepdims=True)
        weights[t, q] = jnp.exp(logits - peak)
        for r in range(spread):
            peaks[t, q, r:r + 1, :] = peak[:, r * lanes:(r + 1) * lanes]
        wide = block.astype(jnp.float32)
        squares[group, pl.ds(q * 4, 4)] = (wide * wide).astype(jnp.bfloat16).reshape(
            4, row_count, width
        )

    def partial_lse(all_half, q):
        block = rows_all[g, q * 4 + spot]
        inner = lax.dot_general(
            cents_all[...].reshape(4 * cents, width), block, contract_width,
            preferred_element_type=jnp.float32,
        )
        logits = factor * (inner - all_half)
        peak = jnp.max(logits, axis=0, keepdims=True)
        value = peak + jnp.log(jnp.sum(jnp.exp(logits - peak), axis=0, keepdims=True))
        row = (q * 4 + spot) * row_count + lax.broadcasted_iota(jnp.int32, value.shape, 1)
        parts[g, i, pl.ds(q, 1), :] = jnp.where(row < length_ref[0], value, masked)

    def joined(values):
        highest = values[0]
        for value in values[1:]:
            highest = jnp.maximum(highest, value)
        amount = jnp.exp(values[0] - highest)
        for value in values[1:]:
            amount = amount + jnp.exp(value - highest)
        return highest + jnp.log(amount)

    def move_parts(group, count, k):
        return move(parts.at[group, pl.ds(0, count)], p_send.at[k], p_recv.at[k], (g, y_peer))

    def whole_lse(group):
        return [joined([parts[group, p * 4 + w] for p in range(line)]) for w in range(4)]

    ones = jnp.ones((8, total), jnp.bfloat16)

    def weigh(t, q, place_in_resp):
        for r in range(spread):
            left = r * lanes
            scale = jnp.exp(peaks[t, q, r:r + 1, :] - lse_ref[t, r, pl.ds(q, 1), :])
            resp[:, place_in_resp * chunk + left:place_in_resp * chunk + left + lanes] = (
                weights[t, q, :, left:left + lanes] * scale
            ).astype(jnp.bfloat16)

    def times(left, right):
        return lax.dot_general(left, right, contract_rows, preferred_element_type=jnp.float32)

    def mass_of(block):
        return lax.dot_general(
            ones[:, :block.shape[1]], block, contract_width, preferred_element_type=jnp.float32
        )

    def keep_lse(t, lse):
        for r in range(spread):
            lse_ref[t, r] = jnp.concatenate([lse[2 * r], lse[2 * r + 1]], axis=1)

    def add_there(orders):
        mass = 0.0
        weighted = cent_out[...]
        moments = mom_out[...]
        for n, (q, weighed) in enumerate(orders):
            if not weighed:
                weigh(1, q, line + n)
            block = resp[:, total + n * chunk:total + (n + 1) * chunk]
            mass = mass + mass_of(block)
            weighted = weighted + times(block, rows_all[there, pl.ds(q * 4, 4)].reshape(chunk, width))
            moments = moments + times(block, squares[there, pl.ds(q * 4, 4)].reshape(chunk, width))
        cent_out[...] = weighted
        mom_out[...] = moments
        return mass

    places = [place] + [nth(j) for j in range(1, line)]
    state = {"half": None, "mass": None, "lse": None, "told": False, "ready": [], "there": False, "moments": False}

    def near_rows(h):
        for way, s in near:
            z_take(way, s, h)

    def far_rows(h):
        for way, s in far:
            z_take(way, s, h)

    def other_column(_):
        if cross == row_count:
            return
        o_come().wait_recv()
        both(lambda way: w_move(way, place, 1).start(), starts)

        def w_far(way):
            for s in range(2, line):
                w_move(way, place, s).start()

        if line > 2:
            both(w_far, ends)
        c_high(place).start()

    def tell(_):
        pl.semaphore_wait(know.at[0], 3)
        for peer in cube:
            signal(know.at[1], peer)

    def tell_line(_):
        pl.semaphore_wait(know.at[1], 3)
        for q in range(1, line):
            signal(know.at[2], (g, lax.rem(place + q, line) * 4 + spot))

    def cents_out(_):
        cent_move(None, 2, 0, y_peer).start()

    def half_of(k):
        wide = cents_all[k].astype(jnp.float32)
        return 0.5 * jnp.sum(wide * wide, axis=1, keepdims=True)

    def cents_in(_):
        cent_come(2).wait_recv()
        cent_move(2, 3, 2, core_peer).start()
        cent_come(1).wait_recv()
        state["halves"] = [half_norm, half_of(1), half_of(2)]

    def cents_ready(_):
        cent_come(3).wait_recv()
        state["half"] = jnp.concatenate([*state["halves"], half_of(3)], axis=0)

    def normaliser(k):
        if k == 0:
            partial_lse(state["half"], place)
        for way, s in (near, far)[k - 1] if k else ():
            at(way, s, functools.partial(partial_lse, state["half"]))

    def send_parts(_):
        pl.semaphore_wait(know.at[2], line - 1)
        mine_part = parts.at[g, i]
        for k in range(shards - 1, -1, -1):
            peer = lax.rem(i + k, shards)
            for group, t in ((there, 1), (g, 0)):
                if k > 0 or t:
                    pltpu.make_async_remote_copy(
                        src_ref=mine_part, dst_ref=mine_part, send_sem=p_send.at[t],
                        recv_sem=p_recv.at[t], device_id=(group, peer), device_id_type=MESH,
                    ).start()

    def crossed(k):
        for way, s in (near, far)[k]:
            w_take(way, s)

    def own_sums(_):
        move_parts(g, shards - 1, 0).wait_recv()
        lse = whole_lse(g)
        keep_lse(0, lse)
        for q in range(line):
            weigh(0, q, q)
        state["mass"] = mass_of(resp[:, :total])
        cent_out[...] = prior_weight * cent_wide + times(
            resp[:, :total], rows_all[g].reshape(total, width)
        )
        state["lse"] = lse

    def own_moments(_):
        mom_out[...] = prior_weight + times(resp[:, :total], squares[g].reshape(total, width))
        state["moments"] = True

    def score_there(j):
        score(False, places[j])
        state["ready"].append((places[j], False))

    def lse_from_there():
        if not state["there"]:
            move_parts(there, shards, 1).wait_recv()
            keep_lse(1, whole_lse(there))
            state["there"] = True

    def weigh_there(j):
        lse_from_there()
        q = places[j]
        c_come(False, q).wait_recv()
        block = rows_all[there, pl.ds(q * 4, 4)].reshape(chunk, width)
        inner = lax.dot_general(
            cents_all[0], block, contract_width, preferred_element_type=jnp.float32
        )
        first = total + len(state["ready"]) * chunk
        for r in range(spread):
            left = r * lanes
            logits = factor * (inner[:, left:left + lanes] - half_norm)
            resp[:, first + left:first + left + lanes] = jnp.exp(
                logits - lse_ref[1, r, pl.ds(q, 1), :]
            ).astype(jnp.bfloat16)
        wide = block.astype(jnp.float32)
        squares[there, pl.ds(q * 4, 4)] = (wide * wide).astype(jnp.bfloat16).reshape(
            4, row_count, width
        )
        state["ready"].append((q, True))

    def sums_there(_):
        if not state["moments"] or not state["ready"]:
            return
        lse_from_there()
        state["mass"] = state["mass"] + add_there(state["ready"])
        state["ready"] = []

    def write_lik(_):
        lse = state["lse"]
        pick = lse[0]
        for w in range(1, 4):
            pick = jnp.where(spot == w, lse[w], pick)
        own_lik = pick[0:1]
        for q in range(1, line):
            own_lik = jnp.where(place == q, pick[q:q + 1], own_lik)
        row = i * row_count + lax.broadcasted_iota(jnp.int32, own_lik.shape, 1)
        lik_out[...] = jnp.where(row < length_ref[0], own_lik, 0.0)

    acts = {
        "N": near_rows, "Z": far_rows, "O": other_column, "E": tell, "F": tell_line,
        "K": cents_out, "I": cents_in, "C": cents_ready, "A": normaliser, "L": send_parts,
        "W": crossed, "Y": lambda j: y_take(places[j]), "H": lambda j: x_take(places[j], 1),
        "G": lambda j: x_take(places[j], 0), "T": lambda j: turn_take(places[j], 0),
        "D": lambda j: turn_take(places[j], 1), "S": lambda j: score(True, places[j]),
        "s": score_there, "f": weigh_there, "R": own_sums, "M": own_moments, "r": sums_there, "l": write_lik,
    }
    for step in steps:
        acts[step[0]](int(step[1:] or 0))
    mass = state["mass"]
    inverse = 1.0 / (mass[0:1, :] + prior_weight)
    inverse_out[...] = jnp.transpose(jnp.broadcast_to(inverse, (cents, cents)))

    def drain(sem, count):
        step = max(b for b in range(piece, row_count + 1, piece) if count % b == 0)
        rows = rows_all.at[g, pl.ds(0, count // step), pl.ds(0, step)]
        move(rows, sem, own_sem, (g, y_peer)).wait_send()

    drain(z_send, (line - 1) * row_count)
    drain(y_send, line * (cross + row_count - turn))
    drain(x_send, line * (row_count + turn))
    drain(c_send, 4 * line * row_count)
    if cross < row_count:
        drain(w_send, line * (row_count - cross))
    for k in range(3):
        move(cents_all.at[1], k_send.at[k], own_sem, (g, y_peer)).wait_send()
    move_parts(g, shards - 1, 0).wait_send()
    move_parts(there, shards, 1).wait_send()


schedule = (
    "N0", "N1", "Y0", "E", "O", "N2", "S0", "G1", "H0", "N3", "G0", "Z1",
    "Z0", "F", "I", "T0", "Z2", "W0", "H1", "Z3", "Y1", "C", "A0", "A1",
    "A2", "Y2", "L", "H2", "Y3", "G2", "D0", "H3", "W1", "S1", "D1", "s0",
    "T1", "S3", "G3", "S2", "s1", "T2", "D2", "R", "T3", "M", "D3", "r",
    "f2", "l", "f3", "r",
)


def gather_steps(line, split):
    assert line == 4 and split == 4
    return schedule


def gather_call(shards, row_count, width, cents, out_shape):
    line = shards // 4
    split = 4
    cross = row_count * 2 // 4
    turn = row_count * 2 // 4
    total = shards * row_count
    spread = 4 * row_count // lanes
    vmem = pl.BlockSpec(memory_space=pltpu.VMEM)
    hbm = pl.BlockSpec(memory_space=pltpu.HBM)
    dma = pltpu.SemaphoreType.DMA
    regular = pltpu.SemaphoreType.REGULAR
    return pl.pallas_call(
        functools.partial(gather_kernel, shards, split, turn, cross, gather_steps(line, split)),
        out_shape=out_shape,
        in_specs=[pl.BlockSpec(memory_space=pltpu.SMEM), hbm, hbm],
        out_specs=(vmem, vmem, vmem, vmem),
        scratch_shapes=[
            pltpu.VMEM((4, cents, width), jnp.bfloat16),
            pltpu.VMEM((2, shards, row_count, width), jnp.bfloat16),
            pltpu.VMEM((2, shards, row_count, width), jnp.bfloat16),
            pltpu.VMEM((2, line, cents, 4 * row_count), jnp.float32),
            pltpu.VMEM((cents, 2 * total), jnp.bfloat16),
            pltpu.VMEM((2, line, spread, lanes), jnp.float32),
            pltpu.VMEM((2, shards, line, row_count), jnp.float32),
            pltpu.VMEM((2, spread, line, lanes), jnp.float32),
            dma, dma, regular((2,)), regular((3,)),
            dma, dma((line, split)), dma, dma((line,)), dma, dma((line,)), dma,
            dma, dma((line, 3)), dma((line,)), dma, dma((2, line)), dma((3,)), dma((3,)),
            dma((2,)), dma((2,)),
        ],
        compiler_params=pltpu.CompilerParams(
            collective_id=0, has_side_effects=True, vmem_limit_bytes=32 * 1024 * 1024
        ),
        name="soft_em",
    )


def solution(mesh):
    groups = mesh.shape["rows"]
    shards = mesh.shape["cent"]
    line = shards // 4

    def step(embeddings, centroids, group_length):
        row_count, width = embeddings.shape
        cents = centroids.shape[0]
        total = row_count * shards
        column_step = 256 if width % 256 == 0 else width
        pieces = 2 * (width // column_step)
        split = 2 if row_count % 32 == 0 else 1
        vmem = pl.BlockSpec(memory_space=pltpu.VMEM)
        hbm = pl.BlockSpec(memory_space=pltpu.HBM)
        held = 4 * total * width + 4 * cents * total + 2 * (groups * 2 + 1) * cents * width
        steps = 2 * line - 1
        dma = pltpu.SemaphoreType.DMA
        out_shape = (
            jax.ShapeDtypeStruct((cents, width), jnp.float32),
            jax.ShapeDtypeStruct((cents, width), jnp.float32),
            jax.ShapeDtypeStruct((1, row_count), jnp.float32),
            jax.ShapeDtypeStruct((cents, cents), jnp.float32),
        )
        if groups == 2 and shards == 16 and row_count % 64 == 0 and total <= 2048:
            call = gather_call(shards, row_count, width, cents, out_shape)
        else:
            call = pl.pallas_call(
                functools.partial(sums_kernel, groups, shards, column_step, split),
                out_shape=out_shape,
                in_specs=[pl.BlockSpec(memory_space=pltpu.SMEM), hbm, hbm],
                out_specs=(vmem, vmem, vmem, vmem),
                scratch_shapes=[
                    pltpu.VMEM((cents, width), jnp.bfloat16),
                    pltpu.VMEM((shards * split, row_count // split, width), jnp.bfloat16),
                    pltpu.VMEM((shards * split, row_count // split, width), jnp.bfloat16),
                    pltpu.VMEM((cents, total), jnp.float32),
                    pltpu.VMEM((2 + 2 * line, 2, total), jnp.float32),
                    pltpu.VMEM((groups, pieces, cents, column_step), jnp.bfloat16),
                    pltpu.VMEM((groups, 8, cents), jnp.float32),
                    dma((split,)), dma, dma((2, line, split)), dma((2, line, split)),
                    dma((steps, split)), dma((steps, split)),
                    dma((2 * steps, split)), dma((2 * steps, split)),
                    dma((2 * line,)), dma((2 * line,)),
                    dma((pieces, groups)), dma((pieces, groups)),
                    dma((groups,)), dma((groups,)),
                ],
                compiler_params=pltpu.CompilerParams(
                    collective_id=0, has_side_effects=True, vmem_limit_bytes=2 * held + 4 * 1024 * 1024
                ),
                name="soft_em",
            )
        cent_sums, moment_sums, loglik, inverse = call(group_length, pltpu.with_memory_space_constraint(embeddings, pltpu.HBM), pltpu.with_memory_space_constraint(centroids, pltpu.HBM))
        new_centroids = (cent_sums * inverse[:, 0:1]).astype(jnp.bfloat16)
        new_moments = (moment_sums * inverse[:, 0:1]).astype(jnp.bfloat16)
        return new_centroids, new_moments, loglik.reshape(row_count)

    return jax.shard_map(
        step,
        mesh=mesh,
        in_specs=(P(("rows", "cent"), None), P("cent", None), P("rows")),
        out_specs=(P("cent", None), P("cent", None), P(("rows", "cent"))),
        check_vma=False,
    )
```

```python
import functools
import math

import jax
import jax.numpy as jnp
from jax import lax
from jax.experimental import pallas as pl
from jax.experimental.pallas import tpu as pltpu
from jax.sharding import PartitionSpec as P

score_factor = 3.0
prior_weight = 1.0
MESH = pl.DeviceIdType.MESH
contract_width = (((1,), (1,)), ((), ()))
contract_rows = (((1,), (0,)), ((), ()))


lanes = 128
masked = 1e30


def sums_kernel(
    groups, shards, column_step, split,
    length_ref, emb_hbm, cent_hbm,
    cent_out, mom_out, lik_out, inverse_out,
    cent_ref, rows_all, squares, weights, parts, stats, masses,
    own_sem, cent_sem, z_send, z_recv, y_send, y_recv, c_send, c_recv,
    p_send, p_recv, s_send, s_recv, m_send, m_recv,
):
    g = lax.axis_index("rows")
    i = lax.axis_index("cent")
    row_count, width = emb_hbm.shape
    cents = cent_ref.shape[0]
    total = shards * row_count
    piece_rows = row_count // split
    line = shards // 4
    spot = lax.rem(i, 4)
    place = i // 4
    core = lax.rem(i, 2)
    core_peer = i + 1 - 2 * core
    y_spot = lax.rem(spot + 2, 4)
    y_peer = place * 4 + y_spot
    factor = score_factor / math.sqrt(width)

    def across(step):
        return lax.rem(g + step, groups)

    def signal(peer):
        pl.semaphore_signal(barrier, inc=1, device_id=peer, device_id_type=MESH)

    barrier = pltpu.get_barrier_semaphore()
    for peer in [(g, y_peer), (g, core_peer)] + [(across(s), i) for s in range(1, groups)]:
        signal(peer)
    has_right = place < line - 1
    has_left = place > 0
    pl.when(has_right)(lambda: signal((g, i + 4)))
    pl.when(has_left)(lambda: signal((g, i - 4)))
    own = [
        pltpu.make_async_copy(
            emb_hbm.at[pl.ds(h * piece_rows, piece_rows)], rows_all.at[i * split + h], own_sem.at[h]
        )
        for h in range(split)
    ]
    for copy in own:
        copy.start()
    cent_copy = pltpu.make_async_copy(cent_hbm, cent_ref, cent_sem)
    cent_copy.start()
    for copy in own:
        copy.wait()
    sides = has_right.astype(jnp.int32) + has_left.astype(jnp.int32)
    pl.semaphore_wait(barrier, 1 + groups + sides)

    def describe(src, dst, send_sem, recv_sem, peer):
        return pltpu.make_async_remote_copy(
            src_ref=src, dst_ref=dst, send_sem=send_sem, recv_sem=recv_sem,
            device_id=peer, device_id_type=MESH,
        )

    def send(*spec):
        copy = describe(*spec)
        copy.start()
        return copy

    def z_copy(unit, way, s, h):
        slot = rows_all.at[unit]
        peer = (g, i + 4 if way == 0 else i - 4)
        return describe(slot, slot, z_send.at[way, s, h], z_recv.at[way, s, h], peer)

    def y_copy(unit, k, h):
        slot = rows_all.at[unit]
        return describe(slot, slot, y_send.at[k, h], y_recv.at[k, h], (g, y_peer))

    def c_copy(unit, k, h):
        slot = rows_all.at[unit]
        return describe(slot, slot, c_send.at[k, h], c_recv.at[k, h], (g, core_peer))

    def square(unit):
        wide = rows_all[unit].astype(jnp.float32)
        squares[unit] = (wide * wide).astype(jnp.bfloat16)

    steps = 2 * line - 1
    order = [(way, s) for s in range(1, line) for way in range(2)]

    def present(way, s):
        return place >= s if way == 0 else place + s < line

    def unit_of(way, s, where, h):
        source = place - s if way == 0 else place + s
        return (source * 4 + where) * split + h

    for h in range(split):
        unit = i * split + h
        pl.when(has_right)(lambda: z_copy(unit, 0, 1, h).start())
        pl.when(has_left)(lambda: z_copy(unit, 1, 1, h).start())
        y_copy(unit, 0, h).start()
        c_copy(unit, 0, h).start()
    for h in range(split):
        square(i * split + h)
    for k, (way, s) in enumerate(order, 1):
        for h in range(split):
            def relay():
                unit = unit_of(way, s, spot, h)
                z_copy(unit, way, s, h).wait_recv()
                onward = has_right if way == 0 else has_left
                if s + 1 < line:
                    pl.when(onward)(lambda: z_copy(unit, way, s + 1, h).start())
                y_copy(unit, k, h).start()
                c_copy(unit, k, h).start()
                square(unit)

            pl.when(present(way, s))(relay)
    for h in range(split):
        unit = unit_of(0, 0, y_spot, h)
        y_copy(unit, 0, h).wait_recv()
        c_copy(unit, steps, h).start()
        square(unit)
    for k, (way, s) in enumerate(order, 1):
        for h in range(split):
            def pass_on():
                unit = unit_of(way, s, y_spot, h)
                y_copy(unit, k, h).wait_recv()
                c_copy(unit, steps + k, h).start()
                square(unit)

            pl.when(present(way, s))(pass_on)
    other = spot + 1 - 2 * core
    for j, where in enumerate((other, lax.rem(other + 2, 4))):
        for h in range(split):
            unit = unit_of(0, 0, where, h)
            c_copy(unit, j * steps, h).wait_recv()
            square(unit)
        for k, (way, s) in enumerate(order, 1):
            for h in range(split):
                def take():
                    unit = unit_of(way, s, where, h)
                    c_copy(unit, j * steps + k, h).wait_recv()
                    square(unit)

                pl.when(present(way, s))(take)
    sent = []
    cent_copy.wait()
    cent_wide = cent_ref[...].astype(jnp.float32)
    half_norm = 0.5 * jnp.sum(cent_wide * cent_wide, axis=1, keepdims=True)

    slots = split * max(1, min(shards, 512 // row_count))
    chunk = slots * piece_rows
    chunks = shards * split // slots

    def score(k, carry):
        first = k * slots
        columns = k * chunk
        if not isinstance(k, int):
            columns = pl.multiple_of(columns, chunk)
        block = rows_all[pl.ds(first, slots)].reshape(chunk, width)
        inner = lax.dot_general(
            cent_ref[...], block, contract_width, preferred_element_type=jnp.float32
        )
        logits = factor * (inner - half_norm)
        peak = jnp.max(logits, axis=0, keepdims=True)
        weight = jnp.exp(logits - peak)
        weights[:, pl.ds(columns, chunk)] = weight
        parts[0, 0:1, pl.ds(columns, chunk)] = peak
        parts[0, 1:2, pl.ds(columns, chunk)] = jnp.sum(weight, axis=0, keepdims=True)
        return carry

    for k in range(chunks) if chunks <= 4 else ():
        score(k, 0)
    if chunks > 4:
        lax.fori_loop(0, chunks, score, 0)

    own_peak = parts[0, 0:1, :]

    def joined(part_list):
        highest = part_list[0][0]
        for peak, _ in part_list[1:]:
            highest = jnp.maximum(highest, peak)
        amount = None
        for peak, exp_sum in part_list:
            term = exp_sum * jnp.exp(peak - highest)
            amount = term if amount is None else amount + term
        return highest, amount

    def part(k):
        return parts[k, 0:1, :], parts[k, 1:2, :]

    hop = send(parts.at[0], parts.at[1], p_send.at[0], p_recv.at[0], (g, core_peer))

    hop.wait()
    peak, amount = joined([part(0), part(1)])
    parts[2, 0:1, :] = peak
    parts[2, 1:2, :] = amount
    hops = []
    for k in range(2 * line - 1, 0, -1):
        peer = lax.rem(place + k // 2, line) * 4 + lax.rem(spot + 2 * (k % 2), 4)
        hops.append(send(parts.at[2], parts.at[2 + k], p_send.at[k], p_recv.at[k], (g, peer)))
    for hop in hops:
        hop.wait_recv()
    sent += hops
    peak, amount = joined([part(2 + k) for k in range(2 * line)])
    lse = peak + jnp.log(amount)
    valid = lax.broadcasted_iota(jnp.int32, (1, total), 1) < length_ref[0]
    scale = jnp.where(valid, jnp.exp(own_peak - lse), 0.0)
    resp = (weights[...] * scale).astype(jnp.bfloat16)

    ones = jnp.ones((8, total), jnp.bfloat16)
    masses[g] = lax.dot_general(ones, resp, contract_width, preferred_element_type=jnp.float32)
    s_copies = {}
    for s in range(1, groups):
        sent.append(
            send(masses.at[g], masses.at[g], m_send.at[s], m_recv.at[s], (across(s), i))
        )
    m_copies = sent[len(sent) - (groups - 1):]
    pieces = 2 * (width // column_step)
    for k in range(pieces):
        left = (k // 2) * column_step
        source = rows_all if k % 2 == 0 else squares
        block = source[:, :, left:left + column_step].reshape(total, column_step)
        sums = lax.dot_general(resp, block, contract_rows, preferred_element_type=jnp.float32)
        stats[g, k] = sums.astype(jnp.bfloat16)
        for s in range(1, groups):
            s_copies[k, s] = send(
                stats.at[g, k], stats.at[g, k], s_send.at[k, s], s_recv.at[k, s], (across(s), i)
            )

    own_lik = jnp.where(valid, lse, 0.0)
    pick = own_lik[:, 0:row_count]
    for j in range(1, shards):
        pick = jnp.where(i == j, own_lik[:, j * row_count:(j + 1) * row_count], pick)
    lik_out[...] = pick

    for copy in m_copies:
        copy.wait_recv()
    mass = masses[0, 0:1, :]
    for r in range(1, groups):
        mass = mass + masses[r, 0:1, :]
    inverse = 1.0 / (mass + prior_weight)
    inverse_out[...] = jnp.transpose(jnp.broadcast_to(inverse, (cents, cents)))
    for k in range(pieces):
        for s in range(1, groups):
            s_copies[k, s].wait_recv()
        left = (k // 2) * column_step
        sums = stats[0, k].astype(jnp.float32)
        for r in range(1, groups):
            sums = sums + stats[r, k].astype(jnp.float32)
        if k % 2 == 0:
            sums = sums + prior_weight * cent_ref[:, left:left + column_step].astype(jnp.float32)
            cent_out[:, left:left + column_step] = sums
        else:
            mom_out[:, left:left + column_step] = sums + prior_weight
    for h in range(split):
        unit = i * split + h
        pl.when(has_right)(lambda: z_copy(unit, 0, 1, h).wait_send())
        pl.when(has_left)(lambda: z_copy(unit, 1, 1, h).wait_send())
        y_copy(unit, 0, h).wait_send()
        c_copy(unit, 0, h).wait_send()
        c_copy(unit_of(0, 0, y_spot, h), steps, h).wait_send()
    for k, (way, s) in enumerate(order, 1):
        for h in range(split):
            def finish():
                unit = unit_of(way, s, spot, h)
                onward = has_right if way == 0 else has_left
                if s + 1 < line:
                    pl.when(onward)(lambda: z_copy(unit, way, s + 1, h).wait_send())
                y_copy(unit, k, h).wait_send()
                c_copy(unit, k, h).wait_send()
                c_copy(unit_of(way, s, y_spot, h), steps + k, h).wait_send()

            pl.when(present(way, s))(finish)
    for copy in sent + list(s_copies.values()):
        copy.wait_send()


def gather_kernel(
    shards, split, turn, cross, steps,
    length_ref, emb_hbm, cent_hbm,
    cent_out, mom_out, lik_out, inverse_out,
    cents_all, rows_all, squares, weights, resp, peaks, parts, lse_ref,
    own_sem, cent_sem, ready, know, z_send, z_recv, w_send, w_recv, y_send, y_recv, o_recv,
    x_send, x_recv, d_recv, c_send, c_recv, k_send, k_recv, p_send, p_recv,
):
    g = lax.axis_index("rows")
    i = lax.axis_index("cent")
    row_count, width = emb_hbm.shape
    cents = cents_all.shape[1]
    total = shards * row_count
    piece = row_count // split
    line = shards // 4
    chunk = 4 * row_count
    spread = chunk // lanes
    spot = lax.rem(i, 4)
    place = i // 4
    core = lax.rem(i, 2)
    core_peer = i + 1 - 2 * core
    core_spot = spot + 1 - 2 * core
    y_spot = lax.rem(spot + 2, 4)
    core_y_spot = lax.rem(core_spot + 2, 4)
    y_peer = place * 4 + y_spot
    there = 1 - g
    factor = score_factor / math.sqrt(width)

    def signal(sem, peer):
        pl.semaphore_signal(sem, inc=1, device_id=peer, device_id_type=MESH)

    barrier = pltpu.get_barrier_semaphore()
    has_right = place < line - 1
    has_left = place > 0
    pl.when(has_right)(lambda: signal(barrier, (g, i + 4)))
    pl.when(has_left)(lambda: signal(barrier, (g, i - 4)))
    for peer in [(g, y_peer), (there, i), (g, core_peer)]:
        signal(barrier, peer)
    own = pltpu.make_async_copy(emb_hbm, rows_all.at[g, i], own_sem)
    own.start()
    cent_copy = pltpu.make_async_copy(cent_hbm, cents_all.at[0], cent_sem)
    cent_copy.start()
    own.wait()
    sides = has_right.astype(jnp.int32) + has_left.astype(jnp.int32)
    pl.semaphore_wait(barrier, 3 + sides)

    def move(ref, send_sem, recv_sem, peer):
        return pltpu.make_async_remote_copy(
            src_ref=ref, dst_ref=ref, send_sem=send_sem, recv_sem=recv_sem,
            device_id=peer, device_id_type=MESH,
        )

    def slot(group, q, where, h):
        if h is None:
            return rows_all.at[group, q * 4 + where]
        return rows_all.at[group, q * 4 + where, pl.ds(h * piece, piece)]

    def column(side):
        return spot if side == 0 else y_spot

    def z_own(way, s, h):
        peer = (g, i + 4 * s if way == 0 else i - 4 * s)
        return move(slot(g, place, spot, h), z_send, z_recv.at[place, h], peer)

    def z_move(way, q, h):
        peer = (g, i + 4 if way == 0 else i - 4)
        return move(slot(g, q, spot, h), z_send, z_recv.at[q, h], peer)

    def low(ref, q, where):
        return ref.at[g, q * 4 + where, pl.ds(0, cross)]

    def high(ref, q, where):
        return ref.at[g, q * 4 + where, pl.ds(cross, row_count - cross)]

    def y_move(q, h):
        return move(slot(g, q, spot, h), y_send, y_recv.at[q], (g, y_peer))

    def y_own():
        return move(low(rows_all, place, spot), y_send, y_recv.at[place], (g, y_peer))

    def y_come(q):
        return move(low(rows_all, q, y_spot), y_send, y_recv.at[q], (g, y_peer))

    def o_own():
        return move(high(rows_all, place, spot), w_send, o_recv, (g, y_peer))

    def o_come():
        return move(high(rows_all, place, y_spot), w_send, o_recv, (g, y_peer))

    def w_move(way, q, s):
        peer = (g, i + 4 * s if way == 0 else i - 4 * s)
        return move(high(rows_all, q, y_spot), w_send, w_recv.at[q], peer)

    def cent_move(src, k, sem, peer):
        return pltpu.make_async_remote_copy(
            src_ref=cent_hbm if src is None else cents_all.at[src], dst_ref=cents_all.at[k],
            send_sem=k_send.at[sem], recv_sem=k_recv.at[k - 1], device_id=(g, peer), device_id_type=MESH,
        )

    def cent_come(k):
        return move(cents_all.at[k], k_send.at[0], k_recv.at[k - 1], (g, y_peer))

    def part(group, q, where, side):
        rows = pl.ds(0, turn) if side == 0 else pl.ds(turn, row_count - turn)
        return rows_all.at[group, q * 4 + where, rows]

    def x_move(q, h):
        side = 0 if h * piece < turn else 1
        return move(slot(g, q, spot, h), x_send, x_recv.at[q, side], (there, i))

    def x_own(side):
        return move(part(g, place, spot, side), x_send, x_recv.at[place, side], (there, i))

    def x_come(q, side):
        return move(part(there, q, spot, side), x_send, x_recv.at[q, side], (there, i))

    def c_part(q, side):
        return move(part(there, q, spot, side), c_send, c_recv.at[1, q], (g, core_peer))

    def x_turn(q):
        return move(part(g, q, y_spot, 0), x_send, x_recv.at[q, 2], (there, i))

    def x_turned(q):
        return move(part(there, q, y_spot, 0), x_send, x_recv.at[q, 2], (there, i))

    def y_turn(q):
        return move(part(there, q, spot, 1), y_send, d_recv.at[q], (g, y_peer))

    def y_turned(q):
        return move(part(there, q, y_spot, 1), y_send, d_recv.at[q], (g, y_peer))

    def c_low(q):
        return move(low(rows_all, q, y_spot), c_send, c_recv.at[0, q], (g, core_peer))

    def c_high(q):
        return move(high(rows_all, q, y_spot), c_send, c_recv.at[0, q], (g, core_peer))

    def c_turn(q, side):
        return move(part(there, q, y_spot, side), c_send, c_recv.at[1, q], (g, core_peer))

    def c_move(mine, q, side, h):
        ref = slot(g if mine else there, q, column(side), h)
        return move(ref, c_send, c_recv.at[0 if mine else 1, q], (g, core_peer))

    def c_come(mine, q):
        ref = rows_all.at[g if mine else there, pl.ds(q * 4, 2)]
        return move(ref, c_send, c_recv.at[0 if mine else 1, q], (g, core_peer))

    def source(way, s):
        return place - s if way == 0 else place + s

    def present(way, s):
        return place >= s if way == 0 else place + s < line

    def starts(way):
        return has_right if way == 0 else has_left

    def onward(way, s):
        if way == 0:
            return jnp.logical_and(place > s, has_right)
        return jnp.logical_and(place + s < line - 1, has_left)

    def ends(way):
        return place == 0 if way == 0 else place == line - 1

    def both(fn, cond):
        for way in range(2):
            pl.when(cond(way))(functools.partial(fn, way))

    def z_take(way, s, h):
        def take():
            q = source(way, s)
            z_move(way, q, h).wait_recv()
            if s + 1 < line:
                pl.when(onward(way, s))(lambda: z_move(way, q, h).start())
            if h * piece < cross:
                y_move(q, h).start()
            x_move(q, h).start()
            c_move(True, q, 0, h).start()

        pl.when(present(way, s))(take)

    def at(way, s, fn):
        if s == 0:
            fn(place)
        else:
            pl.when(present(way, s))(lambda: fn(source(way, s)))

    def y_take(q):
        y_come(q).wait_recv()
        x_turn(q).start()
        c_low(q).start()

    def x_take(q, side):
        x_come(q, side).wait_recv()
        if side == 1:
            y_turn(q).start()
        c_part(q, side).start()

    def turn_take(q, side):
        (y_turned if side else x_turned)(q).wait_recv()
        c_turn(q, side).start()

    def w_take(way, s):
        def take():
            q = source(way, s)
            w_move(way, q, 1).wait_recv()
            if s + 1 < line:
                pl.when(onward(way, s))(lambda: w_move(way, q, 1).start())
            c_high(q).start()

        if cross < row_count:
            pl.when(present(way, s))(take)

    def nth(j):
        orders = [sorted(range(line), key=lambda q: abs(q - p)) for p in range(line)]
        q = orders[0][j]
        for p in range(1, line):
            q = jnp.where(place == p, orders[p][j], q)
        return q

    near = [(way, 1) for way in range(2)]
    far = [(way, s) for s in range(2, line) for way in range(2)]
    for h in range(split):
        both(lambda way: z_own(way, 1, h).start(), starts)
    if cross < row_count:
        o_own().start()
    y_own().start()
    cent_move(None, 2, 0, y_peer).start()
    x_own(0).start()
    x_own(1).start()
    cent_move(None, 1, 1, core_peer).start()
    c_move(True, place, 0, None).start()

    cube = [(g, y_peer), (there, i), (g, core_peer)]
    for peer in cube:
        signal(know.at[0], peer)
    if line > 2:
        pl.when(jnp.logical_and(place == 1, has_right))(lambda: signal(ready.at[0], (g, i + 4)))
        pl.when(jnp.logical_and(place == line - 2, has_left))(lambda: signal(ready.at[1], (g, i - 4)))

        def pass_up():
            pl.semaphore_wait(ready.at[0], 1)
            pl.when(has_right)(lambda: signal(ready.at[0], (g, i + 4)))

        def pass_down():
            pl.semaphore_wait(ready.at[1], 1)
            pl.when(has_left)(lambda: signal(ready.at[1], (g, i - 4)))

        pl.when(place >= 2)(pass_up)
        pl.when(place <= line - 3)(pass_down)

        def far_go(way):
            for h in range(split):
                for s in range(2, line):
                    z_own(way, s, h).start()

        both(far_go, ends)

    cent_copy.wait()
    cent_wide = cents_all[0].astype(jnp.float32)
    half_norm = 0.5 * jnp.sum(cent_wide * cent_wide, axis=1, keepdims=True)

    def score(mine, q):
        t = 0 if mine else 1
        c_come(mine, q).wait_recv()
        group = g if mine else there
        block = rows_all[group, pl.ds(q * 4, 4)].reshape(chunk, width)
        inner = lax.dot_general(
            cents_all[0], block, contract_width, preferred_element_type=jnp.float32
        )
        logits = factor * (inner - half_norm)
        peak = jnp.max(logits, axis=0, keepdims=True)
        weights[t, q] = jnp.exp(logits - peak)
        for r in range(spread):
            peaks[t, q, r:r + 1, :] = peak[:, r * lanes:(r + 1) * lanes]
        wide = block.astype(jnp.float32)
        squares[group, pl.ds(q * 4, 4)] = (wide * wide).astype(jnp.bfloat16).reshape(
            4, row_count, width
        )

    def partial_lse(all_half, q):
        block = rows_all[g, q * 4 + spot]
        inner = lax.dot_general(
            cents_all[...].reshape(4 * cents, width), block, contract_width,
            preferred_element_type=jnp.float32,
        )
        logits = factor * (inner - all_half)
        peak = jnp.max(logits, axis=0, keepdims=True)
        value = peak + jnp.log(jnp.sum(jnp.exp(logits - peak), axis=0, keepdims=True))
        row = (q * 4 + spot) * row_count + lax.broadcasted_iota(jnp.int32, value.shape, 1)
        parts[g, i, pl.ds(q, 1), :] = jnp.where(row < length_ref[0], value, masked)

    def joined(values):
        highest = values[0]
        for value in values[1:]:
            highest = jnp.maximum(highest, value)
        amount = jnp.exp(values[0] - highest)
        for value in values[1:]:
            amount = amount + jnp.exp(value - highest)
        return highest + jnp.log(amount)

    def move_parts(group, count, k):
        return move(parts.at[group, pl.ds(0, count)], p_send.at[k], p_recv.at[k], (g, y_peer))

    def whole_lse(group):
        return [joined([parts[group, p * 4 + w] for p in range(line)]) for w in range(4)]

    ones = jnp.ones((8, total), jnp.bfloat16)

    def weigh(t, q, place_in_resp):
        for r in range(spread):
            left = r * lanes
            scale = jnp.exp(peaks[t, q, r:r + 1, :] - lse_ref[t, r, pl.ds(q, 1), :])
            resp[:, place_in_resp * chunk + left:place_in_resp * chunk + left + lanes] = (
                weights[t, q, :, left:left + lanes] * scale
            ).astype(jnp.bfloat16)

    def times(left, right):
        return lax.dot_general(left, right, contract_rows, preferred_element_type=jnp.float32)

    def mass_of(block):
        return lax.dot_general(
            ones[:, :block.shape[1]], block, contract_width, preferred_element_type=jnp.float32
        )

    def keep_lse(t, lse):
        for r in range(spread):
            lse_ref[t, r] = jnp.concatenate([lse[2 * r], lse[2 * r + 1]], axis=1)

    def add_there(orders):
        mass = 0.0
        weighted = cent_out[...]
        moments = mom_out[...]
        for n, (q, weighed) in enumerate(orders):
            if not weighed:
                weigh(1, q, line + n)
            block = resp[:, total + n * chunk:total + (n + 1) * chunk]
            mass = mass + mass_of(block)
            weighted = weighted + times(block, rows_all[there, pl.ds(q * 4, 4)].reshape(chunk, width))
            moments = moments + times(block, squares[there, pl.ds(q * 4, 4)].reshape(chunk, width))
        cent_out[...] = weighted
        mom_out[...] = moments
        return mass

    places = [place] + [nth(j) for j in range(1, line)]
    state = {"half": None, "mass": None, "lse": None, "told": False, "ready": [], "there": False, "moments": False}

    def near_rows(h):
        for way, s in near:
            z_take(way, s, h)

    def far_rows(h):
        for way, s in far:
            z_take(way, s, h)

    def other_column(_):
        if cross == row_count:
            return
        o_come().wait_recv()
        both(lambda way: w_move(way, place, 1).start(), starts)

        def w_far(way):
            for s in range(2, line):
                w_move(way, place, s).start()

        if line > 2:
            both(w_far, ends)
        c_high(place).start()

    def tell(_):
        pl.semaphore_wait(know.at[0], 3)
        for peer in cube:
            signal(know.at[1], peer)

    def tell_line(_):
        pl.semaphore_wait(know.at[1], 3)
        for q in range(1, line):
            signal(know.at[2], (g, lax.rem(place + q, line) * 4 + spot))

    def cents_out(_):
        cent_move(None, 2, 0, y_peer).start()

    def half_of(k):
        wide = cents_all[k].astype(jnp.float32)
        return 0.5 * jnp.sum(wide * wide, axis=1, keepdims=True)

    def cents_in(_):
        cent_come(2).wait_recv()
        cent_move(2, 3, 2, core_peer).start()
        cent_come(1).wait_recv()
        state["halves"] = [half_norm, half_of(1), half_of(2)]

    def cents_ready(_):
        cent_come(3).wait_recv()
        state["half"] = jnp.concatenate([*state["halves"], half_of(3)], axis=0)

    def normaliser(k):
        if k == 0:
            partial_lse(state["half"], place)
        for way, s in (near, far)[k - 1] if k else ():
            at(way, s, functools.partial(partial_lse, state["half"]))

    def send_parts(_):
        pl.semaphore_wait(know.at[2], line - 1)
        mine_part = parts.at[g, i]
        for k in range(shards - 1, -1, -1):
            peer = lax.rem(i + k, shards)
            for group, t in ((there, 1), (g, 0)):
                if k > 0 or t:
                    pltpu.make_async_remote_copy(
                        src_ref=mine_part, dst_ref=mine_part, send_sem=p_send.at[t],
                        recv_sem=p_recv.at[t], device_id=(group, peer), device_id_type=MESH,
                    ).start()

    def crossed(k):
        for way, s in (near, far)[k]:
            w_take(way, s)

    def own_sums(_):
        move_parts(g, shards - 1, 0).wait_recv()
        lse = whole_lse(g)
        keep_lse(0, lse)
        for q in range(line):
            weigh(0, q, q)
        state["mass"] = mass_of(resp[:, :total])
        cent_out[...] = prior_weight * cent_wide + times(
            resp[:, :total], rows_all[g].reshape(total, width)
        )
        state["lse"] = lse

    def own_moments(_):
        mom_out[...] = prior_weight + times(resp[:, :total], squares[g].reshape(total, width))
        state["moments"] = True

    def score_there(j):
        score(False, places[j])
        state["ready"].append((places[j], False))

    def lse_from_there():
        if not state["there"]:
            move_parts(there, shards, 1).wait_recv()
            keep_lse(1, whole_lse(there))
            state["there"] = True

    def weigh_there(j):
        lse_from_there()
        q = places[j]
        c_come(False, q).wait_recv()
        block = rows_all[there, pl.ds(q * 4, 4)].reshape(chunk, width)
        inner = lax.dot_general(
            cents_all[0], block, contract_width, preferred_element_type=jnp.float32
        )
        first = total + len(state["ready"]) * chunk
        for r in range(spread):
            left = r * lanes
            logits = factor * (inner[:, left:left + lanes] - half_norm)
            resp[:, first + left:first + left + lanes] = jnp.exp(
                logits - lse_ref[1, r, pl.ds(q, 1), :]
            ).astype(jnp.bfloat16)
        wide = block.astype(jnp.float32)
        squares[there, pl.ds(q * 4, 4)] = (wide * wide).astype(jnp.bfloat16).reshape(
            4, row_count, width
        )
        state["ready"].append((q, True))

    def sums_there(_):
        if not state["moments"] or not state["ready"]:
            return
        lse_from_there()
        state["mass"] = state["mass"] + add_there(state["ready"])
        state["ready"] = []

    def write_lik(_):
        lse = state["lse"]
        pick = lse[0]
        for w in range(1, 4):
            pick = jnp.where(spot == w, lse[w], pick)
        own_lik = pick[0:1]
        for q in range(1, line):
            own_lik = jnp.where(place == q, pick[q:q + 1], own_lik)
        row = i * row_count + lax.broadcasted_iota(jnp.int32, own_lik.shape, 1)
        lik_out[...] = jnp.where(row < length_ref[0], own_lik, 0.0)

    acts = {
        "N": near_rows, "Z": far_rows, "O": other_column, "E": tell, "F": tell_line,
        "K": cents_out, "I": cents_in, "C": cents_ready, "A": normaliser, "L": send_parts,
        "W": crossed, "Y": lambda j: y_take(places[j]), "H": lambda j: x_take(places[j], 1),
        "G": lambda j: x_take(places[j], 0), "T": lambda j: turn_take(places[j], 0),
        "D": lambda j: turn_take(places[j], 1), "S": lambda j: score(True, places[j]),
        "s": score_there, "f": weigh_there, "R": own_sums, "M": own_moments, "r": sums_there, "l": write_lik,
    }
    for step in steps:
        acts[step[0]](int(step[1:] or 0))
    mass = state["mass"]
    inverse = 1.0 / (mass[0:1, :] + prior_weight)
    inverse_out[...] = jnp.transpose(jnp.broadcast_to(inverse, (cents, cents)))

    def drain(sem, count):
        step = max(b for b in range(piece, row_count + 1, piece) if count % b == 0)
        rows = rows_all.at[g, pl.ds(0, count // step), pl.ds(0, step)]
        move(rows, sem, own_sem, (g, y_peer)).wait_send()

    drain(z_send, (line - 1) * row_count)
    drain(y_send, line * (cross + row_count - turn))
    drain(x_send, line * (row_count + turn))
    drain(c_send, 4 * line * row_count)
    if cross < row_count:
        drain(w_send, line * (row_count - cross))
    for k in range(3):
        move(cents_all.at[1], k_send.at[k], own_sem, (g, y_peer)).wait_send()
    move_parts(g, shards - 1, 0).wait_send()
    move_parts(there, shards, 1).wait_send()


schedule = (
    "N0", "N1", "Y0", "E", "O", "N2", "S0", "G1", "H0", "N3", "G0", "Z1",
    "Z0", "F", "I", "T0", "Z2", "W0", "H1", "Z3", "Y1", "C", "A0", "A1",
    "A2", "L", "Y2", "H2", "Y3", "G2", "D0", "H3", "W1", "S1", "D1", "s0",
    "T1", "S3", "G3", "S2", "s1", "T2", "D2", "R", "T3", "M", "D3", "r",
    "f2", "l", "f3", "r",
)


def gather_steps(line, split):
    assert line == 4 and split == 4
    return schedule


def gather_call(shards, row_count, width, cents, out_shape):
    line = shards // 4
    split = 4
    cross = row_count * 2 // 4
    turn = row_count * 2 // 4
    total = shards * row_count
    spread = 4 * row_count // lanes
    vmem = pl.BlockSpec(memory_space=pltpu.VMEM)
    hbm = pl.BlockSpec(memory_space=pltpu.HBM)
    dma = pltpu.SemaphoreType.DMA
    regular = pltpu.SemaphoreType.REGULAR
    return pl.pallas_call(
        functools.partial(gather_kernel, shards, split, turn, cross, gather_steps(line, split)),
        out_shape=out_shape,
        in_specs=[pl.BlockSpec(memory_space=pltpu.SMEM), hbm, hbm],
        out_specs=(vmem, vmem, vmem, vmem),
        scratch_shapes=[
            pltpu.VMEM((4, cents, width), jnp.bfloat16),
            pltpu.VMEM((2, shards, row_count, width), jnp.bfloat16),
            pltpu.VMEM((2, shards, row_count, width), jnp.bfloat16),
            pltpu.VMEM((2, line, cents, 4 * row_count), jnp.float32),
            pltpu.VMEM((cents, 2 * total), jnp.bfloat16),
            pltpu.VMEM((2, line, spread, lanes), jnp.float32),
            pltpu.VMEM((2, shards, line, row_count), jnp.float32),
            pltpu.VMEM((2, spread, line, lanes), jnp.float32),
            dma, dma, regular((2,)), regular((3,)),
            dma, dma((line, split)), dma, dma((line,)), dma, dma((line,)), dma,
            dma, dma((line, 3)), dma((line,)), dma, dma((2, line)), dma((3,)), dma((3,)),
            dma((2,)), dma((2,)),
        ],
        compiler_params=pltpu.CompilerParams(
            collective_id=0, has_side_effects=True, vmem_limit_bytes=32 * 1024 * 1024
        ),
        name="soft_em",
    )


def solution(mesh):
    groups = mesh.shape["rows"]
    shards = mesh.shape["cent"]
    line = shards // 4

    def step(embeddings, centroids, group_length):
        row_count, width = embeddings.shape
        cents = centroids.shape[0]
        total = row_count * shards
        column_step = 256 if width % 256 == 0 else width
        pieces = 2 * (width // column_step)
        split = 2 if row_count % 32 == 0 else 1
        vmem = pl.BlockSpec(memory_space=pltpu.VMEM)
        hbm = pl.BlockSpec(memory_space=pltpu.HBM)
        held = 4 * total * width + 4 * cents * total + 2 * (groups * 2 + 1) * cents * width
        steps = 2 * line - 1
        dma = pltpu.SemaphoreType.DMA
        out_shape = (
            jax.ShapeDtypeStruct((cents, width), jnp.float32),
            jax.ShapeDtypeStruct((cents, width), jnp.float32),
            jax.ShapeDtypeStruct((1, row_count), jnp.float32),
            jax.ShapeDtypeStruct((cents, cents), jnp.float32),
        )
        if groups == 2 and shards == 16 and row_count % 64 == 0 and total <= 2048:
            call = gather_call(shards, row_count, width, cents, out_shape)
        else:
            call = pl.pallas_call(
                functools.partial(sums_kernel, groups, shards, column_step, split),
                out_shape=out_shape,
                in_specs=[pl.BlockSpec(memory_space=pltpu.SMEM), hbm, hbm],
                out_specs=(vmem, vmem, vmem, vmem),
                scratch_shapes=[
                    pltpu.VMEM((cents, width), jnp.bfloat16),
                    pltpu.VMEM((shards * split, row_count // split, width), jnp.bfloat16),
                    pltpu.VMEM((shards * split, row_count // split, width), jnp.bfloat16),
                    pltpu.VMEM((cents, total), jnp.float32),
                    pltpu.VMEM((2 + 2 * line, 2, total), jnp.float32),
                    pltpu.VMEM((groups, pieces, cents, column_step), jnp.bfloat16),
                    pltpu.VMEM((groups, 8, cents), jnp.float32),
                    dma((split,)), dma, dma((2, line, split)), dma((2, line, split)),
                    dma((steps, split)), dma((steps, split)),
                    dma((2 * steps, split)), dma((2 * steps, split)),
                    dma((2 * line,)), dma((2 * line,)),
                    dma((pieces, groups)), dma((pieces, groups)),
                    dma((groups,)), dma((groups,)),
                ],
                compiler_params=pltpu.CompilerParams(
                    collective_id=0, has_side_effects=True, vmem_limit_bytes=2 * held + 4 * 1024 * 1024
                ),
                name="soft_em",
            )
        cent_sums, moment_sums, loglik, inverse = call(group_length, pltpu.with_memory_space_constraint(embeddings, pltpu.HBM), pltpu.with_memory_space_constraint(centroids, pltpu.HBM))
        new_centroids = (cent_sums * inverse[:, 0:1]).astype(jnp.bfloat16)
        new_moments = (moment_sums * inverse[:, 0:1]).astype(jnp.bfloat16)
        return new_centroids, new_moments, loglik.reshape(row_count)

    return jax.shard_map(
        step,
        mesh=mesh,
        in_specs=(P(("rows", "cent"), None), P("cent", None), P("rows")),
        out_specs=(P("cent", None), P("cent", None), P(("rows", "cent"))),
        check_vma=False,
    )
```
